32 devices in a mesh: gx: 8 (over y, x, core), gy: 4 (over z).
Axes of the slice: x: 2, y: 2, z: 4, core: 2. Of those that a mesh axis runs over, the one named last changes fastest.
Arguments:
- leaf_multipoles: bfloat16 [36, 32, 32, 128], P(None, 'gx', 'gy'), may hold values from -6 to 6
- positions: float32 [3, 8, 32, 32, 128], P(None, None, 'gx', 'gy'), may hold values from 0 to 1
- masses: float32 [8, 32, 32, 128], P(None, 'gx', 'gy'), may hold values from 0.1 to 1
- counts: int32 [32, 32, 128], P('gx', 'gy'), may hold values from 0 to 8
- up_operator: bfloat16 [288, 36], replicated, may hold values from -0.375 to 0.375
- far_operator: bfloat16 [36, 11376], replicated, may hold values from -0.078125 to 0.078125
- down_operator: bfloat16 [36, 288], replicated, may hold values from -1 to 1
Outputs:
- local_expansion: float32 [36, 32, 32, 128], P(None, 'gx', 'gy')
- near_potential: float32 [8, 32, 32, 128], P(None, 'gx', 'gy')
The draws below stay inside these ranges and needn't reach their ends.
Inputs may be any that keep to these rules, and one draw needn't show every extreme that they name: Slots 0 to counts - 1 of a cell hold its particles, the others are empty.
All inputs are finite; a program needn't handle non-finite values.
Results may differ from the reference program's by a relative error of at most 0.0042.
Values may be sent and summed in bfloat16 or wider, within the bound.
No kernel may reach another device: no remote copies, remote signals or barrier semaphores. Data moves between devices by JAX's collectives and lax.ppermute only.
A program may use at most 128 MiB of HBM per device.

```python
import math
import jax
import jax.numpy as jnp
import numpy as np
from jax import lax

COEF = 36
NOFF = 316
NZL = 128
SLOTS = 8
NX = 32
NY = 32


def touch_ends(array, key, smallest, high):
    extent = array.shape
    index_at = [jax.random.randint(jax.random.fold_in(key, axis), (), 0, extent[axis]) for axis in range(len(extent))]
    array = array.at[tuple(index_at)].set(smallest)
    longest = extent.index(max(extent))
    index_at[longest] = (index_at[longest] + 1) % extent[longest]
    return array.at[tuple(index_at)].set(high)


def block_scale(key, shape, shards, low, high):
    def one(axis_at, blocks):
        steps = jax.random.uniform(jax.random.fold_in(jax.random.fold_in(key, 6), axis_at), (blocks,), jnp.float32, low / len(shards), high / len(shards))
        return jnp.repeat(jnp.exp(steps), shape[axis_at] // blocks).reshape((-1,) + (1,) * (len(shape) - axis_at - 1))

    level = one(*shards[0])
    for cut in shards[1:]:
        level = level * one(*cut)
    return level


def bell_draw(rng, shape, scale, bound, shards=(), kind=jnp.bfloat16):
    gain = block_scale(rng, shape, shards, -0.22, 0.18) if shards else 1.0
    result = jax.random.normal(rng, shape, jnp.float32) * scale * gain
    return jnp.minimum(jnp.maximum(result, -bound), bound).astype(kind)


def setup_inputs(seed: int = 0) -> dict:
    keys = jax.random.split(jax.random.key(seed), 8)
    return {
        "leaf_multipoles": bell_draw(keys[0], (COEF, NX, NY, NZL), 1.0, 6.0, ((1, 8), (2, 4))),
        "positions": jnp.clip(1.0 * jax.random.uniform(keys[1], (3, SLOTS, NX, NY, NZL), jnp.float32) ** block_scale(keys[1], (3, SLOTS, NX, NY, NZL), ((2, 8), (3, 4)), -0.2, 0.2), 0.0, 1.0),
        "masses": jnp.clip(jnp.exp(math.log(1.0) - 2.3025851 * jax.random.uniform(keys[2], (SLOTS, NX, NY, NZL), jnp.float32) ** block_scale(keys[2], (SLOTS, NX, NY, NZL), ((1, 8), (2, 4)), -0.2, 0.2)), 0.1, 1.0),
        "counts": touch_ends(jax.random.randint(keys[3], (NX, NY, NZL), 0, SLOTS + 1), jax.random.fold_in(keys[3], 1), 0, SLOTS).astype(jnp.int32),
        "up_operator": bell_draw(keys[4], (8 * COEF, COEF), (8 * COEF) ** -0.5, 0.375),
        "far_operator": bell_draw(keys[5], (COEF, NOFF * COEF), (189 * COEF) ** -0.5, 0.078125),
        "down_operator": bell_draw(keys[6], (COEF, 8 * COEF), COEF ** -0.5, 1.0),
    }


SOFTENING = 0.05

def shift_list():
    return [(step_x, step_y, step_z) for step_x in (-1, 0, 1) for step_y in (-1, 0, 1) for step_z in (-1, 0, 1)]

def child_bits(number):
    return (number // 4, number // 2 % 2, number % 2)

def offset_table():
    vectors = [(step_x, step_y, step_z) for step_x in range(-3, 4) for step_y in range(-3, 4) for step_z in range(-3, 4) if max(abs(step_x), abs(step_y), abs(step_z)) >= 2]
    lookup = np.full((27, 8, 8), len(vectors), dtype=np.int32)
    for shift_id, offset in enumerate(shift_list()):
        for source in range(8):
            for target in range(8):
                vector = tuple((2 * offset[axis_id] + child_bits(source)[axis_id] - child_bits(target)[axis_id] for axis_id in range(3)))
                if max(abs(vector[0]), abs(vector[1]), abs(vector[2])) >= 2:
                    lookup[shift_id, source, target] = vectors.index(vector)
    return lookup

def assemble(far_operator):
    coeff_count = far_operator.shape[0]
    blocks = far_operator.reshape(coeff_count, -1, coeff_count)
    blocks = jnp.concatenate([blocks, jnp.zeros((coeff_count, 1, coeff_count), blocks.dtype)], axis=1)
    picked = jnp.take(blocks, jnp.asarray(offset_table().reshape(-1), dtype=jnp.int32), axis=1)
    picked = picked.reshape(coeff_count, 27, 8, 8, coeff_count).transpose(1, 2, 0, 3, 4)
    return picked.reshape(27, 8 * coeff_count, 8 * coeff_count)

def group_cells(volume):
    coeff_count, size_x, size_y, size_z = volume.shape
    reshaped = volume.reshape(coeff_count, size_x // 2, 2, size_y // 2, 2, size_z // 2, 2)
    return reshaped.transpose(2, 4, 6, 0, 1, 3, 5).reshape(8 * coeff_count, size_x // 2, size_y // 2, size_z // 2)

def spread_cells(grouped):
    total_rows, size_x, size_y, size_z = grouped.shape
    coeff_count = total_rows // 8
    reshaped = grouped.reshape(2, 2, 2, coeff_count, size_x, size_y, size_z)
    return reshaped.transpose(3, 4, 0, 5, 1, 6, 2).reshape(coeff_count, 2 * size_x, 2 * size_y, 2 * size_z)

def upward(up_operator, grouped):
    parent = jnp.einsum('sj,sxyz->jxyz', up_operator.astype(jnp.float32), grouped.astype(jnp.float32), precision=lax.Precision.HIGHEST)
    return parent.astype(jnp.bfloat16)

def downward(down_operator, parent):
    children = jnp.einsum('it,ixyz->txyz', down_operator.astype(jnp.float32), parent, precision=lax.Precision.HIGHEST)
    return spread_cells(children)

def far_full(grouped, kernel):
    running = jnp.zeros(grouped.shape, jnp.float32)
    for shift_id, offset in enumerate(shift_list()):
        rolled = jnp.roll(grouped, (-offset[0], -offset[1], -offset[2]), axis=(1, 2, 3))
        running = running + jnp.einsum('st,sxyz->txyz', kernel[shift_id], rolled, precision=lax.Precision.HIGHEST)
    return running

def near_field(positions, masses, counts):
    slot_count = masses.shape[0]
    live_slot = lax.broadcasted_iota(jnp.int32, masses.shape, 0) < counts[None]
    live_mass = jnp.where(live_slot, masses, jnp.float32(0.0))
    slot_ids = lax.broadcasted_iota(jnp.int32, (slot_count, 1, 1, 1), 0)
    running = jnp.zeros(masses.shape, jnp.float32)
    for offset in shift_list():
        source_pos = jnp.roll(positions, (-offset[0], -offset[1], -offset[2]), axis=(2, 3, 4))
        source_mass = jnp.roll(live_mass, (-offset[0], -offset[1], -offset[2]), axis=(1, 2, 3))
        centre = offset == (0, 0, 0)

        def one_target(target):
            target_pos = lax.dynamic_index_in_dim(positions, target, axis=1, keepdims=False)
            squared = jnp.float32(SOFTENING * SOFTENING)
            for axis_id in range(3):
                separation = source_pos[axis_id] + jnp.float32(offset[axis_id]) - target_pos[axis_id][None]
                squared = squared + separation * separation
            pair_terms = source_mass * lax.rsqrt(squared)
            if centre:
                pair_terms = jnp.where(slot_ids == target, jnp.float32(0.0), pair_terms)
            return lax.optimization_barrier(jnp.sum(pair_terms, axis=0))
        running = running + lax.map(one_target, jnp.arange(slot_count, dtype=jnp.int32))
    return jnp.where(live_slot, -running / slot_count, jnp.float32(0.0))

def reference(leaf_multipoles, positions, masses, counts, up_operator, far_operator, down_operator):
    kernel = assemble(far_operator).astype(jnp.float32)
    moments = [leaf_multipoles]
    for level_id in range(4):
        moments.append(upward(up_operator, group_cells(moments[-1])))
    expansion = None
    for depth in range(4, -1, -1):
        grouped = group_cells(moments[depth]).astype(jnp.float32)
        far_part = spread_cells(far_full(grouped, kernel))
        if expansion is None:
            expansion = far_part
        else:
            expansion = far_part + downward(down_operator, expansion)
    return (expansion, near_field(positions, masses, counts))
```

```python
import functools

import jax
import jax.numpy as jnp
import numpy as np
from jax import lax
from jax.experimental import pallas as pl
from jax.experimental.pallas import tpu as pltpu
from jax.sharding import PartitionSpec as P

SOFTENING = 0.05
EPS = SOFTENING * SOFTENING
F32 = jnp.float32
BF16 = jnp.bfloat16
COEF = 36
GROUP = 4 * COEF
NEAR_ROWS = 256
Y_LEAF = NEAR_ROWS
Y_SIX = Y_LEAF + 2 * GROUP
Y_FIVE = Y_SIX + GROUP
Y_ROWS = Y_FIVE + 80
X_NEAR = 320
X_LEAF = 2 * X_NEAR
X_SIX = X_LEAF + 6 * GROUP
X_HALO = X_SIX + GROUP
X_FIVE = X_HALO + GROUP
X_ROWS = X_FIVE + 80

VMEM = pl.BlockSpec(memory_space=pltpu.VMEM)
SMEM = pl.BlockSpec(memory_space=pltpu.SMEM)


def shape(dims, dtype):
    return jax.ShapeDtypeStruct(dims, dtype)


def kernel_call(body, outs, inputs, scratch=(), scalars=0, limit=48):
    return pl.pallas_call(
        body,
        out_shape=outs,
        in_specs=[SMEM] * scalars + [VMEM] * (len(inputs) - scalars),
        out_specs=[VMEM] * len(outs),
        scratch_shapes=list(scratch),
        compiler_params=pltpu.CompilerParams(vmem_limit_bytes=limit * 1024 * 1024),
    )(*inputs)


def iota(dims, axis):
    return lax.broadcasted_iota(jnp.int32, dims, axis)


def dot(lhs, rhs):
    return lax.dot_general(lhs, rhs, (((1,), (0,)), ((), ())), preferred_element_type=F32)


def dot_nt(lhs, rhs):
    return lax.dot_general(lhs, rhs, (((1,), (1,)), ((), ())), preferred_element_type=F32)


def one_hot(mask):
    return jnp.where(mask, F32(1.0), F32(0.0)).astype(BF16)


def parts(value):
    high = value.astype(BF16)
    return high, (value - high.astype(F32)).astype(BF16)


def lane_roll(value, shift):
    return pltpu.roll(value, shift % 128, 1) if shift % 128 else value


def up_blocks(up_ref):
    eye = one_hot(iota((COEF, COEF), 0) == iota((COEF, COEF), 1))
    whole = up_ref[...].astype(F32)
    halves = []
    for bit in range(2):
        rows = jnp.concatenate(
            [whole[(2 * k + bit) * COEF : (2 * k + bit + 1) * COEF] for k in range(4)], axis=0
        )
        halves.append(dot_nt(eye, rows.astype(BF16)).astype(BF16))
    return halves


def prep_kernel(
    place, m_ref, pos_ref, mass_ref, count_ref, up_ref,
    grid_ref, up_msg, down_msg, five_ref, live_ref, m32, x32, six32, five32,
):
    m32[...] = m_ref[...].astype(F32)
    for x in range(4):
        for y in range(8):
            start = ((x // 2) * 4 + y // 2) * GROUP + (2 * (x % 2) + y % 2) * COEF
            x32[start : start + COEF, :] = m32[pl.ds(x * 8 + y, COEF, stride=32), :]
    grid = x32[...].astype(BF16)
    grid_ref[...] = grid
    count = count_ref[...]
    for slot in range(8):
        live_ref[slot * 32 : slot * 32 + 32, :] = jnp.where(
            count > slot, mass_ref[slot * 32 : slot * 32 + 32, :], F32(0.0)
        )
    for msg, y, parent in ((up_msg, 7, 3), (down_msg, 0, 0)):
        rows = []
        for x in range(4):
            rows.append(pos_ref[pl.ds(x * 8 + y, 24, stride=32), :])
            rows.append(live_ref[pl.ds(x * 8 + y, 8, stride=32), :])
        high, low = parts(jnp.concatenate(rows, axis=0))
        msg[0:128, :] = high
        msg[128:256, :] = low
        for xp in range(2):
            msg[Y_LEAF + xp * GROUP : Y_LEAF + (xp + 1) * GROUP, :] = grid_ref[
                (xp * 4 + parent) * GROUP : (xp * 4 + parent + 1) * GROUP, :
            ]
    low_half = iota((COEF, 128), 1) < 64
    even_up, odd_up = up_blocks(up_ref)
    row, col = iota((128, 128), 0), iota((128, 128), 1)
    split_z = one_hot(row == 2 * (col % 64) + col // 64)
    split = dot(grid, split_z).astype(BF16)
    columns = jnp.concatenate([split[k * GROUP : (k + 1) * GROUP] for k in range(8)], axis=1)
    even, odd = dot(even_up, columns), dot(odd_up, columns)
    for xp in range(2):
        for y in range(2):
            first, second = (xp * 4 + y) * 128, (xp * 4 + 2 + y) * 128
            near_part = even[:, first : first + 128] + lane_roll(odd[:, first : first + 128], 64)
            far_part = lane_roll(even[:, second : second + 128], 64) + odd[:, second : second + 128]
            start = (2 * xp + y) * COEF
            six32[start : start + COEF, :] = jnp.where(low_half, near_part, far_part)
    six = six32[...].astype(BF16)
    split_six = one_hot(row == ((col // 32) % 2) * 64 + 2 * (col % 32) + col // 64)
    split = dot(six, split_six).astype(BF16)
    five = dot(even_up, split) + lane_roll(dot(odd_up, split), 64)
    five32[...] = jnp.zeros_like(five32)
    mine = iota((COEF, 128), 1) // 32 == place[1]
    for y in range(2):
        moved = pltpu.roll(five, (32 * place[1] + 96 * y) % 128, 1)
        five32[y * COEF : (y + 1) * COEF, :] = jnp.where(mine, moved, F32(0.0))
    five_ref[...] = five32[...].astype(BF16)
    for msg in (up_msg, down_msg):
        msg[Y_SIX:Y_FIVE, :] = six
        msg[Y_FIVE:Y_ROWS, :] = five_ref[...]


def prepare(place, leaf, positions, masses, counts, up_operator):
    return kernel_call(
        prep_kernel,
        (
            shape((8 * GROUP, 128), BF16),
            shape((Y_ROWS, 128), BF16),
            shape((Y_ROWS, 128), BF16),
            shape((80, 128), BF16),
            shape((256, 128), F32),
        ),
        (place, leaf, positions, masses, counts, up_operator),
        (
            pltpu.VMEM((1152, 128), F32),
            pltpu.VMEM((1152, 128), F32),
            pltpu.VMEM((GROUP, 128), F32),
            pltpu.VMEM((80, 128), F32),
        ),
        scalars=1,
    )


def cross_kernel(
    below, above, two, mine, grid_ref, pos_ref, live_ref, to_low, to_high, near32
):
    five = (
        mine[Y_FIVE:Y_ROWS, :].astype(F32)
        + below[Y_FIVE:Y_ROWS, :].astype(F32)
        + above[Y_FIVE:Y_ROWS, :].astype(F32)
        + two[...].astype(F32)
    ).astype(BF16)
    low_half = iota((GROUP, 128), 1) < 64
    halo = jnp.where(
        low_half, above[Y_SIX:Y_FIVE, :].astype(F32), below[Y_SIX:Y_FIVE, :].astype(F32)
    ).astype(BF16)
    for msg, x, xp in ((to_low, 0, 0), (to_high, 3, 1)):
        for slot in range(8):
            for axis in range(3):
                start = (axis * 8 + slot) * 32 + x * 8
                near32[pl.ds(axis * 8 + slot, 8, stride=32), :] = pos_ref[start : start + 8, :]
            start = slot * 32 + x * 8
            near32[pl.ds(24 + slot, 8, stride=32), :] = live_ref[start : start + 8, :]
        high, low = parts(near32[...])
        for half, value in ((0, high), (1, low)):
            base = half * X_NEAR
            msg[base + 32 : base + 288, :] = value
            source = half * 128 + x * 32
            msg[base : base + 32, :] = below[source : source + 32, :]
            msg[base + 288 : base + 320, :] = above[source : source + 32, :]
        source = Y_LEAF + xp * GROUP
        msg[X_LEAF : X_LEAF + GROUP, :] = below[source : source + GROUP, :]
        msg[X_LEAF + GROUP : X_LEAF + 5 * GROUP, :] = grid_ref[
            xp * 4 * GROUP : (xp + 1) * 4 * GROUP, :
        ]
        msg[X_LEAF + 5 * GROUP : X_SIX, :] = above[source : source + GROUP, :]
        msg[X_SIX:X_HALO, :] = mine[Y_SIX:Y_FIVE, :]
        msg[X_HALO:X_FIVE, :] = halo
        msg[X_FIVE:X_ROWS, :] = five


def cross(below, above, two, mine, grid, positions, live):
    return kernel_call(
        cross_kernel,
        (shape((X_ROWS, 128), BF16), shape((X_ROWS, 128), BF16)),
        (below, above, two, mine, grid, positions, live),
        (pltpu.VMEM((256, 128), F32),),
    )


def inverse_distance(target, source):
    squared = F32(EPS)
    for axis in range(3):
        separation = source[axis] - target[axis]
        squared = squared + separation * separation
    return lax.rsqrt(squared)


def inner_kernel(pos_ref, live_ref, out_ref, shifted, sums):
    row = iota((8, 128), 0)
    sums[...] = jnp.zeros_like(sums)

    def fill(x, carry):
        for slot in range(8):
            values = [pos_ref[axis, slot, x] for axis in range(3)] + [live_ref[slot, x]]
            for index, step in enumerate((-1, 0, 1)):
                moved = [lane_roll(value, -step) for value in values]
                if step:
                    moved[2] = moved[2] + F32(step)
                for k in range(4):
                    shifted[index, k, slot, x] = moved[k]
        return carry

    lax.fori_loop(0, 4, fill, 0)

    def targets(x):
        return [[shifted[1, k, slot, x] for k in range(4)] for slot in range(8)]

    def pairs(goals, x, step, totals):
        step_x, step_y, step_z = step
        edge = row == (7 if step_y > 0 else 0)
        for slot in range(8):
            source = [shifted[step_z + 1, k, slot, x] for k in range(4)]
            if step_y:
                source = [pltpu.roll(value, (-step_y) % 8, 0) for value in source]
                source[1] = source[1] + F32(step_y)
                source[3] = jnp.where(edge, F32(0.0), source[3])
            if step_x:
                source[0] = source[0] + F32(step_x)
            back = None
            for goal in range(8):
                inverse = inverse_distance(goals[goal], source)
                totals[goal] = totals[goal] + source[3] * inverse
                term = goals[goal][3] * inverse
                back = term if back is None else back + term
            if step_y:
                back = pltpu.roll(jnp.where(edge, F32(0.0), back), step_y % 8, 0)
            sums[step_z + 1, slot, x] = sums[step_z + 1, slot, x] + back

    def plane(x, carry):
        goals = targets(x)
        totals = [jnp.zeros((8, 128), F32) for slot in range(8)]
        for slot in range(8):
            for goal in range(slot):
                inverse = inverse_distance(goals[goal], goals[slot])
                totals[goal] = totals[goal] + goals[slot][3] * inverse
                totals[slot] = totals[slot] + goals[goal][3] * inverse
        for step in ((0, 0, 1), (0, 1, -1), (0, 1, 0), (0, 1, 1)):
            pairs(goals, x, step, totals)
        for slot in range(8):
            sums[1, slot, x] = sums[1, slot, x] + totals[slot]
        return carry

    def planes(x, carry):
        for step_y in (-1, 0, 1):
            goals = targets(x)
            totals = [sums[1, slot, x] for slot in range(8)]
            for step_z in (-1, 0, 1):
                pairs(goals, x + 1, (1, step_y, step_z), totals)
            for slot in range(8):
                sums[1, slot, x] = totals[slot]
        return carry

    lax.fori_loop(0, 4, plane, 0)
    lax.fori_loop(0, 3, planes, 0)

    def finish(x, carry):
        for slot in range(8):
            out_ref[slot, x] = (
                sums[1, slot, x] + lane_roll(sums[0, slot, x], -1) + lane_roll(sums[2, slot, x], 1)
            )
        return carry

    lax.fori_loop(0, 4, finish, 0)


def inner_pairs(positions, live):
    return kernel_call(
        inner_kernel,
        (shape((8, 4, 8, 128), F32),),
        (positions, live),
        (pltpu.VMEM((3, 4, 8, 4, 8, 128), F32), pltpu.VMEM((3, 8, 4, 8, 128), F32)),
    )[0]


def edge_kernel(
    inner_ref, pos_ref, live_ref, count_ref, below, above, low, high, out_ref,
    sides, near32, shifted, sums,
):
    row = iota((8, 128), 0)
    for index, msg in enumerate((low, high)):
        sides[index] = msg[0:X_NEAR, :].astype(F32) + msg[X_NEAR : 2 * X_NEAR, :].astype(F32)
    for index, msg in enumerate((below, above)):
        near32[index] = msg[0:128, :].astype(F32) + msg[128:256, :].astype(F32)

    def fill_face(index, carry):
        for slot in range(8):
            for step_y in range(3):
                values = [
                    sides[index, pl.ds(step_y * 32 + 8 * k + slot, 8, stride=32), :]
                    for k in range(4)
                ]
                values[0] = values[0] + (2 * index - 1).astype(F32)
                values[1] = values[1] + F32(step_y - 1)
                for step_z in range(3):
                    moved = [lane_roll(value, 1 - step_z) for value in values]
                    moved[2] = moved[2] + F32(step_z - 1)
                    for k in range(4):
                        shifted[step_y * 3 + step_z, k, slot] = moved[k]
        return carry

    def gather(goals, totals):
        def body(index, carry):
            carry = list(carry)
            for slot in range(8):
                source = [shifted[index, k, slot] for k in range(4)]
                for goal in range(8):
                    carry[goal] = carry[goal] + source[3] * inverse_distance(goals[goal], source)
            return tuple(carry)

        return lax.fori_loop(0, 9, body, tuple(totals))

    def face(index, carry):
        fill_face(index, 0)
        x = 3 * index
        goals = [[pos_ref[axis, slot, x] for axis in range(3)] for slot in range(8)]
        totals = gather(goals, [inner_ref[slot, x] for slot in range(8)])
        for slot in range(8):
            sums[slot, x] = totals[slot]
        return carry

    lax.fori_loop(0, 2, face, 0)
    for x in (1, 2):
        for slot in range(8):
            sums[slot, x] = inner_ref[slot, x]
    upper = row >= 4
    turn = jnp.where(upper, F32(1.0), F32(-1.0))
    for slot in range(8):
        for k in range(4):
            r = 8 * k + slot
            none = jnp.zeros((1, 128), F32)
            source = [
                [none] + [near32[side, pl.ds(x * 32 + r, 1), :] for x in range(4)] + [none]
                for side in range(2)
            ]
            for step_x in range(3):
                value = jnp.concatenate(
                    source[0][step_x : step_x + 4] + source[1][step_x : step_x + 4], axis=0
                )
                if k == 0:
                    value = value + F32(step_x - 1)
                if k == 1:
                    value = value + turn
                for step_z in range(3):
                    moved = lane_roll(value, 1 - step_z)
                    if k == 2:
                        moved = moved + F32(step_z - 1)
                    shifted[step_x * 3 + step_z, k, slot] = moved

    def edge_rows(ref, lead):
        return jnp.concatenate(
            [ref[lead + (x, pl.ds(0, 1))] for x in range(4)]
            + [ref[lead + (x, pl.ds(7, 1))] for x in range(4)],
            axis=0,
        )

    goals = [[edge_rows(pos_ref, (axis, slot)) for axis in range(3)] for slot in range(8)]
    totals = gather(goals, [jnp.zeros((8, 128), F32) for slot in range(8)])
    for slot in range(8):
        for x in range(4):
            sums[slot, x, pl.ds(0, 1)] = sums[slot, x, pl.ds(0, 1)] + totals[slot][x : x + 1]
            sums[slot, x, pl.ds(7, 1)] = sums[slot, x, pl.ds(7, 1)] + totals[slot][x + 4 : x + 5]
    for slot in range(8):
        out_ref[slot] = jnp.where(count_ref[...] > slot, -sums[slot] / 8, F32(0.0))


def edge_pairs(inner, positions, live, counts, below, above, low, high):
    return kernel_call(
        edge_kernel,
        (shape((8, 4, 8, 128), F32),),
        (inner, positions, live, counts, below, above, low, high),
        (
            pltpu.VMEM((2, X_NEAR, 128), F32),
            pltpu.VMEM((2, 128, 128), F32),
            pltpu.VMEM((9, 4, 8, 8, 128), F32),
            pltpu.VMEM((8, 4, 8, 128), F32),
        ),
    )[0]


def far_starts():
    starts, count = {}, 0
    for step_x in range(-3, 4):
        for step_y in range(-3, 4):
            starts[step_x, step_y] = count * COEF
            count += 7 if max(abs(step_x), abs(step_y)) >= 2 else 4
    return starts


def operator_kernel(far_ref, out_ref, far32, stack):
    far32[:, 0:11264] = far_ref[:, 0:11264].astype(F32)
    far32[:, 11264:11520] = jnp.zeros((COEF, 256), F32)
    far32[:, 11264:11376] = far_ref[:, 11264:11376].astype(F32)
    lane = iota((COEF, 256), 1)

    def window(start):
        base = start // 128 * 128
        value = far32[:, base : base + 384]
        shift = start - base
        return (pltpu.roll(value, 384 - shift, 1) if shift else value)[:, 0:256]

    starts = far_starts()
    for step_x in range(-3, 4):
        for step_y in range(-3, 4):
            start = starts[step_x, step_y]
            if max(abs(step_x), abs(step_y)) >= 2:
                block = jnp.where(lane < 7 * COEF, window(start), F32(0.0))
            else:
                block = jnp.where(
                    lane < 2 * COEF,
                    window(start),
                    jnp.where(
                        (lane >= 5 * COEF) & (lane < 7 * COEF), window(start - 3 * COEF), F32(0.0)
                    ),
                )
            for bit_x in range(2):
                for bit_y in range(2):
                    source_x, source_y = step_x + bit_x, step_y + bit_y
                    if -2 <= source_x <= 3 and -2 <= source_y <= 3:
                        shift_x, child_x = source_x // 2 + 1, source_x % 2
                        shift_y, child_y = source_y // 2 + 1, source_y % 2
                        first = shift_y * GROUP + (2 * child_x + child_y) * COEF
                        bits = (2 * bit_x + bit_y) * 256
                        stack[shift_x, first : first + COEF, bits : bits + 256] = block
    for shift_x in range(3):
        for k in range(8):
            out_ref[shift_x, k * 128 : (k + 1) * 128, :] = jnp.transpose(
                stack[shift_x, :, k * 128 : (k + 1) * 128]
            ).astype(BF16)


def far_matrix(far_operator):
    return kernel_call(
        operator_kernel,
        (shape((3, 1024, 3 * GROUP), BF16),),
        (far_operator,),
        (pltpu.VMEM((COEF, 11520), F32), pltpu.VMEM((3, 3 * GROUP, 1024), F32)),
    )[0]


def z_sum(products, bits, lanes, roll):
    odd = iota((COEF, 128), 1) % 2 == 1
    total = None
    for step in range(-3, 4):
        first = bits * 256 + (step + 3) * COEF
        value = roll(products[first : first + COEF, lanes], step)
        if step == 3:
            value = jnp.where(odd, F32(0.0), value)
        if step == -3:
            value = jnp.where(odd, value, F32(0.0))
        total = value if total is None else total + value
    return total


def leaf_roll(value, step):
    return lane_roll(value, -step)


def six_roll(value, step):
    if not step:
        return value
    cell = iota(value.shape, 1) % 64 + step
    inside = (cell >= 0) & (cell < 64)
    return jnp.where(inside, lane_roll(value, -step), lane_roll(value, 64 - step))


def coarse_roll(value, step):
    if not step:
        return value
    lane = iota(value.shape, 1)
    period = jnp.where(lane < 32, 32, jnp.where(lane < 48, 16, 8))
    cell = jnp.where(lane < 32, lane, jnp.where(lane < 48, lane - 32, lane - 48))
    inside = (cell + step >= 0) & (cell + step < period)
    sign = 1 if step > 0 else -1
    wrapped = jnp.where(
        period == 32,
        lane_roll(value, sign * 32 - step),
        jnp.where(period == 16, lane_roll(value, sign * 16 - step), lane_roll(value, sign * 8 - step)),
    )
    return jnp.where(inside, lane_roll(value, -step), wrapped)


def far_kernel(
    place, matrix, grid_ref, mine, below, above, low, high, near_three, up_three, down_three,
    up_ref, down_ref, out_ref, cells, fives, fours, three32, products, coarse, down32, downs, expand,
    lifted,
):
    gx, gy = place[0], place[1]
    row, col = iota((128, 128), 0), iota((128, 128), 1)
    cells[:, 0:128] = low[X_LEAF:X_SIX, :]
    cells[:, 384:512] = high[X_LEAF:X_SIX, :]
    for xp in range(2):
        lanes = slice(128 + 128 * xp, 256 + 128 * xp)
        source = Y_LEAF + xp * GROUP
        cells[0:GROUP, lanes] = below[source : source + GROUP, :]
        cells[GROUP : 5 * GROUP, lanes] = grid_ref[xp * 4 * GROUP : (xp + 1) * 4 * GROUP, :]
        cells[5 * GROUP : 6 * GROUP, lanes] = above[source : source + GROUP, :]
    size = lax.axis_size("gx")
    for shift, msg, first in (
        (-1, near_three, 0), (0, near_three, 80), (1, near_three, 160),
        (-4, up_three, 0), (-3, up_three, 80), (-2, up_three, 160),
        (2, down_three, 0), (3, down_three, 80), (4, down_three, 160),
    ):
        at = pl.multiple_of(lax.rem(gx + shift + size, size) * 72, 8)
        fives[pl.ds(at, 72), :] = msg[first : first + 72, :].astype(F32)
    even_up, odd_up = up_blocks(up_ref)

    def upward(grouped, split):
        children = dot(grouped.astype(BF16), split).astype(BF16)
        value = dot(even_up, children) + lane_roll(dot(odd_up, children), 64)
        return value.astype(BF16).astype(F32)

    lane = col % 64
    split_five = one_hot(
        (row == ((lane // 16 % 2) * 2 + lane // 32) * 32 + 2 * (lane % 16) + col // 64)
    )
    for x in range(4):
        value = upward(fives[x * GROUP : (x + 1) * GROUP, :], split_five)
        first = (x // 2) * GROUP + (x % 2) * 2 * COEF
        fours[first : first + COEF, :] = value
        fours[first + COEF : first + 2 * COEF, :] = lane_roll(value, 96)
    split_four = one_hot((row == (lane // 8) * 16 + 2 * (lane % 8) + col // 64) & (lane < 16))
    for x in range(2):
        value = upward(fours[x * GROUP : (x + 1) * GROUP, :], split_four)
        three32[x * 2 * COEF : x * 2 * COEF + COEF, :] = value
        three32[x * 2 * COEF + COEF : (x + 1) * 2 * COEF, :] = lane_roll(value, 120)
    three = dot(three32[...].astype(BF16), one_hot((row == col - 48) & (col >= 48) & (col < 56)))
    halo = jnp.where(
        iota((GROUP, 128), 1) < 64,
        above[Y_SIX:Y_FIVE, :].astype(F32),
        below[Y_SIX:Y_FIVE, :].astype(F32),
    )
    wide_low = iota((GROUP, 128), 1) < 64
    total = None
    for shift_x in range(3):
        if shift_x == 1:
            own, other = mine[Y_SIX:Y_FIVE, :].astype(F32), halo
        else:
            msg = low if shift_x == 0 else high
            own = msg[X_SIX:X_HALO, :].astype(F32)
            other = msg[X_HALO:X_FIVE, :].astype(F32)
        six = [
            lane_roll(jnp.where(wide_low, own, other), 64),
            own,
            lane_roll(jnp.where(wide_low, other, own), 64),
        ]
        at = pl.multiple_of(lax.rem(gx // 2 + shift_x + 3, 4) * GROUP, 8)
        five = fives[pl.ds(at, GROUP), :].astype(BF16)
        at = pl.multiple_of(lax.rem(gx // 4 + shift_x + 1, 2) * GROUP, 8)
        four = fours[pl.ds(at, GROUP), :].astype(BF16)
        blocks = []
        for shift_y in range(3):
            y_five = lax.rem(gy + shift_y + 3, 4)
            y_four = lax.rem(gy // 2 + shift_y + 1, 2)
            part = dot(five, one_hot((row == y_five * 32 + col) & (col < 32)))
            part = part + dot(
                four, one_hot((row == y_four * 16 + col - 32) & (col >= 32) & (col < 48))
            )
            blocks.append(jnp.concatenate([six[shift_y], part + three], axis=1))
        window = jnp.concatenate(blocks, axis=0).astype(BF16)
        term = dot(matrix[shift_x], window)
        total = term if total is None else total + term
    products[...] = total
    for bits in range(4):
        coarse[bits, 0:COEF, 0:128] = z_sum(products, bits, slice(0, 128), six_roll)
        coarse[bits, 0:COEF, 128:256] = z_sum(products, bits, slice(128, 256), coarse_roll)
    eye = one_hot(iota((8 * COEF, 8 * COEF), 0) == iota((8 * COEF, 8 * COEF), 1))
    down32[...] = dot_nt(eye, down_ref[...])
    downs[...] = jnp.zeros_like(downs)
    for bits in range(4):
        for bit in range(2):
            first = (2 * bits + bit) * COEF
            downs[bit, bits * 40 : bits * 40 + COEF, :] = down32[first : first + COEF, :]
    operators = [downs[bit].astype(BF16) for bit in range(2)]

    def spread(value, mask):
        return [dot(part, one_hot(mask)).astype(BF16) for part in parts(value)]

    def lift(wide, lanes):
        halves = [dot(value, wide[0]) + dot(value, wide[1]) for value in operators]
        lifted[:, lanes] = jnp.where(iota(halves[0].shape, 1) % 2 == 1, halves[1], halves[0])

    def child(bits, lanes):
        first = bits * 40 if isinstance(bits, int) else pl.multiple_of(bits * 40, 8)
        return lifted[pl.ds(first, COEF), lanes]

    first_lanes = slice(0, 128)

    right = slice(128, 256)
    bits = 2 * lax.rem(gx // 4, 2) + lax.rem(gy // 2, 2)
    value = coarse[bits, 0:COEF, right]
    wide = spread(value, (row == 48 + (col - 32) // 2) & (col >= 32) & (col < 48))
    bits = 2 * lax.rem(gx // 2, 2) + lax.rem(gy, 2)
    lift(wide, first_lanes)
    value = coarse[bits, 0:COEF, right] + child(bits, first_lanes)
    wide = spread(value, (row == 32 + col // 2) & (col < 32))
    lift(wide, first_lanes)
    wides = []
    for y in range(2):
        bits = 2 * lax.rem(gx, 2) + y
        value = coarse[bits, 0:COEF, right] + child(bits, first_lanes)
        wides.append(spread(value, (row == (col % 64) // 2) & (col // 64 == y)))
    wide = [(a.astype(F32) + b.astype(F32)).astype(BF16) for a, b in zip(*wides)]
    lift(wide, first_lanes)
    for bits in range(4):
        value = coarse[bits, 0:COEF, 0:128] + child(bits, first_lanes)
        for y in range(2):
            for k, part in enumerate(spread(value, row == y * 64 + col // 2)):
                at = ((bits // 2) * 4 + 2 * y + bits % 2) * 128
                expand[k, :, at : at + 128] = part
    lift([expand[k] for k in range(2)], slice(0, 1024))
    for parent in range(4):
        rows = slice(parent * GROUP, (parent + 3) * GROUP)
        total = None
        for shift_x in range(3):
            lanes = slice(shift_x * 128, shift_x * 128 + 256)
            term = dot(matrix[shift_x], cells[rows, lanes])
            total = term if total is None else total + term
        products[...] = total
        for xp in range(2):
            at = (xp * 4 + parent) * 128
            for bits in range(4):
                value = z_sum(products, bits, slice(xp * 128, xp * 128 + 128), leaf_roll)
                value = value + child(bits, slice(at, at + 128))
                x, y = 2 * xp + bits // 2, 2 * parent + bits % 2
                out_ref[pl.ds(x * 8 + y, COEF, stride=32), :] = value


def all_levels(*inputs):
    return kernel_call(
        far_kernel,
        (shape((1152, 128), F32),),
        inputs,
        (
            pltpu.VMEM((6 * GROUP, 512), BF16),
            pltpu.VMEM((576, 128), F32),
            pltpu.VMEM((2 * GROUP, 128), F32),
            pltpu.VMEM((GROUP, 128), F32),
            pltpu.VMEM((1024, 256), F32),
            pltpu.VMEM((4, 40, 256), F32),
            pltpu.VMEM((8 * COEF, COEF), F32),
            pltpu.VMEM((2, 160, COEF), F32),
            pltpu.VMEM((2, COEF, 1024), BF16),
            pltpu.VMEM((160, 1024), F32),
        ),
        scalars=1,
    )[0]


def moved(value, step_x, step_y):
    size_x, size_y = lax.axis_size("gx"), lax.axis_size("gy")
    table = [
        (x * size_y + y, (x + step_x) % size_x * size_y + (y + step_y) % size_y)
        for x in range(size_x)
        for y in range(size_y)
    ]
    return lax.ppermute(value, ("gx", "gy"), table)


def per_device(
    leaf_multipoles, positions, masses, counts, up_operator, far_operator, down_operator
):
    place = jnp.stack([lax.axis_index("gx"), lax.axis_index("gy")]).astype(jnp.int32)
    flat_positions = positions.reshape(768, 128)
    flat_counts = counts.reshape(32, 128)
    grid, up_msg, down_msg, five, live = prepare(
        place, leaf_multipoles.reshape(1152, 128), flat_positions, masses.reshape(256, 128),
        flat_counts, up_operator,
    )
    below = moved(up_msg, 0, 1)
    above = moved(down_msg, 0, -1)
    two = moved(five, 0, 2)
    live_cells = live.reshape(8, 4, 8, 128)
    matrix = far_matrix(far_operator)
    below, above, two, matrix = lax.optimization_barrier((below, above, two, matrix))
    to_low, to_high = cross(below, above, two, up_msg, grid, flat_positions, live)
    low = moved(to_high, 1, 0)
    high = moved(to_low, -1, 0)
    inner = inner_pairs(positions, live_cells)
    low, high, inner = lax.optimization_barrier((low, high, inner))
    own_five = to_low[X_FIVE:]
    three = jnp.concatenate([low[X_FIVE:], own_five, high[X_FIVE:]], axis=0)
    up_three = moved(three, 3, 0)
    down_three = moved(three, -3, 0)
    potential = edge_pairs(inner, positions, live_cells, counts, below, above, low, high)
    up_three, down_three, potential = lax.optimization_barrier((up_three, down_three, potential))
    expansion = all_levels(
        place, matrix, grid, up_msg, below, above, low, high, three, up_three, down_three,
        up_operator, down_operator,
    )
    return expansion.reshape(36, 4, 8, 128), potential


def extended(cells, sides, width):
    for axis, dim in sides:
        count = lax.axis_size(axis)
        head = lax.slice_in_dim(cells, 0, width, axis=dim)
        tail = lax.slice_in_dim(cells, cells.shape[dim] - width, cells.shape[dim], axis=dim)
        cells = jnp.concatenate(
            [
                lax.ppermute(tail, axis, [(i, (i + 1) % count) for i in range(count)]),
                cells,
                lax.ppermute(head, axis, [((i + 1) % count, i) for i in range(count)]),
            ],
            axis=dim,
        )
    return cells


def shift_list():
    return [
        (step_x, step_y, step_z)
        for step_x in (-1, 0, 1)
        for step_y in (-1, 0, 1)
        for step_z in (-1, 0, 1)
    ]


def child_bits(number):
    return (number // 4, number // 2 % 2, number % 2)


def offset_table():
    vectors = [
        (step_x, step_y, step_z)
        for step_x in range(-3, 4)
        for step_y in range(-3, 4)
        for step_z in range(-3, 4)
        if max(abs(step_x), abs(step_y), abs(step_z)) >= 2
    ]
    lookup = np.full((27, 8, 8), len(vectors), dtype=np.int32)
    for shift_id, offset in enumerate(shift_list()):
        for source in range(8):
            for target in range(8):
                vector = tuple(
                    (
                        2 * offset[axis_id]
                        + child_bits(source)[axis_id]
                        - child_bits(target)[axis_id]
                        for axis_id in range(3)
                    )
                )
                if max(abs(vector[0]), abs(vector[1]), abs(vector[2])) >= 2:
                    lookup[shift_id, source, target] = vectors.index(vector)
    return lookup


def assemble(far_operator):
    coeff_count = far_operator.shape[0]
    blocks = far_operator.reshape(coeff_count, -1, coeff_count)
    blocks = jnp.concatenate(
        [blocks, jnp.zeros((coeff_count, 1, coeff_count), blocks.dtype)], axis=1
    )
    picked = jnp.take(blocks, jnp.asarray(offset_table().reshape(-1), dtype=jnp.int32), axis=1)
    picked = picked.reshape(coeff_count, 27, 8, 8, coeff_count).transpose(1, 2, 0, 3, 4)
    return picked.reshape(27, 8 * coeff_count, 8 * coeff_count)


def group_cells(volume):
    size_x, size_y, size_z, coeff_count = volume.shape
    reshaped = volume.reshape(size_x // 2, 2, size_y // 2, 2, size_z // 2, 2, coeff_count)
    return reshaped.transpose(0, 2, 4, 1, 3, 5, 6).reshape(
        size_x // 2, size_y // 2, size_z // 2, 8 * coeff_count
    )


def spread_cells(grouped):
    size_x, size_y, size_z, total_rows = grouped.shape
    coeff_count = total_rows // 8
    reshaped = grouped.reshape(size_x, size_y, size_z, 2, 2, 2, coeff_count)
    return reshaped.transpose(0, 3, 1, 4, 2, 5, 6).reshape(
        2 * size_x, 2 * size_y, 2 * size_z, coeff_count
    )


def wrap_pad(volume, axis_id):
    extent = volume.shape[axis_id]
    lower = lax.slice_in_dim(volume, extent - 1, extent, axis=axis_id)
    upper = lax.slice_in_dim(volume, 0, 1, axis=axis_id)
    return jnp.concatenate([lower, volume, upper], axis=axis_id)


def wrap_window(volume, axis_id, anchor, extent):
    return lax.dynamic_slice_in_dim(wrap_pad(volume, axis_id), anchor, extent + 2, axis_id)


def region(index_now, cells, levels_up):
    anchor = index_now * cells // 2**levels_up
    extent = max(cells // 2**levels_up, 1)
    return (anchor, extent)


def cut(children, index_x, index_y, cells_x, cells_y, levels_up):
    anchor_x, extent_x = region(index_x, cells_x, levels_up)
    parent_x = region(index_x, cells_x, levels_up + 1)[0]
    anchor_y, extent_y = region(index_y, cells_y, levels_up)
    parent_y = region(index_y, cells_y, levels_up + 1)[0]
    children = lax.dynamic_slice_in_dim(children, anchor_x - 2 * parent_x, extent_x, 0)
    return lax.dynamic_slice_in_dim(children, anchor_y - 2 * parent_y, extent_y, 1)


def coarse_window(grouped, index_x, index_y, cells_x, cells_y, levels_up):
    anchor_x, extent_x = region(index_x, cells_x, levels_up)
    anchor_y, extent_y = region(index_y, cells_y, levels_up)
    windowed = wrap_window(grouped, 0, anchor_x, extent_x)
    windowed = wrap_window(windowed, 1, anchor_y, extent_y)
    return wrap_pad(windowed, 2)


def upward(up_operator, grouped):
    parent = jnp.einsum("xyzs,sj->xyzj", grouped, up_operator, preferred_element_type=jnp.float32)
    return parent.astype(jnp.bfloat16)


def downward(down_operator, parent):
    children = jnp.einsum(
        "xyzi,it->xyzt", parent, down_operator.astype(jnp.float32), precision=lax.Precision.HIGHEST
    )
    return spread_cells(children)


def far_field(padded, kernel):
    size_x = padded.shape[0] - 2
    size_y = padded.shape[1] - 2
    size_z = padded.shape[2] - 2
    running = None
    for shift_id, offset in enumerate(shift_list()):
        window_piece = padded[
            1 + offset[0] : 1 + offset[0] + size_x, 1 + offset[1] : 1 + offset[1] + size_y
        ]
        product_term = jnp.einsum(
            "xyzs,st->xyzt", window_piece, kernel[shift_id], preferred_element_type=jnp.float32
        )
        product_term = product_term[:, :, 1 + offset[2] : 1 + offset[2] + size_z]
        running = product_term if running is None else running + product_term
    return running


def near_field(positions, masses, counts):
    slot_count = masses.shape[0]
    size_x, size_y, size_z = (masses.shape[1], masses.shape[2], masses.shape[3])
    live_slot = lax.broadcasted_iota(jnp.int32, masses.shape, 0) < counts[None]
    live_mass = jnp.where(live_slot, masses, jnp.float32(0.0))
    stacked = jnp.concatenate([positions, live_mass[None]], axis=0)
    padded = wrap_pad(extended(stacked, (("gx", 2), ("gy", 3)), 1), 4)
    block_size = min(8, slot_count)
    same_slot = lax.broadcasted_iota(
        jnp.int32, (block_size, slot_count, 1, 1, 1), 0
    ) + 0 == lax.broadcasted_iota(jnp.int32, (block_size, slot_count, 1, 1, 1), 1)
    running = jnp.zeros((block_size, size_x, size_y, size_z), jnp.float32)
    for offset in shift_list():
        source = padded[
            :,
            :,
            1 + offset[0] : 1 + offset[0] + size_x,
            1 + offset[1] : 1 + offset[1] + size_y,
            1 + offset[2] : 1 + offset[2] + size_z,
        ]
        squared = jnp.float32(SOFTENING * SOFTENING)
        for axis_id in range(3):
            separation = (
                source[axis_id][None] + jnp.float32(offset[axis_id]) - positions[axis_id][:, None]
            )
            squared = squared + separation * separation
        pair_terms = source[3][None] * lax.rsqrt(squared)
        if offset == (0, 0, 0):
            pair_terms = jnp.where(same_slot, jnp.float32(0.0), pair_terms)
        running = running + jnp.sum(pair_terms, axis=1)
    results = running
    running = results
    return jnp.where(live_slot, -running / slot_count, jnp.float32(0.0))


def general_device(
    leaf_multipoles, positions, masses, counts, up_operator, far_operator, down_operator
):
    potential = near_field(positions, masses, counts)
    kernel = assemble(far_operator)
    index_x = lax.axis_index("gx")
    index_y = lax.axis_index("gy")
    cells_x = leaf_multipoles.shape[1]
    cells_y = leaf_multipoles.shape[2]
    leaf_cells = jnp.transpose(leaf_multipoles, (1, 2, 3, 0))
    grouped_leaf = group_cells(leaf_cells)
    padded = wrap_pad(extended(grouped_leaf, (("gx", 0), ("gy", 1)), 1), 2)
    far_leaf = spread_cells(far_field(padded, kernel))
    grouped_six = group_cells(upward(up_operator, grouped_leaf))
    padded = wrap_pad(extended(grouped_six, (("gx", 0), ("gy", 1)), 1), 2)
    far_six = spread_cells(far_field(padded, kernel))
    moments_five = upward(up_operator, grouped_six)
    columns = lax.all_gather(moments_five, "gy", axis=1, tiled=True)
    whole_five = lax.all_gather(columns, "gx", axis=0, tiled=True)
    grouped_five = group_cells(whole_five)
    window_five = coarse_window(grouped_five, index_x, index_y, cells_x, cells_y, 3)
    moments_four = upward(up_operator, grouped_five)
    far_five = cut(
        spread_cells(far_field(window_five, kernel)), index_x, index_y, cells_x, cells_y, 2
    )
    grouped_four = group_cells(moments_four)
    window_four = coarse_window(grouped_four, index_x, index_y, cells_x, cells_y, 4)
    far_four = cut(
        spread_cells(far_field(window_four, kernel)), index_x, index_y, cells_x, cells_y, 3
    )
    grouped_three = group_cells(upward(up_operator, grouped_four))
    window_three = coarse_window(grouped_three, index_x, index_y, cells_x, cells_y, 5)
    far_three = cut(
        spread_cells(far_field(window_three, kernel)), index_x, index_y, cells_x, cells_y, 4
    )
    expansion = far_three
    expansion = far_four + cut(
        downward(down_operator, expansion), index_x, index_y, cells_x, cells_y, 3
    )
    expansion = far_five + cut(
        downward(down_operator, expansion), index_x, index_y, cells_x, cells_y, 2
    )
    expansion = far_six + cut(
        downward(down_operator, expansion), index_x, index_y, cells_x, cells_y, 1
    )
    expansion = far_leaf + cut(
        downward(down_operator, expansion), index_x, index_y, cells_x, cells_y, 0
    )
    return (jnp.transpose(expansion, (3, 0, 1, 2)), potential)


def solution(mesh):
    small = (mesh.shape["gx"], mesh.shape["gy"]) == (8, 4)
    return jax.shard_map(
        per_device if small else general_device,
        mesh=mesh,
        in_specs=(
            P(None, "gx", "gy", None),
            P(None, None, "gx", "gy", None),
            P(None, "gx", "gy", None),
            P("gx", "gy", None),
            P(),
            P(),
            P(),
        ),
        out_specs=(P(None, "gx", "gy", None), P(None, "gx", "gy", None)),
        check_vma=False,
    )
```

```python
import functools

import jax
import jax.numpy as jnp
import numpy as np
from jax import lax
from jax.experimental import pallas as pl
from jax.experimental.pallas import tpu as pltpu
from jax.sharding import PartitionSpec as P

SOFTENING = 0.05
EPS = SOFTENING * SOFTENING
F32 = jnp.float32
BF16 = jnp.bfloat16
COEF = 36
GROUP = 4 * COEF
Y_LEAF = 256
Y_SIX = Y_LEAF + 2 * GROUP
Y_FIVE = Y_SIX + GROUP // 2
Y_ROWS = Y_FIVE + 40
X_LEAF = 512
X_SIX = X_LEAF + 4 * GROUP
X_ROWS = X_SIX + GROUP
C_LEAF = 128
C_SIX = C_LEAF + 2 * GROUP
C_FIVE = C_SIX + GROUP
C_ROWS = C_FIVE + 80

VMEM = pl.BlockSpec(memory_space=pltpu.VMEM)
SMEM = pl.BlockSpec(memory_space=pltpu.SMEM)
HBM = pl.BlockSpec(memory_space=pltpu.MemorySpace.HBM)


def shape(dims, dtype):
    return jax.ShapeDtypeStruct(dims, dtype)


def kernel_call(body, outs, inputs, scratch=(), scalars=0, space=VMEM, limit=48):
    return pl.pallas_call(
        body,
        out_shape=outs,
        in_specs=[SMEM] * scalars + [space] * (len(inputs) - scalars),
        out_specs=[VMEM] * len(outs),
        scratch_shapes=list(scratch),
        compiler_params=pltpu.CompilerParams(vmem_limit_bytes=limit * 1024 * 1024),
    )(*inputs)


def iota(dims, axis):
    return lax.broadcasted_iota(jnp.int32, dims, axis)


def dot(lhs, rhs):
    return lax.dot_general(lhs, rhs, (((1,), (0,)), ((), ())), preferred_element_type=F32)


def dot_nt(lhs, rhs):
    return lax.dot_general(lhs, rhs, (((1,), (1,)), ((), ())), preferred_element_type=F32)


def one_hot(mask):
    return jnp.where(mask, F32(1.0), F32(0.0)).astype(BF16)


def parts(value):
    high = value.astype(BF16)
    return high, (value - high.astype(F32)).astype(BF16)


def lane_roll(value, shift):
    return pltpu.roll(value, shift % 128, 1) if shift % 128 else value


def up_blocks(up_ref):
    row, col = iota((8 * COEF, GROUP), 0), iota((8 * COEF, GROUP), 1)
    return [
        dot(up_ref[...], one_hot(row == (col // COEF * 2 + bit) * COEF + col % COEF)).astype(BF16)
        for bit in range(2)
    ]


def prep_kernel(
    leaf_hbm, pos_hbm, mass_hbm, count_hbm, up_hbm, down_hbm, far_hbm,
    grid_ref, up_msg, down_msg, low_msg, high_msg, six_ref, five_ref, live_ref,
    pos_ref, count_ref, up_ref, down_ref, far_ref,
    leaf_ref, mass_ref, m32, x32, six32, near32, sems,
):
    copies = [
        pltpu.make_async_copy(source, target, sems.at[k])
        for k, (source, target) in enumerate(
            (
                (leaf_hbm, leaf_ref), (pos_hbm, pos_ref), (mass_hbm, mass_ref),
                (count_hbm, count_ref), (up_hbm, up_ref), (down_hbm, down_ref), (far_hbm, far_ref),
            )
        )
    ]
    for copy in copies:
        copy.start()
    copies[0].wait()
    m32[...] = leaf_ref[...].astype(F32)
    for x in range(4):
        for y in range(8):
            start = ((x // 2) * 4 + y // 2) * GROUP + (2 * (x % 2) + y % 2) * COEF
            x32[start : start + COEF, :] = m32[pl.ds(x * 8 + y, COEF, stride=32), :]
    grid = x32[...].astype(BF16)
    grid_ref[...] = grid
    for msg, parent in ((up_msg, 3), (down_msg, 0)):
        for xp in range(2):
            msg[Y_LEAF + xp * GROUP : Y_LEAF + (xp + 1) * GROUP, :] = grid_ref[
                (xp * 4 + parent) * GROUP : (xp * 4 + parent + 1) * GROUP, :
            ]
    low_msg[X_LEAF:X_SIX, :] = grid_ref[0 : 4 * GROUP, :]
    high_msg[X_LEAF:X_SIX, :] = grid_ref[4 * GROUP : 8 * GROUP, :]
    for copy in copies[1:5]:
        copy.wait()
    count = count_ref[...]
    for slot in range(8):
        live_ref[slot * 32 : slot * 32 + 32, :] = jnp.where(
            count > slot, mass_ref[slot * 32 : slot * 32 + 32, :], F32(0.0)
        )
    for msg, y in ((up_msg, 7), (down_msg, 0)):
        rows = []
        for x in range(4):
            rows.append(pos_ref[pl.ds(x * 8 + y, 24, stride=32), :])
            rows.append(live_ref[pl.ds(x * 8 + y, 8, stride=32), :])
        high, low = parts(jnp.concatenate(rows, axis=0))
        msg[0:128, :] = high
        msg[128:256, :] = low
    for msg, x in ((low_msg, 0), (high_msg, 3)):
        for slot in range(8):
            for axis in range(3):
                start = (axis * 8 + slot) * 32 + x * 8
                near32[pl.ds(axis * 8 + slot, 8, stride=32), :] = pos_ref[start : start + 8, :]
            start = slot * 32 + x * 8
            near32[pl.ds(24 + slot, 8, stride=32), :] = live_ref[start : start + 8, :]
        high, low = parts(near32[...])
        msg[0:256, :] = high
        msg[256:512, :] = low
    low_half = iota((COEF, 128), 1) < 64
    even_up, odd_up = up_blocks(up_ref)
    row, col = iota((128, 128), 0), iota((128, 128), 1)
    split_z = one_hot(row == 2 * (col % 64) + col // 64)
    split = dot(grid, split_z).astype(BF16)
    columns = jnp.concatenate([split[k * GROUP : (k + 1) * GROUP] for k in range(8)], axis=1)
    even, odd = dot(even_up, columns), dot(odd_up, columns)
    for xp in range(2):
        for y in range(2):
            first, second = (xp * 4 + y) * 128, (xp * 4 + 2 + y) * 128
            near_part = even[:, first : first + 128] + lane_roll(odd[:, first : first + 128], 64)
            far_part = lane_roll(even[:, second : second + 128], 64) + odd[:, second : second + 128]
            start = (2 * xp + y) * COEF
            six32[start : start + COEF, :] = jnp.where(low_half, near_part, far_part)
    six = six32[...].astype(BF16)
    six_ref[...] = six
    low_msg[X_SIX:X_ROWS, :] = six
    high_msg[X_SIX:X_ROWS, :] = six
    left = iota((72, 128), 1) < 64
    first, second = six32[0:72, :], six32[72:144, :]
    up_msg[Y_SIX:Y_FIVE, :] = jnp.where(left, lane_roll(first, 64), second).astype(BF16)
    down_msg[Y_SIX:Y_FIVE, :] = jnp.where(left, first, lane_roll(second, 64)).astype(BF16)
    split_six = one_hot(row == ((col // 32) % 2) * 64 + 2 * (col % 32) + col // 64)
    split = dot(six, split_six).astype(BF16)
    five = dot(even_up, split) + lane_roll(dot(odd_up, split), 64)
    five = jnp.concatenate([five, jnp.zeros((4, 128), F32)], axis=0).astype(BF16)
    five_ref[...] = five
    for msg in (up_msg, down_msg):
        msg[Y_FIVE:Y_ROWS, :] = five
    for copy in copies[5:]:
        copy.wait()


def prepare(leaf, positions, masses, counts, up_operator, down_operator, far_operator):
    inputs = (leaf, positions, masses, counts, up_operator, down_operator, far_operator)
    return kernel_call(
        prep_kernel,
        (
            shape((8 * GROUP, 128), BF16),
            shape((Y_ROWS, 128), BF16),
            shape((Y_ROWS, 128), BF16),
            shape((X_ROWS, 128), BF16),
            shape((X_ROWS, 128), BF16),
            shape((GROUP, 128), BF16),
            shape((40, 128), BF16),
            shape((256, 128), F32),
            shape((768, 128), F32),
            shape((32, 128), jnp.int32),
            shape(up_operator.shape, BF16),
            shape(down_operator.shape, BF16),
            shape(far_operator.shape, BF16),
        ),
        [pltpu.with_memory_space_constraint(value, pltpu.MemorySpace.HBM) for value in inputs],
        (
            pltpu.VMEM((1152, 128), BF16),
            pltpu.VMEM((256, 128), F32),
            pltpu.VMEM((1152, 128), F32),
            pltpu.VMEM((1152, 128), F32),
            pltpu.VMEM((GROUP, 128), F32),
            pltpu.VMEM((256, 128), F32),
            pltpu.SemaphoreType.DMA((7,)),
        ),
        space=HBM,
    )


def halo_six(below, above):
    upper, lower = above[Y_SIX:Y_FIVE, :].astype(F32), below[Y_SIX:Y_FIVE, :].astype(F32)
    left = iota((72, 128), 1) < 64
    return jnp.concatenate(
        [
            jnp.where(left, upper, lane_roll(lower, 64)),
            jnp.where(left, lane_roll(upper, 64), lower),
        ],
        axis=0,
    )


def cross_kernel(place, below, above, two, own, to_low, to_high, five32):
    lane = iota((COEF, 128), 1) // 32
    five32[...] = jnp.zeros_like(five32)
    for shift, ref, first in ((0, own, 0), (3, below, Y_FIVE), (1, above, Y_FIVE), (2, two, 0)):
        at = lax.rem(place[1] + shift, 4)
        value = ref[first : first + 40, :].astype(F32)
        for y in range(2):
            moved = pltpu.roll(value, lax.rem(32 * at + 96 * y, 128), 1)[0:COEF]
            rows = slice(y * COEF, (y + 1) * COEF)
            five32[rows, :] = jnp.where(lane == at, moved, five32[rows, :])
    five = five32[...].astype(BF16)
    halo = halo_six(below, above).astype(BF16)
    for msg, x, xp in ((to_low, 0, 0), (to_high, 3, 1)):
        for side, ref in enumerate((below, above)):
            for half in range(2):
                source = half * 128 + x * 32
                first = side * 64 + half * 32
                msg[first : first + 32, :] = ref[source : source + 32, :]
            source, first = Y_LEAF + xp * GROUP, C_LEAF + side * GROUP
            msg[first : first + GROUP, :] = ref[source : source + GROUP, :]
        msg[C_SIX:C_FIVE, :] = halo
        msg[C_FIVE:C_ROWS, :] = five


def cross(*inputs):
    return kernel_call(
        cross_kernel,
        (shape((C_ROWS, 128), BF16), shape((C_ROWS, 128), BF16)),
        inputs,
        (pltpu.VMEM((80, 128), F32),),
        scalars=1,
    )


def inverse_distance(target, source):
    squared = F32(EPS)
    for axis in range(3):
        separation = source[axis] - target[axis]
        squared = squared + separation * separation
    return lax.rsqrt(squared)


def inner_kernel(pos_ref, live_ref, out_ref, shifted, sums):
    row = iota((8, 128), 0)
    sums[...] = jnp.zeros_like(sums)

    def fill(x, carry):
        for slot in range(8):
            values = [pos_ref[axis, slot, x] for axis in range(3)] + [live_ref[slot, x]]
            for index, step in enumerate((-1, 0, 1)):
                moved = [lane_roll(value, -step) for value in values]
                if step:
                    moved[2] = moved[2] + F32(step)
                for k in range(4):
                    shifted[index, k, slot, x] = moved[k]
        return carry

    lax.fori_loop(0, 4, fill, 0)

    def targets(x):
        return [[shifted[1, k, slot, x] for k in range(4)] for slot in range(8)]

    def pairs(goals, x, step, totals):
        step_x, step_y, step_z = step
        edge = row == (7 if step_y > 0 else 0)
        for slot in range(8):
            source = [shifted[step_z + 1, k, slot, x] for k in range(4)]
            if step_y:
                source = [pltpu.roll(value, (-step_y) % 8, 0) for value in source]
                source[1] = source[1] + F32(step_y)
                source[3] = jnp.where(edge, F32(0.0), source[3])
            if step_x:
                source[0] = source[0] + F32(step_x)
            back = None
            for goal in range(8):
                inverse = inverse_distance(goals[goal], source)
                totals[goal] = totals[goal] + source[3] * inverse
                term = goals[goal][3] * inverse
                back = term if back is None else back + term
            if step_y:
                back = pltpu.roll(jnp.where(edge, F32(0.0), back), step_y % 8, 0)
            sums[step_z + 1, slot, x] = sums[step_z + 1, slot, x] + back

    def plane(x, carry):
        goals = targets(x)
        totals = [jnp.zeros((8, 128), F32) for slot in range(8)]
        for slot in range(8):
            for goal in range(slot):
                inverse = inverse_distance(goals[goal], goals[slot])
                totals[goal] = totals[goal] + goals[slot][3] * inverse
                totals[slot] = totals[slot] + goals[goal][3] * inverse
        for step in ((0, 0, 1), (0, 1, -1), (0, 1, 0), (0, 1, 1)):
            pairs(goals, x, step, totals)
        for slot in range(8):
            sums[1, slot, x] = sums[1, slot, x] + totals[slot]
        return carry

    def planes(x, carry):
        for step_y in (-1, 0, 1):
            goals = targets(x)
            totals = [sums[1, slot, x] for slot in range(8)]
            for step_z in (-1, 0, 1):
                pairs(goals, x + 1, (1, step_y, step_z), totals)
            for slot in range(8):
                sums[1, slot, x] = totals[slot]
        return carry

    lax.fori_loop(0, 4, plane, 0)
    lax.fori_loop(0, 3, planes, 0)

    def finish(x, carry):
        for slot in range(8):
            out_ref[slot, x] = (
                sums[1, slot, x] + lane_roll(sums[0, slot, x], -1) + lane_roll(sums[2, slot, x], 1)
            )
        return carry

    lax.fori_loop(0, 4, finish, 0)


def inner_pairs(positions, live):
    return kernel_call(
        inner_kernel,
        (shape((8, 4, 8, 128), F32),),
        (positions, live),
        (pltpu.VMEM((3, 4, 8, 4, 8, 128), F32), pltpu.VMEM((3, 8, 4, 8, 128), F32)),
    )[0]


def gather(shifted, goals, totals):
    def body(index, carry):
        carry = list(carry)
        for slot in range(8):
            source = [shifted[index, k, slot] for k in range(4)]
            for goal in range(8):
                carry[goal] = carry[goal] + source[3] * inverse_distance(goals[goal], source)
        return tuple(carry)

    return lax.fori_loop(0, 9, body, tuple(totals))


def rows_kernel(inner_ref, pos_ref, below, above, out_ref, near32, shifted):
    row = iota((8, 128), 0)
    for index, msg in enumerate((below, above)):
        near32[index] = msg[0:128, :].astype(F32) + msg[128:256, :].astype(F32)
    turn = jnp.where(row >= 4, F32(1.0), F32(-1.0))
    none = jnp.zeros((1, 128), F32)
    for slot in range(8):
        for k in range(4):
            source = [
                [none] + [near32[side, pl.ds(x * 32 + 8 * k + slot, 1), :] for x in range(4)] + [none]
                for side in range(2)
            ]
            for step_x in range(3):
                value = jnp.concatenate(
                    source[0][step_x : step_x + 4] + source[1][step_x : step_x + 4], axis=0
                )
                if k == 0:
                    value = value + F32(step_x - 1)
                if k == 1:
                    value = value + turn
                for step_z in range(3):
                    moved = lane_roll(value, 1 - step_z)
                    if k == 2:
                        moved = moved + F32(step_z - 1)
                    shifted[step_x * 3 + step_z, k, slot] = moved

    def edge_rows(ref, lead):
        return jnp.concatenate(
            [ref[lead + (x, pl.ds(0, 1))] for x in range(4)]
            + [ref[lead + (x, pl.ds(7, 1))] for x in range(4)],
            axis=0,
        )

    goals = [[edge_rows(pos_ref, (axis, slot)) for axis in range(3)] for slot in range(8)]
    totals = gather(shifted, goals, [jnp.zeros((8, 128), F32) for slot in range(8)])
    out_ref[...] = inner_ref[...]
    for slot in range(8):
        for x in range(4):
            for y, r in ((0, x), (7, x + 4)):
                out_ref[slot, x, pl.ds(y, 1)] = out_ref[slot, x, pl.ds(y, 1)] + totals[slot][r : r + 1]


def faces_kernel(
    inner_ref, pos_ref, count_ref, low, high, low_corner, high_corner, out_ref, sides, shifted, sums
):
    for index, (msg, corner) in enumerate(((low, low_corner), (high, high_corner))):
        sides[index, 0:32, :] = corner[0:32, :].astype(F32) + corner[32:64, :].astype(F32)
        sides[index, 32:288, :] = msg[0:256, :].astype(F32) + msg[256:512, :].astype(F32)
        sides[index, 288:320, :] = corner[64:96, :].astype(F32) + corner[96:128, :].astype(F32)

    def face(index, carry):
        for slot in range(8):
            for step_y in range(3):
                values = [
                    sides[index, pl.ds(step_y * 32 + 8 * k + slot, 8, stride=32), :]
                    for k in range(4)
                ]
                values[0] = values[0] + (2 * index - 1).astype(F32)
                values[1] = values[1] + F32(step_y - 1)
                for step_z in range(3):
                    moved = [lane_roll(value, 1 - step_z) for value in values]
                    moved[2] = moved[2] + F32(step_z - 1)
                    for k in range(4):
                        shifted[step_y * 3 + step_z, k, slot] = moved[k]
        x = 3 * index
        goals = [[pos_ref[axis, slot, x] for axis in range(3)] for slot in range(8)]
        totals = gather(shifted, goals, [inner_ref[slot, x] for slot in range(8)])
        for slot in range(8):
            sums[slot, x] = totals[slot]
        return carry

    lax.fori_loop(0, 2, face, 0)
    for x in (1, 2):
        for slot in range(8):
            sums[slot, x] = inner_ref[slot, x]
    for slot in range(8):
        out_ref[slot] = jnp.where(count_ref[...] > slot, -sums[slot] / 8, F32(0.0))


def row_pairs(*inputs):
    return kernel_call(
        rows_kernel,
        (shape((8, 4, 8, 128), F32),),
        inputs,
        (pltpu.VMEM((2, 128, 128), F32), pltpu.VMEM((9, 4, 8, 8, 128), F32)),
    )[0]


def face_pairs(*inputs):
    return kernel_call(
        faces_kernel,
        (shape((8, 4, 8, 128), F32),),
        inputs,
        (
            pltpu.VMEM((2, 320, 128), F32),
            pltpu.VMEM((9, 4, 8, 8, 128), F32),
            pltpu.VMEM((8, 4, 8, 128), F32),
        ),
    )[0]


def far_starts():
    starts, count = {}, 0
    for step_x in range(-3, 4):
        for step_y in range(-3, 4):
            starts[step_x, step_y] = count * COEF
            count += 7 if max(abs(step_x), abs(step_y)) >= 2 else 4
    return starts


def operator_kernel(far_ref, out_ref, far32, stack):
    far32[:, 0:11264] = far_ref[:, 0:11264].astype(F32)
    far32[:, 11264:11520] = jnp.zeros((COEF, 256), F32)
    far32[:, 11264:11376] = far_ref[:, 11264:11376].astype(F32)
    lane = iota((COEF, 256), 1)

    def window(start):
        base = start // 128 * 128
        value = far32[:, base : base + 384]
        shift = start - base
        return (pltpu.roll(value, 384 - shift, 1) if shift else value)[:, 0:256]

    starts = far_starts()
    for step_x in range(-3, 4):
        for step_y in range(-3, 4):
            start = starts[step_x, step_y]
            if max(abs(step_x), abs(step_y)) >= 2:
                block = jnp.where(lane < 7 * COEF, window(start), F32(0.0))
            else:
                block = jnp.where(
                    lane < 2 * COEF,
                    window(start),
                    jnp.where(
                        (lane >= 5 * COEF) & (lane < 7 * COEF), window(start - 3 * COEF), F32(0.0)
                    ),
                )
            for bit_x in range(2):
                for bit_y in range(2):
                    source_x, source_y = step_x + bit_x, step_y + bit_y
                    if -2 <= source_x <= 3 and -2 <= source_y <= 3:
                        shift_x, child_x = source_x // 2 + 1, source_x % 2
                        shift_y, child_y = source_y // 2 + 1, source_y % 2
                        first = shift_y * GROUP + (2 * child_x + child_y) * COEF
                        bits = (2 * bit_x + bit_y) * 256
                        stack[shift_x, first : first + COEF, bits : bits + 256] = block
    for shift_x in range(3):
        for k in range(8):
            out_ref[shift_x, k * 128 : (k + 1) * 128, :] = jnp.transpose(
                stack[shift_x, :, k * 128 : (k + 1) * 128]
            ).astype(BF16)


def far_matrix(far_operator):
    return kernel_call(
        operator_kernel,
        (shape((3, 1024, 3 * GROUP), BF16),),
        (far_operator,),
        (pltpu.VMEM((COEF, 11520), F32), pltpu.VMEM((3, 3 * GROUP, 1024), F32)),
    )[0]


def z_sum(products, bits, lanes, roll):
    odd = iota((COEF, 128), 1) % 2 == 1
    total = None
    for step in range(-3, 4):
        first = bits * 256 + (step + 3) * COEF
        value = roll(products[first : first + COEF, lanes], step)
        if step == 3:
            value = jnp.where(odd, F32(0.0), value)
        if step == -3:
            value = jnp.where(odd, value, F32(0.0))
        total = value if total is None else total + value
    return total


def leaf_roll(value, step):
    return lane_roll(value, -step)


def six_roll(value, step):
    if not step:
        return value
    cell = iota(value.shape, 1) % 64 + step
    inside = (cell >= 0) & (cell < 64)
    return jnp.where(inside, lane_roll(value, -step), lane_roll(value, 64 - step))


def coarse_roll(value, step):
    if not step:
        return value
    lane = iota(value.shape, 1)
    period = jnp.where(lane < 32, 32, jnp.where(lane < 48, 16, 8))
    cell = jnp.where(lane < 32, lane, jnp.where(lane < 48, lane - 32, lane - 48))
    inside = (cell + step >= 0) & (cell + step < period)
    sign = 1 if step > 0 else -1
    wrapped = jnp.where(
        period == 32,
        lane_roll(value, sign * 32 - step),
        jnp.where(period == 16, lane_roll(value, sign * 16 - step), lane_roll(value, sign * 8 - step)),
    )
    return jnp.where(inside, lane_roll(value, -step), wrapped)


def leaf_kernel(
    matrix, grid_ref, below, above, low, high, low_corner, high_corner, out_ref, cells, products
):
    for first, msg, corner in ((0, low, low_corner), (384, high, high_corner)):
        lanes = slice(first, first + 128)
        cells[0:GROUP, lanes] = corner[C_LEAF : C_LEAF + GROUP, :]
        cells[GROUP : 5 * GROUP, lanes] = msg[X_LEAF:X_SIX, :]
        cells[5 * GROUP : 6 * GROUP, lanes] = corner[C_LEAF + GROUP : C_SIX, :]
    for xp in range(2):
        lanes = slice(128 + 128 * xp, 256 + 128 * xp)
        source = Y_LEAF + xp * GROUP
        cells[0:GROUP, lanes] = below[source : source + GROUP, :]
        cells[GROUP : 5 * GROUP, lanes] = grid_ref[xp * 4 * GROUP : (xp + 1) * 4 * GROUP, :]
        cells[5 * GROUP : 6 * GROUP, lanes] = above[source : source + GROUP, :]
    for parent in range(4):
        rows = slice(parent * GROUP, (parent + 3) * GROUP)
        total = None
        for shift_x in range(3):
            lanes = slice(shift_x * 128, shift_x * 128 + 256)
            term = dot(matrix[shift_x], cells[rows, lanes])
            total = term if total is None else total + term
        products[...] = total
        for xp in range(2):
            for bits in range(4):
                value = z_sum(products, bits, slice(xp * 128, xp * 128 + 128), leaf_roll)
                x, y = 2 * xp + bits // 2, 2 * parent + bits % 2
                out_ref[pl.ds(x * 8 + y, COEF, stride=32), :] = value


def leaf_level(*inputs):
    return kernel_call(
        leaf_kernel,
        (shape((1152, 128), F32),),
        inputs,
        (pltpu.VMEM((6 * GROUP, 512), BF16), pltpu.VMEM((1024, 256), F32)),
    )[0]


def levels_kernel(
    place, matrix, leaf_ref, six_ref, below, above, low, high, low_corner, high_corner,
    near_three, up_three, down_three, up_ref, down_ref, out_ref,
    fives, fours, three32, products, coarse, down32, downs, expand, lifted,
):
    gx, gy = place[0], place[1]
    row, col = iota((128, 128), 0), iota((128, 128), 1)
    size = lax.axis_size("gx")
    for shift, msg, first in (
        (-1, near_three, 0), (0, near_three, 80), (1, near_three, 160),
        (-4, up_three, 0), (-3, up_three, 80), (-2, up_three, 160),
        (2, down_three, 0), (3, down_three, 80), (4, down_three, 160),
    ):
        at = pl.multiple_of(lax.rem(gx + shift + size, size) * 72, 8)
        fives[pl.ds(at, 72), :] = msg[first : first + 72, :].astype(F32)
    even_up, odd_up = up_blocks(up_ref)

    def upward(grouped, split):
        children = dot(grouped.astype(BF16), split).astype(BF16)
        value = dot(even_up, children) + lane_roll(dot(odd_up, children), 64)
        return value.astype(BF16).astype(F32)

    lane = col % 64
    split_five = one_hot(
        (row == ((lane // 16 % 2) * 2 + lane // 32) * 32 + 2 * (lane % 16) + col // 64)
    )
    for x in range(4):
        value = upward(fives[x * GROUP : (x + 1) * GROUP, :], split_five)
        first = (x // 2) * GROUP + (x % 2) * 2 * COEF
        fours[first : first + COEF, :] = value
        fours[first + COEF : first + 2 * COEF, :] = lane_roll(value, 96)
    split_four = one_hot((row == (lane // 8) * 16 + 2 * (lane % 8) + col // 64) & (lane < 16))
    for x in range(2):
        value = upward(fours[x * GROUP : (x + 1) * GROUP, :], split_four)
        three32[x * 2 * COEF : x * 2 * COEF + COEF, :] = value
        three32[x * 2 * COEF + COEF : (x + 1) * 2 * COEF, :] = lane_roll(value, 120)
    three = dot(three32[...].astype(BF16), one_hot((row == col - 48) & (col >= 48) & (col < 56)))
    wide_low = iota((GROUP, 128), 1) < 64
    total = None
    for shift_x in range(3):
        if shift_x == 1:
            own, other = six_ref[...].astype(F32), halo_six(below, above)
        else:
            own = (low if shift_x == 0 else high)[X_SIX:X_ROWS, :].astype(F32)
            other = (low_corner if shift_x == 0 else high_corner)[C_SIX:C_FIVE, :].astype(F32)
        six = [
            lane_roll(jnp.where(wide_low, own, other), 64),
            own,
            lane_roll(jnp.where(wide_low, other, own), 64),
        ]
        at = pl.multiple_of(lax.rem(gx // 2 + shift_x + 3, 4) * GROUP, 8)
        five = fives[pl.ds(at, GROUP), :].astype(BF16)
        at = pl.multiple_of(lax.rem(gx // 4 + shift_x + 1, 2) * GROUP, 8)
        four = fours[pl.ds(at, GROUP), :].astype(BF16)
        blocks = []
        for shift_y in range(3):
            y_five = lax.rem(gy + shift_y + 3, 4)
            y_four = lax.rem(gy // 2 + shift_y + 1, 2)
            part = dot(five, one_hot((row == y_five * 32 + col) & (col < 32)))
            part = part + dot(
                four, one_hot((row == y_four * 16 + col - 32) & (col >= 32) & (col < 48))
            )
            blocks.append(jnp.concatenate([six[shift_y], part + three], axis=1))
        window = jnp.concatenate(blocks, axis=0).astype(BF16)
        term = dot(matrix[shift_x], window)
        total = term if total is None else total + term
    products[...] = total
    for bits in range(4):
        coarse[bits, 0:COEF, 0:128] = z_sum(products, bits, slice(0, 128), six_roll)
        coarse[bits, 0:COEF, 128:256] = z_sum(products, bits, slice(128, 256), coarse_roll)
    eye = one_hot(iota((8 * COEF, 8 * COEF), 0) == iota((8 * COEF, 8 * COEF), 1))
    down32[...] = dot_nt(eye, down_ref[...])
    downs[...] = jnp.zeros_like(downs)
    for bits in range(4):
        for bit in range(2):
            first = (2 * bits + bit) * COEF
            downs[bit, bits * 40 : bits * 40 + COEF, :] = down32[first : first + COEF, :]
    operators = [downs[bit].astype(BF16) for bit in range(2)]

    def spread(value, mask):
        return [dot(part, one_hot(mask)).astype(BF16) for part in parts(value)]

    def lift(wide, lanes):
        halves = [dot(value, wide[0]) + dot(value, wide[1]) for value in operators]
        lifted[:, lanes] = jnp.where(iota(halves[0].shape, 1) % 2 == 1, halves[1], halves[0])

    def child(bits, lanes):
        first = bits * 40 if isinstance(bits, int) else pl.multiple_of(bits * 40, 8)
        return lifted[pl.ds(first, COEF), lanes]

    first_lanes = slice(0, 128)

    right = slice(128, 256)
    bits = 2 * lax.rem(gx // 4, 2) + lax.rem(gy // 2, 2)
    value = coarse[bits, 0:COEF, right]
    wide = spread(value, (row == 48 + (col - 32) // 2) & (col >= 32) & (col < 48))
    bits = 2 * lax.rem(gx // 2, 2) + lax.rem(gy, 2)
    lift(wide, first_lanes)
    value = coarse[bits, 0:COEF, right] + child(bits, first_lanes)
    wide = spread(value, (row == 32 + col // 2) & (col < 32))
    lift(wide, first_lanes)
    wides = []
    for y in range(2):
        bits = 2 * lax.rem(gx, 2) + y
        value = coarse[bits, 0:COEF, right] + child(bits, first_lanes)
        wides.append(spread(value, (row == (col % 64) // 2) & (col // 64 == y)))
    wide = [(a.astype(F32) + b.astype(F32)).astype(BF16) for a, b in zip(*wides)]
    lift(wide, first_lanes)
    for bits in range(4):
        value = coarse[bits, 0:COEF, 0:128] + child(bits, first_lanes)
        for y in range(2):
            for k, part in enumerate(spread(value, row == y * 64 + col // 2)):
                at = ((bits // 2) * 4 + 2 * y + bits % 2) * 128
                expand[k, :, at : at + 128] = part
    lift([expand[k] for k in range(2)], slice(0, 1024))
    for x in range(4):
        for y in range(8):
            at = ((x // 2) * 4 + y // 2) * 128
            rows = pl.ds(x * 8 + y, COEF, stride=32)
            out_ref[rows, :] = leaf_ref[rows, :] + child(2 * (x % 2) + y % 2, slice(at, at + 128))


def all_levels(*inputs):
    return kernel_call(
        levels_kernel,
        (shape((1152, 128), F32),),
        inputs,
        (
            pltpu.VMEM((576, 128), F32),
            pltpu.VMEM((2 * GROUP, 128), F32),
            pltpu.VMEM((GROUP, 128), F32),
            pltpu.VMEM((1024, 256), F32),
            pltpu.VMEM((4, 40, 256), F32),
            pltpu.VMEM((8 * COEF, COEF), F32),
            pltpu.VMEM((2, 160, COEF), F32),
            pltpu.VMEM((2, COEF, 1024), BF16),
            pltpu.VMEM((160, 1024), F32),
        ),
        scalars=1,
    )[0]


def moved(value, step_x, step_y):
    size_x, size_y = lax.axis_size("gx"), lax.axis_size("gy")
    table = [
        (x * size_y + y, (x + step_x) % size_x * size_y + (y + step_y) % size_y)
        for x in range(size_x)
        for y in range(size_y)
    ]
    return lax.ppermute(value, ("gx", "gy"), table)


def per_device(
    leaf_multipoles, positions, masses, counts, up_operator, far_operator, down_operator
):
    place = jnp.stack([lax.axis_index("gx"), lax.axis_index("gy")]).astype(jnp.int32)
    (
        grid, up_msg, down_msg, low_msg, high_msg, six, five, live,
        positions, counts, up_operator, down_operator, far_operator,
    ) = prepare(
        leaf_multipoles.reshape(1152, 128), positions.reshape(768, 128), masses.reshape(256, 128),
        counts.reshape(32, 128), up_operator.T, down_operator, far_operator,
    )
    positions = positions.reshape(3, 8, 4, 8, 128)
    counts = counts.reshape(4, 8, 128)
    below, above, two = moved(up_msg, 0, 1), moved(down_msg, 0, -1), moved(five, 0, 2)
    low, high = moved(high_msg, 1, 0), moved(low_msg, -1, 0)
    inner = inner_pairs(positions, live.reshape(8, 4, 8, 128))
    below, above, two, inner = lax.optimization_barrier((below, above, two, inner))
    to_low, to_high = cross(place, below, above, two, five)
    low_corner, high_corner = moved(to_high, 1, 0), moved(to_low, -1, 0)
    matrix = far_matrix(lax.optimization_barrier((far_operator, inner))[0])
    inner = row_pairs(inner, positions, below, above)
    low, high, low_corner, high_corner, inner, matrix = lax.optimization_barrier(
        (low, high, low_corner, high_corner, inner, matrix)
    )
    three = jnp.concatenate([low_corner[C_FIVE:], to_low[C_FIVE:], high_corner[C_FIVE:]], axis=0)
    up_three, down_three = moved(three, 3, 0), moved(three, -3, 0)
    potential = face_pairs(inner, positions, counts, low, high, low_corner, high_corner)
    leaf = leaf_level(matrix, grid, below, above, low, high, low_corner, high_corner)
    up_three, down_three, leaf = lax.optimization_barrier((up_three, down_three, leaf))
    expansion = all_levels(
        place, matrix, leaf, six, below, above, low, high, low_corner, high_corner,
        three, up_three, down_three, up_operator, down_operator,
    )
    return expansion.reshape(36, 4, 8, 128), potential


def extended(cells, sides, width):
    for axis, dim in sides:
        count = lax.axis_size(axis)
        head = lax.slice_in_dim(cells, 0, width, axis=dim)
        tail = lax.slice_in_dim(cells, cells.shape[dim] - width, cells.shape[dim], axis=dim)
        cells = jnp.concatenate(
            [
                lax.ppermute(tail, axis, [(i, (i + 1) % count) for i in range(count)]),
                cells,
                lax.ppermute(head, axis, [((i + 1) % count, i) for i in range(count)]),
            ],
            axis=dim,
        )
    return cells


def shift_list():
    return [
        (step_x, step_y, step_z)
        for step_x in (-1, 0, 1)
        for step_y in (-1, 0, 1)
        for step_z in (-1, 0, 1)
    ]


def child_bits(number):
    return (number // 4, number // 2 % 2, number % 2)


def offset_table():
    vectors = [
        (step_x, step_y, step_z)
        for step_x in range(-3, 4)
        for step_y in range(-3, 4)
        for step_z in range(-3, 4)
        if max(abs(step_x), abs(step_y), abs(step_z)) >= 2
    ]
    lookup = np.full((27, 8, 8), len(vectors), dtype=np.int32)
    for shift_id, offset in enumerate(shift_list()):
        for source in range(8):
            for target in range(8):
                vector = tuple(
                    (
                        2 * offset[axis_id]
                        + child_bits(source)[axis_id]
                        - child_bits(target)[axis_id]
                        for axis_id in range(3)
                    )
                )
                if max(abs(vector[0]), abs(vector[1]), abs(vector[2])) >= 2:
                    lookup[shift_id, source, target] = vectors.index(vector)
    return lookup


def assemble(far_operator):
    coeff_count = far_operator.shape[0]
    blocks = far_operator.reshape(coeff_count, -1, coeff_count)
    blocks = jnp.concatenate(
        [blocks, jnp.zeros((coeff_count, 1, coeff_count), blocks.dtype)], axis=1
    )
    picked = jnp.take(blocks, jnp.asarray(offset_table().reshape(-1), dtype=jnp.int32), axis=1)
    picked = picked.reshape(coeff_count, 27, 8, 8, coeff_count).transpose(1, 2, 0, 3, 4)
    return picked.reshape(27, 8 * coeff_count, 8 * coeff_count)


def group_cells(volume):
    size_x, size_y, size_z, coeff_count = volume.shape
    reshaped = volume.reshape(size_x // 2, 2, size_y // 2, 2, size_z // 2, 2, coeff_count)
    return reshaped.transpose(0, 2, 4, 1, 3, 5, 6).reshape(
        size_x // 2, size_y // 2, size_z // 2, 8 * coeff_count
    )


def spread_cells(grouped):
    size_x, size_y, size_z, total_rows = grouped.shape
    coeff_count = total_rows // 8
    reshaped = grouped.reshape(size_x, size_y, size_z, 2, 2, 2, coeff_count)
    return reshaped.transpose(0, 3, 1, 4, 2, 5, 6).reshape(
        2 * size_x, 2 * size_y, 2 * size_z, coeff_count
    )


def wrap_pad(volume, axis_id):
    extent = volume.shape[axis_id]
    lower = lax.slice_in_dim(volume, extent - 1, extent, axis=axis_id)
    upper = lax.slice_in_dim(volume, 0, 1, axis=axis_id)
    return jnp.concatenate([lower, volume, upper], axis=axis_id)


def wrap_window(volume, axis_id, anchor, extent):
    return lax.dynamic_slice_in_dim(wrap_pad(volume, axis_id), anchor, extent + 2, axis_id)


def region(index_now, cells, levels_up):
    anchor = index_now * cells // 2**levels_up
    extent = max(cells // 2**levels_up, 1)
    return (anchor, extent)


def cut(children, index_x, index_y, cells_x, cells_y, levels_up):
    anchor_x, extent_x = region(index_x, cells_x, levels_up)
    parent_x = region(index_x, cells_x, levels_up + 1)[0]
    anchor_y, extent_y = region(index_y, cells_y, levels_up)
    parent_y = region(index_y, cells_y, levels_up + 1)[0]
    children = lax.dynamic_slice_in_dim(children, anchor_x - 2 * parent_x, extent_x, 0)
    return lax.dynamic_slice_in_dim(children, anchor_y - 2 * parent_y, extent_y, 1)


def coarse_window(grouped, index_x, index_y, cells_x, cells_y, levels_up):
    anchor_x, extent_x = region(index_x, cells_x, levels_up)
    anchor_y, extent_y = region(index_y, cells_y, levels_up)
    windowed = wrap_window(grouped, 0, anchor_x, extent_x)
    windowed = wrap_window(windowed, 1, anchor_y, extent_y)
    return wrap_pad(windowed, 2)


def upward(up_operator, grouped):
    parent = jnp.einsum("xyzs,sj->xyzj", grouped, up_operator, preferred_element_type=jnp.float32)
    return parent.astype(jnp.bfloat16)


def downward(down_operator, parent):
    children = jnp.einsum(
        "xyzi,it->xyzt", parent, down_operator.astype(jnp.float32), precision=lax.Precision.HIGHEST
    )
    return spread_cells(children)


def far_field(padded, kernel):
    size_x = padded.shape[0] - 2
    size_y = padded.shape[1] - 2
    size_z = padded.shape[2] - 2
    running = None
    for shift_id, offset in enumerate(shift_list()):
        window_piece = padded[
            1 + offset[0] : 1 + offset[0] + size_x, 1 + offset[1] : 1 + offset[1] + size_y
        ]
        product_term = jnp.einsum(
            "xyzs,st->xyzt", window_piece, kernel[shift_id], preferred_element_type=jnp.float32
        )
        product_term = product_term[:, :, 1 + offset[2] : 1 + offset[2] + size_z]
        running = product_term if running is None else running + product_term
    return running


def near_field(positions, masses, counts):
    slot_count = masses.shape[0]
    size_x, size_y, size_z = (masses.shape[1], masses.shape[2], masses.shape[3])
    live_slot = lax.broadcasted_iota(jnp.int32, masses.shape, 0) < counts[None]
    live_mass = jnp.where(live_slot, masses, jnp.float32(0.0))
    stacked = jnp.concatenate([positions, live_mass[None]], axis=0)
    padded = wrap_pad(extended(stacked, (("gx", 2), ("gy", 3)), 1), 4)
    block_size = min(8, slot_count)
    same_slot = lax.broadcasted_iota(
        jnp.int32, (block_size, slot_count, 1, 1, 1), 0
    ) + 0 == lax.broadcasted_iota(jnp.int32, (block_size, slot_count, 1, 1, 1), 1)
    running = jnp.zeros((block_size, size_x, size_y, size_z), jnp.float32)
    for offset in shift_list():
        source = padded[
            :,
            :,
            1 + offset[0] : 1 + offset[0] + size_x,
            1 + offset[1] : 1 + offset[1] + size_y,
            1 + offset[2] : 1 + offset[2] + size_z,
        ]
        squared = jnp.float32(SOFTENING * SOFTENING)
        for axis_id in range(3):
            separation = (
                source[axis_id][None] + jnp.float32(offset[axis_id]) - positions[axis_id][:, None]
            )
            squared = squared + separation * separation
        pair_terms = source[3][None] * lax.rsqrt(squared)
        if offset == (0, 0, 0):
            pair_terms = jnp.where(same_slot, jnp.float32(0.0), pair_terms)
        running = running + jnp.sum(pair_terms, axis=1)
    results = running
    running = results
    return jnp.where(live_slot, -running / slot_count, jnp.float32(0.0))


def general_device(
    leaf_multipoles, positions, masses, counts, up_operator, far_operator, down_operator
):
    potential = near_field(positions, masses, counts)
    kernel = assemble(far_operator)
    index_x = lax.axis_index("gx")
    index_y = lax.axis_index("gy")
    cells_x = leaf_multipoles.shape[1]
    cells_y = leaf_multipoles.shape[2]
    leaf_cells = jnp.transpose(leaf_multipoles, (1, 2, 3, 0))
    grouped_leaf = group_cells(leaf_cells)
    padded = wrap_pad(extended(grouped_leaf, (("gx", 0), ("gy", 1)), 1), 2)
    far_leaf = spread_cells(far_field(padded, kernel))
    grouped_six = group_cells(upward(up_operator, grouped_leaf))
    padded = wrap_pad(extended(grouped_six, (("gx", 0), ("gy", 1)), 1), 2)
    far_six = spread_cells(far_field(padded, kernel))
    moments_five = upward(up_operator, grouped_six)
    columns = lax.all_gather(moments_five, "gy", axis=1, tiled=True)
    whole_five = lax.all_gather(columns, "gx", axis=0, tiled=True)
    grouped_five = group_cells(whole_five)
    window_five = coarse_window(grouped_five, index_x, index_y, cells_x, cells_y, 3)
    moments_four = upward(up_operator, grouped_five)
    far_five = cut(
        spread_cells(far_field(window_five, kernel)), index_x, index_y, cells_x, cells_y, 2
    )
    grouped_four = group_cells(moments_four)
    window_four = coarse_window(grouped_four, index_x, index_y, cells_x, cells_y, 4)
    far_four = cut(
        spread_cells(far_field(window_four, kernel)), index_x, index_y, cells_x, cells_y, 3
    )
    grouped_three = group_cells(upward(up_operator, grouped_four))
    window_three = coarse_window(grouped_three, index_x, index_y, cells_x, cells_y, 5)
    far_three = cut(
        spread_cells(far_field(window_three, kernel)), index_x, index_y, cells_x, cells_y, 4
    )
    expansion = far_three
    expansion = far_four + cut(
        downward(down_operator, expansion), index_x, index_y, cells_x, cells_y, 3
    )
    expansion = far_five + cut(
        downward(down_operator, expansion), index_x, index_y, cells_x, cells_y, 2
    )
    expansion = far_six + cut(
        downward(down_operator, expansion), index_x, index_y, cells_x, cells_y, 1
    )
    expansion = far_leaf + cut(
        downward(down_operator, expansion), index_x, index_y, cells_x, cells_y, 0
    )
    return (jnp.transpose(expansion, (3, 0, 1, 2)), potential)


def solution(mesh):
    small = (mesh.shape["gx"], mesh.shape["gy"]) == (8, 4)
    return jax.shard_map(
        per_device if small else general_device,
        mesh=mesh,
        in_specs=(
            P(None, "gx", "gy", None),
            P(None, None, "gx", "gy", None),
            P(None, "gx", "gy", None),
            P("gx", "gy", None),
            P(),
            P(),
            P(),
        ),
        out_specs=(P(None, "gx", "gy", None), P(None, "gx", "gy", None)),
        check_vma=False,
    )
```

```python
import functools

import jax
import jax.numpy as jnp
import numpy as np
from jax import lax
from jax.experimental import pallas as pl
from jax.experimental.pallas import tpu as pltpu
from jax.sharding import PartitionSpec as P

SOFTENING = 0.05
EPS = SOFTENING * SOFTENING
F32 = jnp.float32
BF16 = jnp.bfloat16
COEF = 36
GROUP = 4 * COEF
Y_LEAF = 256
Y_SIX = Y_LEAF + 2 * GROUP
Y_FIVE = Y_SIX + GROUP // 2
Y_ROWS = Y_FIVE + 40
X_LEAF = 512
X_SIX = X_LEAF + 4 * GROUP
X_ROWS = X_SIX + GROUP
C_LEAF = 128
C_SIX = C_LEAF + 2 * GROUP
C_FIVE = C_SIX + GROUP
C_ROWS = C_FIVE + 80

VMEM = pl.BlockSpec(memory_space=pltpu.VMEM)
SMEM = pl.BlockSpec(memory_space=pltpu.SMEM)
HBM = pl.BlockSpec(memory_space=pltpu.MemorySpace.HBM)


def shape(dims, dtype):
    return jax.ShapeDtypeStruct(dims, dtype)


def kernel_call(body, outs, inputs, scratch=(), scalars=0, space=VMEM, limit=20):
    return pl.pallas_call(
        body,
        out_shape=outs,
        in_specs=[SMEM] * scalars + [space] * (len(inputs) - scalars),
        out_specs=[VMEM] * len(outs),
        scratch_shapes=list(scratch),
        compiler_params=pltpu.CompilerParams(vmem_limit_bytes=limit * 1024 * 1024),
    )(*inputs)


def iota(dims, axis):
    return lax.broadcasted_iota(jnp.int32, dims, axis)


def dot(lhs, rhs):
    return lax.dot_general(lhs, rhs, (((1,), (0,)), ((), ())), preferred_element_type=F32)


def dot_tn(lhs, rhs):
    return lax.dot_general(lhs, rhs, (((0,), (0,)), ((), ())), preferred_element_type=F32)


def dot_nt(lhs, rhs):
    return lax.dot_general(lhs, rhs, (((1,), (1,)), ((), ())), preferred_element_type=F32)


def one_hot(mask):
    return jnp.where(mask, F32(1.0), F32(0.0)).astype(BF16)


def parts(value):
    high = value.astype(BF16)
    return high, (value - high.astype(F32)).astype(BF16)


def lane_roll(value, shift):
    return pltpu.roll(value, shift % 128, 1) if shift % 128 else value


def up_blocks(up_ref):
    row, col = iota((8 * COEF, GROUP), 0), iota((8 * COEF, GROUP), 1)
    return [
        dot(up_ref[...], one_hot(row == (col // COEF * 2 + bit) * COEF + col % COEF)).astype(BF16)
        for bit in range(2)
    ]


def prep_kernel(
    leaf_hbm, pos_hbm, mass_hbm, count_hbm, up_hbm,
    grid_ref, up_msg, down_msg, low_msg, high_msg, six_ref, five_ref, live_ref,
    pos_ref, count_ref, up_ref,
    leaf_ref, mass_ref, m32, x32, six32, near32, sems,
):
    copies = [
        pltpu.make_async_copy(source, target, sems.at[k])
        for k, (source, target) in enumerate(
            (
                (leaf_hbm, leaf_ref), (pos_hbm, pos_ref), (mass_hbm, mass_ref),
                (count_hbm, count_ref), (up_hbm, up_ref),
            )
        )
    ]
    for copy in copies:
        copy.start()
    copies[0].wait()
    m32[...] = leaf_ref[...].astype(F32)
    for x in range(4):
        for y in range(8):
            start = ((x // 2) * 4 + y // 2) * GROUP + (2 * (x % 2) + y % 2) * COEF
            x32[start : start + COEF, :] = m32[pl.ds(x * 8 + y, COEF, stride=32), :]
    grid = x32[...].astype(BF16)
    grid_ref[...] = grid
    for msg, parent in ((up_msg, 3), (down_msg, 0)):
        for xp in range(2):
            msg[Y_LEAF + xp * GROUP : Y_LEAF + (xp + 1) * GROUP, :] = grid_ref[
                (xp * 4 + parent) * GROUP : (xp * 4 + parent + 1) * GROUP, :
            ]
    low_msg[X_LEAF:X_SIX, :] = grid_ref[0 : 4 * GROUP, :]
    high_msg[X_LEAF:X_SIX, :] = grid_ref[4 * GROUP : 8 * GROUP, :]
    for copy in copies[1:]:
        copy.wait()
    count = count_ref[...]
    for slot in range(8):
        live_ref[slot * 32 : slot * 32 + 32, :] = jnp.where(
            count > slot, mass_ref[slot * 32 : slot * 32 + 32, :], F32(0.0)
        )
    for msg, y in ((up_msg, 7), (down_msg, 0)):
        rows = []
        for x in range(4):
            rows.append(pos_ref[pl.ds(x * 8 + y, 24, stride=32), :])
            rows.append(live_ref[pl.ds(x * 8 + y, 8, stride=32), :])
        high, low = parts(jnp.concatenate(rows, axis=0))
        msg[0:128, :] = high
        msg[128:256, :] = low
    for msg, x in ((low_msg, 0), (high_msg, 3)):
        for slot in range(8):
            for axis in range(3):
                start = (axis * 8 + slot) * 32 + x * 8
                near32[pl.ds(axis * 8 + slot, 8, stride=32), :] = pos_ref[start : start + 8, :]
            start = slot * 32 + x * 8
            near32[pl.ds(24 + slot, 8, stride=32), :] = live_ref[start : start + 8, :]
        high, low = parts(near32[...])
        msg[0:256, :] = high
        msg[256:512, :] = low
    low_half = iota((COEF, 128), 1) < 64
    even_up, odd_up = up_blocks(up_ref)
    row, col = iota((128, 128), 0), iota((128, 128), 1)
    split_z = one_hot(row == 2 * (col % 64) + col // 64)
    split = dot(grid, split_z).astype(BF16)
    columns = jnp.concatenate([split[k * GROUP : (k + 1) * GROUP] for k in range(8)], axis=1)
    even, odd = dot(even_up, columns), dot(odd_up, columns)
    for xp in range(2):
        for y in range(2):
            first, second = (xp * 4 + y) * 128, (xp * 4 + 2 + y) * 128
            near_part = even[:, first : first + 128] + lane_roll(odd[:, first : first + 128], 64)
            far_part = lane_roll(even[:, second : second + 128], 64) + odd[:, second : second + 128]
            start = (2 * xp + y) * COEF
            six32[start : start + COEF, :] = jnp.where(low_half, near_part, far_part)
    six = six32[...].astype(BF16)
    six_ref[...] = six
    low_msg[X_SIX:X_ROWS, :] = six
    high_msg[X_SIX:X_ROWS, :] = six
    left = iota((72, 128), 1) < 64
    first, second = six32[0:72, :], six32[72:144, :]
    up_msg[Y_SIX:Y_FIVE, :] = jnp.where(left, lane_roll(first, 64), second).astype(BF16)
    down_msg[Y_SIX:Y_FIVE, :] = jnp.where(left, first, lane_roll(second, 64)).astype(BF16)
    split_six = one_hot(row == ((col // 32) % 2) * 64 + 2 * (col % 32) + col // 64)
    split = dot(six, split_six).astype(BF16)
    five = dot(even_up, split) + lane_roll(dot(odd_up, split), 64)
    five = jnp.concatenate([five, jnp.zeros((4, 128), F32)], axis=0).astype(BF16)
    five_ref[...] = five
    for msg in (up_msg, down_msg):
        msg[Y_FIVE:Y_ROWS, :] = five


def in_hbm(value):
    return pltpu.with_memory_space_constraint(value, pltpu.MemorySpace.HBM)


def prepare(leaf, positions, masses, counts, up_operator):
    inputs = (leaf, positions, masses, counts, up_operator)
    return kernel_call(
        prep_kernel,
        (
            shape((8 * GROUP, 128), BF16),
            shape((Y_ROWS, 128), BF16),
            shape((Y_ROWS, 128), BF16),
            shape((X_ROWS, 128), BF16),
            shape((X_ROWS, 128), BF16),
            shape((GROUP, 128), BF16),
            shape((40, 128), BF16),
            shape((256, 128), F32),
            shape((768, 128), F32),
            shape((32, 128), jnp.int32),
            shape(up_operator.shape, BF16),
        ),
        [in_hbm(value) for value in inputs],
        (
            pltpu.VMEM((1152, 128), BF16),
            pltpu.VMEM((256, 128), F32),
            pltpu.VMEM((1152, 128), F32),
            pltpu.VMEM((1152, 128), F32),
            pltpu.VMEM((GROUP, 128), F32),
            pltpu.VMEM((256, 128), F32),
            pltpu.SemaphoreType.DMA((5,)),
        ),
        space=HBM,
    )


def halo_six(below, above):
    upper, lower = above[Y_SIX:Y_FIVE, :].astype(F32), below[Y_SIX:Y_FIVE, :].astype(F32)
    left = iota((72, 128), 1) < 64
    return jnp.concatenate(
        [
            jnp.where(left, upper, lane_roll(lower, 64)),
            jnp.where(left, lane_roll(upper, 64), lower),
        ],
        axis=0,
    )


def cross_kernel(place, below, above, two, own, to_low, to_high, five32):
    lane = iota((COEF, 128), 1) // 32
    five32[...] = jnp.zeros_like(five32)
    for shift, ref, first in ((0, own, 0), (3, below, Y_FIVE), (1, above, Y_FIVE), (2, two, 0)):
        at = lax.rem(place[1] + shift, 4)
        value = ref[first : first + 40, :].astype(F32)
        for y in range(2):
            moved = pltpu.roll(value, lax.rem(32 * at + 96 * y, 128), 1)[0:COEF]
            rows = slice(y * COEF, (y + 1) * COEF)
            five32[rows, :] = jnp.where(lane == at, moved, five32[rows, :])
    five = five32[...].astype(BF16)
    halo = halo_six(below, above).astype(BF16)
    for msg, x, xp in ((to_low, 0, 0), (to_high, 3, 1)):
        for side, ref in enumerate((below, above)):
            for half in range(2):
                source = half * 128 + x * 32
                first = side * 64 + half * 32
                msg[first : first + 32, :] = ref[source : source + 32, :]
            source, first = Y_LEAF + xp * GROUP, C_LEAF + side * GROUP
            msg[first : first + GROUP, :] = ref[source : source + GROUP, :]
        msg[C_SIX:C_FIVE, :] = halo
        msg[C_FIVE:C_ROWS, :] = five


def cross(*inputs):
    return kernel_call(
        cross_kernel,
        (shape((C_ROWS, 128), BF16), shape((C_ROWS, 128), BF16)),
        inputs,
        (pltpu.VMEM((80, 128), F32),),
        scalars=1,
    )


def inverse_distance(target, source):
    squared = F32(EPS)
    for axis in range(3):
        separation = source[axis] - target[axis]
        squared = squared + separation * separation
    return lax.rsqrt(squared)


def pair_sums(shifted, sums, goals, x, step, totals):
    step_x, step_y, step_z = step
    edge = iota((8, 128), 0) == (7 if step_y > 0 else 0)
    for slot in range(8):
        source = [shifted[step_z + 1, k, slot, x] for k in range(4)]
        if step_y:
            source = [pltpu.roll(value, (-step_y) % 8, 0) for value in source]
            source[1] = source[1] + F32(step_y)
            source[3] = jnp.where(edge, F32(0.0), source[3])
        if step_x:
            source[0] = source[0] + F32(step_x)
        back = None
        for goal in range(8):
            inverse = inverse_distance(goals[goal], source)
            totals[goal] = totals[goal] + source[3] * inverse
            term = goals[goal][3] * inverse
            back = term if back is None else back + term
        if step_y:
            back = pltpu.roll(jnp.where(edge, F32(0.0), back), step_y % 8, 0)
        sums[step_z + 1, slot, x] = sums[step_z + 1, slot, x] + back


def plane_goals(shifted, x):
    return [[shifted[1, k, slot, x] for k in range(4)] for slot in range(8)]


def plane_kernel(pos_ref, live_ref, far_hbm, down_hbm, sums, shifted, far_ref, down_ref, sems):
    copies = [
        pltpu.make_async_copy(source, target, sems.at[k])
        for k, (source, target) in enumerate(((far_hbm, far_ref), (down_hbm, down_ref)))
    ]
    for copy in copies:
        copy.start()
    sums[...] = jnp.zeros_like(sums)

    def plane(x, carry):
        for slot in range(8):
            values = [pos_ref[axis, slot, x] for axis in range(3)] + [live_ref[slot, x]]
            for index, step in enumerate((-1, 0, 1)):
                moved = [lane_roll(value, -step) for value in values]
                if step:
                    moved[2] = moved[2] + F32(step)
                for k in range(4):
                    shifted[index, k, slot, x] = moved[k]
        goals = plane_goals(shifted, x)
        totals = [jnp.zeros((8, 128), F32) for slot in range(8)]
        for slot in range(8):
            for goal in range(slot):
                inverse = inverse_distance(goals[goal], goals[slot])
                totals[goal] = totals[goal] + goals[slot][3] * inverse
                totals[slot] = totals[slot] + goals[goal][3] * inverse
        for step in ((0, 0, 1), (0, 1, -1), (0, 1, 0), (0, 1, 1)):
            pair_sums(shifted, sums, goals, x, step, totals)
        for slot in range(8):
            sums[1, slot, x] = sums[1, slot, x] + totals[slot]
        return carry

    lax.fori_loop(0, 4, plane, 0)
    for copy in copies:
        copy.wait()


def step_kernel(sums_ref, shifted, out_ref, sums):
    sums[...] = sums_ref[...]

    def planes(x, carry):
        for step_y in (-1, 0, 1):
            goals = plane_goals(shifted, x)
            totals = [sums[1, slot, x] for slot in range(8)]
            for step_z in (-1, 0, 1):
                pair_sums(shifted, sums, goals, x + 1, (1, step_y, step_z), totals)
            for slot in range(8):
                sums[1, slot, x] = totals[slot]
        return carry

    lax.fori_loop(0, 3, planes, 0)

    def finish(x, carry):
        for slot in range(8):
            out_ref[slot, x] = (
                sums[1, slot, x] + lane_roll(sums[0, slot, x], -1) + lane_roll(sums[2, slot, x], 1)
            )
        return carry

    lax.fori_loop(0, 4, finish, 0)


def plane_pairs(positions, live, far_operator, down_operator):
    return pl.pallas_call(
        plane_kernel,
        out_shape=(
            shape((3, 8, 4, 8, 128), F32),
            shape((3, 4, 8, 4, 8, 128), F32),
            shape(far_operator.shape, BF16),
            shape(down_operator.shape, BF16),
        ),
        in_specs=[VMEM, VMEM, HBM, HBM],
        out_specs=[VMEM] * 4,
        scratch_shapes=[pltpu.SemaphoreType.DMA((2,))],
        compiler_params=pltpu.CompilerParams(vmem_limit_bytes=16 * 1024 * 1024),
    )(positions, live, in_hbm(far_operator), in_hbm(down_operator))


def step_pairs(*inputs):
    return kernel_call(
        step_kernel,
        (shape((8, 4, 8, 128), F32),),
        inputs,
        (pltpu.VMEM((3, 8, 4, 8, 128), F32),),
    )[0]


def gather(shifted, goals, totals):
    def body(index, carry):
        carry = list(carry)
        for slot in range(8):
            source = [shifted[index, k, slot] for k in range(4)]
            for goal in range(8):
                carry[goal] = carry[goal] + source[3] * inverse_distance(goals[goal], source)
        return tuple(carry)

    return lax.fori_loop(0, 9, body, tuple(totals))


def rows_kernel(inner_ref, pos_ref, below, above, out_ref, near32, shifted):
    row = iota((8, 128), 0)
    for index, msg in enumerate((below, above)):
        near32[index] = msg[0:128, :].astype(F32) + msg[128:256, :].astype(F32)
    turn = jnp.where(row >= 4, F32(1.0), F32(-1.0))
    none = jnp.zeros((1, 128), F32)
    for slot in range(8):
        for k in range(4):
            source = [
                [none] + [near32[side, pl.ds(x * 32 + 8 * k + slot, 1), :] for x in range(4)] + [none]
                for side in range(2)
            ]
            for step_x in range(3):
                value = jnp.concatenate(
                    source[0][step_x : step_x + 4] + source[1][step_x : step_x + 4], axis=0
                )
                if k == 0:
                    value = value + F32(step_x - 1)
                if k == 1:
                    value = value + turn
                for step_z in range(3):
                    moved = lane_roll(value, 1 - step_z)
                    if k == 2:
                        moved = moved + F32(step_z - 1)
                    shifted[step_x * 3 + step_z, k, slot] = moved

    def edge_rows(ref, lead):
        return jnp.concatenate(
            [ref[lead + (x, pl.ds(0, 1))] for x in range(4)]
            + [ref[lead + (x, pl.ds(7, 1))] for x in range(4)],
            axis=0,
        )

    goals = [[edge_rows(pos_ref, (axis, slot)) for axis in range(3)] for slot in range(8)]
    totals = gather(shifted, goals, [jnp.zeros((8, 128), F32) for slot in range(8)])
    out_ref[...] = inner_ref[...]
    for slot in range(8):
        for x in range(4):
            for y, r in ((0, x), (7, x + 4)):
                out_ref[slot, x, pl.ds(y, 1)] = out_ref[slot, x, pl.ds(y, 1)] + totals[slot][r : r + 1]


def faces_kernel(
    inner_ref, pos_ref, count_ref, low, high, low_corner, high_corner, out_ref, sides, shifted, sums
):
    for index, (msg, corner) in enumerate(((low, low_corner), (high, high_corner))):
        sides[index, 0:32, :] = corner[0:32, :].astype(F32) + corner[32:64, :].astype(F32)
        sides[index, 32:288, :] = msg[0:256, :].astype(F32) + msg[256:512, :].astype(F32)
        sides[index, 288:320, :] = corner[64:96, :].astype(F32) + corner[96:128, :].astype(F32)

    def face(index, carry):
        for slot in range(8):
            for step_y in range(3):
                values = [
                    sides[index, pl.ds(step_y * 32 + 8 * k + slot, 8, stride=32), :]
                    for k in range(4)
                ]
                values[0] = values[0] + (2 * index - 1).astype(F32)
                values[1] = values[1] + F32(step_y - 1)
                for step_z in range(3):
                    moved = [lane_roll(value, 1 - step_z) for value in values]
                    moved[2] = moved[2] + F32(step_z - 1)
                    for k in range(4):
                        shifted[step_y * 3 + step_z, k, slot] = moved[k]
        x = 3 * index
        goals = [[pos_ref[axis, slot, x] for axis in range(3)] for slot in range(8)]
        totals = gather(shifted, goals, [inner_ref[slot, x] for slot in range(8)])
        for slot in range(8):
            sums[slot, x] = totals[slot]
        return carry

    lax.fori_loop(0, 2, face, 0)
    for x in (1, 2):
        for slot in range(8):
            sums[slot, x] = inner_ref[slot, x]
    for slot in range(8):
        out_ref[slot] = jnp.where(count_ref[...] > slot, -sums[slot] / 8, F32(0.0))


def row_pairs(*inputs):
    return kernel_call(
        rows_kernel,
        (shape((8, 4, 8, 128), F32),),
        inputs,
        (pltpu.VMEM((2, 128, 128), F32), pltpu.VMEM((9, 4, 8, 8, 128), F32)),
    )[0]


def face_pairs(*inputs):
    return kernel_call(
        faces_kernel,
        (shape((8, 4, 8, 128), F32),),
        inputs,
        (
            pltpu.VMEM((2, 320, 128), F32),
            pltpu.VMEM((9, 4, 8, 8, 128), F32),
            pltpu.VMEM((8, 4, 8, 128), F32),
        ),
    )[0]


def far_starts():
    starts, count = {}, 0
    for step_x in range(-3, 4):
        for step_y in range(-3, 4):
            starts[step_x, step_y] = count * COEF
            count += 7 if max(abs(step_x), abs(step_y)) >= 2 else 4
    return starts


def operator_kernel(far_ref, out_ref, far32, stack):
    far32[:, 0:11264] = far_ref[:, 0:11264].astype(F32)
    far32[:, 11264:11520] = jnp.zeros((COEF, 256), F32)
    far32[:, 11264:11376] = far_ref[:, 11264:11376].astype(F32)
    lane = iota((COEF, 256), 1)

    def window(start):
        base = start // 128 * 128
        value = far32[:, base : base + 384]
        shift = start - base
        return (pltpu.roll(value, 384 - shift, 1) if shift else value)[:, 0:256]

    starts = far_starts()
    for step_x in range(-3, 4):
        for step_y in range(-3, 4):
            start = starts[step_x, step_y]
            if max(abs(step_x), abs(step_y)) >= 2:
                block = jnp.where(lane < 7 * COEF, window(start), F32(0.0))
            else:
                block = jnp.where(
                    lane < 2 * COEF,
                    window(start),
                    jnp.where(
                        (lane >= 5 * COEF) & (lane < 7 * COEF), window(start - 3 * COEF), F32(0.0)
                    ),
                )
            for bit_x in range(2):
                for bit_y in range(2):
                    source_x, source_y = step_x + bit_x, step_y + bit_y
                    if -2 <= source_x <= 3 and -2 <= source_y <= 3:
                        shift_x, child_x = source_x // 2 + 1, source_x % 2
                        shift_y, child_y = source_y // 2 + 1, source_y % 2
                        first = shift_y * GROUP + (2 * child_x + child_y) * COEF
                        bits = (2 * bit_x + bit_y) * 256
                        stack[shift_x, first : first + COEF, bits : bits + 256] = block
    out_ref[...] = stack[...].astype(BF16)


def far_matrix(far_operator):
    return kernel_call(
        operator_kernel,
        (shape((3, 3 * GROUP, 1024), BF16),),
        (far_operator,),
        (pltpu.VMEM((COEF, 11520), F32), pltpu.VMEM((3, 3 * GROUP, 1024), F32)),
    )[0]


def z_sum(products, bits, lanes, roll):
    odd = iota((COEF, 128), 1) % 2 == 1
    total = None
    for step in range(-3, 4):
        first = bits * 256 + (step + 3) * COEF
        value = roll(products[first : first + COEF, lanes], step)
        if step == 3:
            value = jnp.where(odd, F32(0.0), value)
        if step == -3:
            value = jnp.where(odd, value, F32(0.0))
        total = value if total is None else total + value
    return total


def leaf_roll(value, step):
    return lane_roll(value, -step)


def six_roll(value, step):
    if not step:
        return value
    cell = iota(value.shape, 1) % 64 + step
    inside = (cell >= 0) & (cell < 64)
    return jnp.where(inside, lane_roll(value, -step), lane_roll(value, 64 - step))


def coarse_roll(value, step):
    if not step:
        return value
    lane = iota(value.shape, 1)
    period = jnp.where(lane < 32, 32, jnp.where(lane < 48, 16, 8))
    cell = jnp.where(lane < 32, lane, jnp.where(lane < 48, lane - 32, lane - 48))
    inside = (cell + step >= 0) & (cell + step < period)
    sign = 1 if step > 0 else -1
    wrapped = jnp.where(
        period == 32,
        lane_roll(value, sign * 32 - step),
        jnp.where(period == 16, lane_roll(value, sign * 16 - step), lane_roll(value, sign * 8 - step)),
    )
    return jnp.where(inside, lane_roll(value, -step), wrapped)


def levels_kernel(
    place, matrix, grid_ref, six_ref, below, above, low, high, low_corner, high_corner,
    near_three, up_three, down_three, up_ref, down_ref, out_ref,
    cells, fives, fours, three32, windows, products, coarse, down32, downs, expand, lifted,
):
    gx, gy = place[0], place[1]
    row, col = iota((128, 128), 0), iota((128, 128), 1)

    def multiply(sources, slot, half):
        rows = slice(half * 512, half * 512 + 512)
        total = None
        for shift_x, source in enumerate(sources):
            term = dot_tn(matrix[shift_x, :, rows], source)
            total = term if total is None else total + term
        products[slot, rows, :] = total

    for first, msg, corner in ((0, low, low_corner), (384, high, high_corner)):
        lanes = slice(first, first + 128)
        cells[0:GROUP, lanes] = corner[C_LEAF : C_LEAF + GROUP, :]
        cells[GROUP : 5 * GROUP, lanes] = msg[X_LEAF:X_SIX, :]
        cells[5 * GROUP : 6 * GROUP, lanes] = corner[C_LEAF + GROUP : C_SIX, :]
    for xp in range(2):
        lanes = slice(128 + 128 * xp, 256 + 128 * xp)
        source = Y_LEAF + xp * GROUP
        cells[0:GROUP, lanes] = below[source : source + GROUP, :]
        cells[GROUP : 5 * GROUP, lanes] = grid_ref[xp * 4 * GROUP : (xp + 1) * 4 * GROUP, :]
        cells[5 * GROUP : 6 * GROUP, lanes] = above[source : source + GROUP, :]

    todo = [(parent, half) for parent in range(4) for half in range(2)]

    def leaf_products(count=1):
        for parent, half in todo[:count]:
            rows = slice(parent * GROUP, (parent + 3) * GROUP)
            lanes = [slice(shift_x * 128, shift_x * 128 + 256) for shift_x in range(3)]
            multiply([cells[rows, lane] for lane in lanes], parent + 1, half)
        del todo[:count]

    size = fives.shape[0] // 72
    for shift, msg, first in (
        (-1, near_three, 0), (0, near_three, 80), (1, near_three, 160),
        (-4, up_three, 0), (-3, up_three, 80), (-2, up_three, 160),
        (2, down_three, 0), (3, down_three, 80), (4, down_three, 160),
    ):
        at = pl.multiple_of(lax.rem(gx + shift + size, size) * 72, 8)
        fives[pl.ds(at, 72), :] = msg[first : first + 72, :].astype(F32)
    even_up, odd_up = up_blocks(up_ref)
    leaf_products()

    def upward(grouped, split):
        children = dot(grouped.astype(BF16), split).astype(BF16)
        value = dot(even_up, children) + lane_roll(dot(odd_up, children), 64)
        return value.astype(BF16).astype(F32)

    lane = col % 64
    split_five = one_hot(
        (row == ((lane // 16 % 2) * 2 + lane // 32) * 32 + 2 * (lane % 16) + col // 64)
    )
    for x in range(4):
        value = upward(fives[x * GROUP : (x + 1) * GROUP, :], split_five)
        first = (x // 2) * GROUP + (x % 2) * 2 * COEF
        fours[first : first + COEF, :] = value
        fours[first + COEF : first + 2 * COEF, :] = lane_roll(value, 96)
    leaf_products()
    split_four = one_hot((row == (lane // 8) * 16 + 2 * (lane % 8) + col // 64) & (lane < 16))
    for x in range(2):
        value = upward(fours[x * GROUP : (x + 1) * GROUP, :], split_four)
        three32[x * 2 * COEF : x * 2 * COEF + COEF, :] = value
        three32[x * 2 * COEF + COEF : (x + 1) * 2 * COEF, :] = lane_roll(value, 120)
    leaf_products()
    three = dot(three32[...].astype(BF16), one_hot((row == col - 48) & (col >= 48) & (col < 56)))
    wide_low = iota((GROUP, 128), 1) < 64
    for shift_x in range(3):
        if shift_x == 1:
            own, other = six_ref[...].astype(F32), halo_six(below, above)
        else:
            own = (low if shift_x == 0 else high)[X_SIX:X_ROWS, :].astype(F32)
            other = (low_corner if shift_x == 0 else high_corner)[C_SIX:C_FIVE, :].astype(F32)
        six = [
            lane_roll(jnp.where(wide_low, own, other), 64),
            own,
            lane_roll(jnp.where(wide_low, other, own), 64),
        ]
        at = pl.multiple_of(lax.rem(gx // 2 + shift_x + 3, 4) * GROUP, 8)
        five = fives[pl.ds(at, GROUP), :].astype(BF16)
        at = pl.multiple_of(lax.rem(gx // 4 + shift_x + 1, 2) * GROUP, 8)
        four = fours[pl.ds(at, GROUP), :].astype(BF16)
        for shift_y in range(3):
            y_five = lax.rem(gy + shift_y + 3, 4)
            y_four = lax.rem(gy // 2 + shift_y + 1, 2)
            part = dot(five, one_hot((row == y_five * 32 + col) & (col < 32)))
            part = part + dot(
                four, one_hot((row == y_four * 16 + col - 32) & (col >= 32) & (col < 48))
            )
            rows = slice(shift_y * GROUP, (shift_y + 1) * GROUP)
            windows[shift_x, rows, 0:128] = six[shift_y].astype(BF16)
            windows[shift_x, rows, 128:256] = (part + three).astype(BF16)
    for half in range(2):
        multiply([windows[shift_x] for shift_x in range(3)], 0, half)
    leaf_products()
    for bits in range(4):
        coarse[bits, 0:COEF, 0:128] = z_sum(products.at[0], bits, slice(0, 128), six_roll)
        coarse[bits, 0:COEF, 128:256] = z_sum(products.at[0], bits, slice(128, 256), coarse_roll)
    eye = one_hot(iota((8 * COEF, 8 * COEF), 0) == iota((8 * COEF, 8 * COEF), 1))
    down32[...] = dot_nt(eye, down_ref[...])
    downs[...] = jnp.zeros_like(downs)
    for bits in range(4):
        for bit in range(2):
            first = (2 * bits + bit) * COEF
            downs[bit, bits * 40 : bits * 40 + COEF, :] = down32[first : first + COEF, :]
    operators = [downs[bit].astype(BF16) for bit in range(2)]

    def spread(value, mask):
        return [dot(part, one_hot(mask)).astype(BF16) for part in parts(value)]

    def lift(wide, lanes):
        halves = [dot(value, wide[0]) + dot(value, wide[1]) for value in operators]
        lifted[:, lanes] = jnp.where(iota(halves[0].shape, 1) % 2 == 1, halves[1], halves[0])

    def child(bits, lanes):
        first = bits * 40 if isinstance(bits, int) else pl.multiple_of(bits * 40, 8)
        return lifted[pl.ds(first, COEF), lanes]

    first_lanes = slice(0, 128)

    right = slice(128, 256)
    bits = 2 * lax.rem(gx // 4, 2) + lax.rem(gy // 2, 2)
    value = coarse[bits, 0:COEF, right]
    wide = spread(value, (row == 48 + (col - 32) // 2) & (col >= 32) & (col < 48))
    bits = 2 * lax.rem(gx // 2, 2) + lax.rem(gy, 2)
    lift(wide, first_lanes)
    leaf_products()
    value = coarse[bits, 0:COEF, right] + child(bits, first_lanes)
    wide = spread(value, (row == 32 + col // 2) & (col < 32))
    lift(wide, first_lanes)
    leaf_products()
    wides = []
    for y in range(2):
        bits = 2 * lax.rem(gx, 2) + y
        value = coarse[bits, 0:COEF, right] + child(bits, first_lanes)
        wides.append(spread(value, (row == (col % 64) // 2) & (col // 64 == y)))
    wide = [(a.astype(F32) + b.astype(F32)).astype(BF16) for a, b in zip(*wides)]
    lift(wide, first_lanes)
    leaf_products()
    for bits in range(4):
        value = coarse[bits, 0:COEF, 0:128] + child(bits, first_lanes)
        for y in range(2):
            for k, part in enumerate(spread(value, row == y * 64 + col // 2)):
                at = ((bits // 2) * 4 + 2 * y + bits % 2) * 128
                expand[k, :, at : at + 128] = part
    leaf_products(8)
    lift([expand[k] for k in range(2)], slice(0, 1024))
    for parent in range(4):
        for xp in range(2):
            at = (xp * 4 + parent) * 128
            for bits in range(4):
                value = z_sum(
                    products.at[parent + 1], bits, slice(xp * 128, xp * 128 + 128), leaf_roll
                )
                x, y = 2 * xp + bits // 2, 2 * parent + bits % 2
                rows = pl.ds(x * 8 + y, COEF, stride=32)
                out_ref[rows, :] = value + child(bits, slice(at, at + 128))


def all_levels(*inputs):
    return kernel_call(
        levels_kernel,
        (shape((1152, 128), F32),),
        inputs,
        (
            pltpu.VMEM((6 * GROUP, 512), BF16),
            pltpu.VMEM((576, 128), F32),
            pltpu.VMEM((2 * GROUP, 128), F32),
            pltpu.VMEM((GROUP, 128), F32),
            pltpu.VMEM((3, 3 * GROUP, 256), BF16),
            pltpu.VMEM((5, 1024, 256), F32),
            pltpu.VMEM((4, 40, 256), F32),
            pltpu.VMEM((8 * COEF, COEF), F32),
            pltpu.VMEM((2, 160, COEF), F32),
            pltpu.VMEM((2, COEF, 1024), BF16),
            pltpu.VMEM((160, 1024), F32),
        ),
        scalars=1,
    )[0]


def moved(value, step_x, step_y):
    size_x, size_y = lax.axis_size("gx"), lax.axis_size("gy")
    table = [
        (x * size_y + y, (x + step_x) % size_x * size_y + (y + step_y) % size_y)
        for x in range(size_x)
        for y in range(size_y)
    ]
    return lax.ppermute(value, ("gx", "gy"), table)


def per_device(
    leaf_multipoles, positions, masses, counts, up_operator, far_operator, down_operator
):
    place = jnp.stack([lax.axis_index("gx"), lax.axis_index("gy")]).astype(jnp.int32)
    (
        grid, up_msg, down_msg, low_msg, high_msg, six, five, live,
        positions, counts, up_operator,
    ) = prepare(
        leaf_multipoles.reshape(1152, 128), positions.reshape(768, 128), masses.reshape(256, 128),
        counts.reshape(32, 128), up_operator.T,
    )
    positions = positions.reshape(3, 8, 4, 8, 128)
    counts = counts.reshape(4, 8, 128)
    below, above, two = moved(up_msg, 0, 1), moved(down_msg, 0, -1), moved(five, 0, 2)
    low, high = moved(high_msg, 1, 0), moved(low_msg, -1, 0)
    inner, shifted, far_operator, down_operator = plane_pairs(
        positions, live.reshape(8, 4, 8, 128), far_operator, down_operator
    )
    matrix = far_matrix(far_operator)
    below, above, two, inner, matrix = lax.optimization_barrier((below, above, two, inner, matrix))
    to_low, to_high = cross(place, below, above, two, five)
    low_corner, high_corner = moved(to_high, 1, 0), moved(to_low, -1, 0)
    inner = step_pairs(inner, shifted)
    inner = row_pairs(inner, positions, below, above)
    low, high, low_corner, high_corner, inner = lax.optimization_barrier(
        (low, high, low_corner, high_corner, inner)
    )
    three = jnp.concatenate([low_corner[C_FIVE:], to_low[C_FIVE:], high_corner[C_FIVE:]], axis=0)
    up_three, down_three = moved(three, 3, 0), moved(three, -3, 0)
    potential = face_pairs(inner, positions, counts, low, high, low_corner, high_corner)
    up_three, down_three, potential = lax.optimization_barrier((up_three, down_three, potential))
    expansion = all_levels(
        place, matrix, grid, six, below, above, low, high, low_corner, high_corner,
        three, up_three, down_three, up_operator, down_operator,
    )
    return expansion.reshape(36, 4, 8, 128), potential


def extended(cells, sides, width):
    for axis, dim in sides:
        count = lax.axis_size(axis)
        head = lax.slice_in_dim(cells, 0, width, axis=dim)
        tail = lax.slice_in_dim(cells, cells.shape[dim] - width, cells.shape[dim], axis=dim)
        cells = jnp.concatenate(
            [
                lax.ppermute(tail, axis, [(i, (i + 1) % count) for i in range(count)]),
                cells,
                lax.ppermute(head, axis, [((i + 1) % count, i) for i in range(count)]),
            ],
            axis=dim,
        )
    return cells


def shift_list():
    return [
        (step_x, step_y, step_z)
        for step_x in (-1, 0, 1)
        for step_y in (-1, 0, 1)
        for step_z in (-1, 0, 1)
    ]


def child_bits(number):
    return (number // 4, number // 2 % 2, number % 2)


def offset_table():
    vectors = [
        (step_x, step_y, step_z)
        for step_x in range(-3, 4)
        for step_y in range(-3, 4)
        for step_z in range(-3, 4)
        if max(abs(step_x), abs(step_y), abs(step_z)) >= 2
    ]
    lookup = np.full((27, 8, 8), len(vectors), dtype=np.int32)
    for shift_id, offset in enumerate(shift_list()):
        for source in range(8):
            for target in range(8):
                vector = tuple(
                    (
                        2 * offset[axis_id]
                        + child_bits(source)[axis_id]
                        - child_bits(target)[axis_id]
                        for axis_id in range(3)
                    )
                )
                if max(abs(vector[0]), abs(vector[1]), abs(vector[2])) >= 2:
                    lookup[shift_id, source, target] = vectors.index(vector)
    return lookup


def assemble(far_operator):
    coeff_count = far_operator.shape[0]
    blocks = far_operator.reshape(coeff_count, -1, coeff_count)
    blocks = jnp.concatenate(
        [blocks, jnp.zeros((coeff_count, 1, coeff_count), blocks.dtype)], axis=1
    )
    picked = jnp.take(blocks, jnp.asarray(offset_table().reshape(-1), dtype=jnp.int32), axis=1)
    picked = picked.reshape(coeff_count, 27, 8, 8, coeff_count).transpose(1, 2, 0, 3, 4)
    return picked.reshape(27, 8 * coeff_count, 8 * coeff_count)


def group_cells(volume):
    size_x, size_y, size_z, coeff_count = volume.shape
    reshaped = volume.reshape(size_x // 2, 2, size_y // 2, 2, size_z // 2, 2, coeff_count)
    return reshaped.transpose(0, 2, 4, 1, 3, 5, 6).reshape(
        size_x // 2, size_y // 2, size_z // 2, 8 * coeff_count
    )


def spread_cells(grouped):
    size_x, size_y, size_z, total_rows = grouped.shape
    coeff_count = total_rows // 8
    reshaped = grouped.reshape(size_x, size_y, size_z, 2, 2, 2, coeff_count)
    return reshaped.transpose(0, 3, 1, 4, 2, 5, 6).reshape(
        2 * size_x, 2 * size_y, 2 * size_z, coeff_count
    )


def wrap_pad(volume, axis_id):
    extent = volume.shape[axis_id]
    lower = lax.slice_in_dim(volume, extent - 1, extent, axis=axis_id)
    upper = lax.slice_in_dim(volume, 0, 1, axis=axis_id)
    return jnp.concatenate([lower, volume, upper], axis=axis_id)


def wrap_window(volume, axis_id, anchor, extent):
    return lax.dynamic_slice_in_dim(wrap_pad(volume, axis_id), anchor, extent + 2, axis_id)


def region(index_now, cells, levels_up):
    anchor = index_now * cells // 2**levels_up
    extent = max(cells // 2**levels_up, 1)
    return (anchor, extent)


def cut(children, index_x, index_y, cells_x, cells_y, levels_up):
    anchor_x, extent_x = region(index_x, cells_x, levels_up)
    parent_x = region(index_x, cells_x, levels_up + 1)[0]
    anchor_y, extent_y = region(index_y, cells_y, levels_up)
    parent_y = region(index_y, cells_y, levels_up + 1)[0]
    children = lax.dynamic_slice_in_dim(children, anchor_x - 2 * parent_x, extent_x, 0)
    return lax.dynamic_slice_in_dim(children, anchor_y - 2 * parent_y, extent_y, 1)


def coarse_window(grouped, index_x, index_y, cells_x, cells_y, levels_up):
    anchor_x, extent_x = region(index_x, cells_x, levels_up)
    anchor_y, extent_y = region(index_y, cells_y, levels_up)
    windowed = wrap_window(grouped, 0, anchor_x, extent_x)
    windowed = wrap_window(windowed, 1, anchor_y, extent_y)
    return wrap_pad(windowed, 2)


def upward(up_operator, grouped):
    parent = jnp.einsum("xyzs,sj->xyzj", grouped, up_operator, preferred_element_type=jnp.float32)
    return parent.astype(jnp.bfloat16)


def downward(down_operator, parent):
    children = jnp.einsum(
        "xyzi,it->xyzt", parent, down_operator.astype(jnp.float32), precision=lax.Precision.HIGHEST
    )
    return spread_cells(children)


def far_field(padded, kernel):
    size_x = padded.shape[0] - 2
    size_y = padded.shape[1] - 2
    size_z = padded.shape[2] - 2
    running = None
    for shift_id, offset in enumerate(shift_list()):
        window_piece = padded[
            1 + offset[0] : 1 + offset[0] + size_x, 1 + offset[1] : 1 + offset[1] + size_y
        ]
        product_term = jnp.einsum(
            "xyzs,st->xyzt", window_piece, kernel[shift_id], preferred_element_type=jnp.float32
        )
        product_term = product_term[:, :, 1 + offset[2] : 1 + offset[2] + size_z]
        running = product_term if running is None else running + product_term
    return running


def near_field(positions, masses, counts):
    slot_count = masses.shape[0]
    size_x, size_y, size_z = (masses.shape[1], masses.shape[2], masses.shape[3])
    live_slot = lax.broadcasted_iota(jnp.int32, masses.shape, 0) < counts[None]
    live_mass = jnp.where(live_slot, masses, jnp.float32(0.0))
    stacked = jnp.concatenate([positions, live_mass[None]], axis=0)
    padded = wrap_pad(extended(stacked, (("gx", 2), ("gy", 3)), 1), 4)
    block_size = min(8, slot_count)
    same_slot = lax.broadcasted_iota(
        jnp.int32, (block_size, slot_count, 1, 1, 1), 0
    ) + 0 == lax.broadcasted_iota(jnp.int32, (block_size, slot_count, 1, 1, 1), 1)
    running = jnp.zeros((block_size, size_x, size_y, size_z), jnp.float32)
    for offset in shift_list():
        source = padded[
            :,
            :,
            1 + offset[0] : 1 + offset[0] + size_x,
            1 + offset[1] : 1 + offset[1] + size_y,
            1 + offset[2] : 1 + offset[2] + size_z,
        ]
        squared = jnp.float32(SOFTENING * SOFTENING)
        for axis_id in range(3):
            separation = (
                source[axis_id][None] + jnp.float32(offset[axis_id]) - positions[axis_id][:, None]
            )
            squared = squared + separation * separation
        pair_terms = source[3][None] * lax.rsqrt(squared)
        if offset == (0, 0, 0):
            pair_terms = jnp.where(same_slot, jnp.float32(0.0), pair_terms)
        running = running + jnp.sum(pair_terms, axis=1)
    results = running
    running = results
    return jnp.where(live_slot, -running / slot_count, jnp.float32(0.0))


def general_device(
    leaf_multipoles, positions, masses, counts, up_operator, far_operator, down_operator
):
    potential = near_field(positions, masses, counts)
    kernel = assemble(far_operator)
    index_x = lax.axis_index("gx")
    index_y = lax.axis_index("gy")
    cells_x = leaf_multipoles.shape[1]
    cells_y = leaf_multipoles.shape[2]
    leaf_cells = jnp.transpose(leaf_multipoles, (1, 2, 3, 0))
    grouped_leaf = group_cells(leaf_cells)
    padded = wrap_pad(extended(grouped_leaf, (("gx", 0), ("gy", 1)), 1), 2)
    far_leaf = spread_cells(far_field(padded, kernel))
    grouped_six = group_cells(upward(up_operator, grouped_leaf))
    padded = wrap_pad(extended(grouped_six, (("gx", 0), ("gy", 1)), 1), 2)
    far_six = spread_cells(far_field(padded, kernel))
    moments_five = upward(up_operator, grouped_six)
    columns = lax.all_gather(moments_five, "gy", axis=1, tiled=True)
    whole_five = lax.all_gather(columns, "gx", axis=0, tiled=True)
    grouped_five = group_cells(whole_five)
    window_five = coarse_window(grouped_five, index_x, index_y, cells_x, cells_y, 3)
    moments_four = upward(up_operator, grouped_five)
    far_five = cut(
        spread_cells(far_field(window_five, kernel)), index_x, index_y, cells_x, cells_y, 2
    )
    grouped_four = group_cells(moments_four)
    window_four = coarse_window(grouped_four, index_x, index_y, cells_x, cells_y, 4)
    far_four = cut(
        spread_cells(far_field(window_four, kernel)), index_x, index_y, cells_x, cells_y, 3
    )
    grouped_three = group_cells(upward(up_operator, grouped_four))
    window_three = coarse_window(grouped_three, index_x, index_y, cells_x, cells_y, 5)
    far_three = cut(
        spread_cells(far_field(window_three, kernel)), index_x, index_y, cells_x, cells_y, 4
    )
    expansion = far_three
    expansion = far_four + cut(
        downward(down_operator, expansion), index_x, index_y, cells_x, cells_y, 3
    )
    expansion = far_five + cut(
        downward(down_operator, expansion), index_x, index_y, cells_x, cells_y, 2
    )
    expansion = far_six + cut(
        downward(down_operator, expansion), index_x, index_y, cells_x, cells_y, 1
    )
    expansion = far_leaf + cut(
        downward(down_operator, expansion), index_x, index_y, cells_x, cells_y, 0
    )
    return (jnp.transpose(expansion, (3, 0, 1, 2)), potential)


def solution(mesh):
    small = (mesh.shape["gx"], mesh.shape["gy"]) == (8, 4)
    return jax.shard_map(
        per_device if small else general_device,
        mesh=mesh,
        in_specs=(
            P(None, "gx", "gy", None),
            P(None, None, "gx", "gy", None),
            P(None, "gx", "gy", None),
            P("gx", "gy", None),
            P(),
            P(),
            P(),
        ),
        out_specs=(P(None, "gx", "gy", None), P(None, "gx", "gy", None)),
        check_vma=False,
    )
```

```python
import functools

import jax
import jax.numpy as jnp
import numpy as np
from jax import lax
from jax.experimental import pallas as pl
from jax.experimental.pallas import tpu as pltpu
from jax.sharding import PartitionSpec as P

SOFTENING = 0.05
EPS = SOFTENING * SOFTENING
F32 = jnp.float32
BF16 = jnp.bfloat16
COEF = 36
GROUP = 4 * COEF
Y_LEAF = 128 + 96
Y_SIX = Y_LEAF + 2 * GROUP
Y_FIVE = Y_SIX + GROUP // 2
Y_ROWS = Y_FIVE + 40
X_LEAF = 256 + 192
X_SIX = X_LEAF + 4 * GROUP
X_ROWS = X_SIX + GROUP
C_LEAF = 2 * 56
C_SIX = C_LEAF + 2 * GROUP
C_FIVE = C_SIX + GROUP
C_ROWS = C_FIVE + 80

VMEM = pl.BlockSpec(memory_space=pltpu.VMEM)
SMEM = pl.BlockSpec(memory_space=pltpu.SMEM)
HBM = pl.BlockSpec(memory_space=pltpu.MemorySpace.HBM)


def shape(dims, dtype):
    return jax.ShapeDtypeStruct(dims, dtype)


def kernel_call(body, outs, inputs, scratch=(), scalars=0, space=VMEM, limit=20):
    return pl.pallas_call(
        body,
        out_shape=outs,
        in_specs=[SMEM] * scalars + [space] * (len(inputs) - scalars),
        out_specs=[VMEM] * len(outs),
        scratch_shapes=list(scratch),
        compiler_params=pltpu.CompilerParams(vmem_limit_bytes=limit * 1024 * 1024),
    )(*inputs)


def iota(dims, axis):
    return lax.broadcasted_iota(jnp.int32, dims, axis)


def dot(lhs, rhs):
    return lax.dot_general(lhs, rhs, (((1,), (0,)), ((), ())), preferred_element_type=F32)


def dot_tn(lhs, rhs):
    return lax.dot_general(lhs, rhs, (((0,), (0,)), ((), ())), preferred_element_type=F32)


def dot_nt(lhs, rhs):
    return lax.dot_general(lhs, rhs, (((1,), (1,)), ((), ())), preferred_element_type=F32)


def one_hot(mask):
    return jnp.where(mask, F32(1.0), F32(0.0)).astype(BF16)


def parts(value):
    high = value.astype(BF16)
    return high, (value - high.astype(F32)).astype(BF16)


def lane_roll(value, shift):
    return pltpu.roll(value, shift % 128, 1) if shift % 128 else value


def up_blocks(up_ref):
    row, col = iota((8 * COEF, GROUP), 0), iota((8 * COEF, GROUP), 1)
    return [
        dot(up_ref[...], one_hot(row == (col // COEF * 2 + bit) * COEF + col % COEF)).astype(BF16)
        for bit in range(2)
    ]


def prep_kernel(
    leaf_hbm, pos_hbm, mass_hbm, count_hbm, up_hbm,
    grid_ref, up_msg, down_msg, low_msg, high_msg, six_ref, five_ref, live_ref,
    pos_ref, count_ref, up_ref,
    leaf_ref, mass_ref, m32, x32, six32, near32, sems,
):
    copies = [
        pltpu.make_async_copy(source, target, sems.at[k])
        for k, (source, target) in enumerate(
            (
                (leaf_hbm, leaf_ref), (pos_hbm, pos_ref), (mass_hbm, mass_ref),
                (count_hbm, count_ref), (up_hbm, up_ref),
            )
        )
    ]
    for copy in copies:
        copy.start()
    copies[0].wait()
    m32[...] = leaf_ref[...].astype(F32)
    for x in range(4):
        for y in range(8):
            start = ((x // 2) * 4 + y // 2) * GROUP + (2 * (x % 2) + y % 2) * COEF
            x32[start : start + COEF, :] = m32[pl.ds(x * 8 + y, COEF, stride=32), :]
    grid = x32[...].astype(BF16)
    grid_ref[...] = grid
    for msg, parent in ((up_msg, 3), (down_msg, 0)):
        for xp in range(2):
            msg[Y_LEAF + xp * GROUP : Y_LEAF + (xp + 1) * GROUP, :] = grid_ref[
                (xp * 4 + parent) * GROUP : (xp * 4 + parent + 1) * GROUP, :
            ]
    low_msg[X_LEAF:X_SIX, :] = grid_ref[0 : 4 * GROUP, :]
    high_msg[X_LEAF:X_SIX, :] = grid_ref[4 * GROUP : 8 * GROUP, :]
    for copy in copies[1:]:
        copy.wait()
    count = count_ref[...]
    for slot in range(8):
        live_ref[slot * 32 : slot * 32 + 32, :] = jnp.where(
            count > slot, mass_ref[slot * 32 : slot * 32 + 32, :], F32(0.0)
        )
    for msg, y in ((up_msg, 7), (down_msg, 0)):
        rows = []
        for x in range(4):
            rows.append(pos_ref[pl.ds(x * 8 + y, 24, stride=32), :])
            rows.append(live_ref[pl.ds(x * 8 + y, 8, stride=32), :])
        high, low = parts(jnp.concatenate(rows, axis=0))
        msg[0:128, :] = high
        for x in range(4):
            msg[128 + 24 * x : 152 + 24 * x, :] = low[32 * x : 32 * x + 24]
    for msg, x in ((low_msg, 0), (high_msg, 3)):
        for slot in range(8):
            for axis in range(3):
                start = (axis * 8 + slot) * 32 + x * 8
                near32[pl.ds(axis * 8 + slot, 8, stride=32), :] = pos_ref[start : start + 8, :]
            start = slot * 32 + x * 8
            near32[pl.ds(24 + slot, 8, stride=32), :] = live_ref[start : start + 8, :]
        high, low = parts(near32[...])
        msg[0:256, :] = high
        for y in range(8):
            msg[256 + 24 * y : 280 + 24 * y, :] = low[32 * y : 32 * y + 24]
    low_half = iota((COEF, 128), 1) < 64
    even_up, odd_up = up_blocks(up_ref)
    row, col = iota((128, 128), 0), iota((128, 128), 1)
    split_z = one_hot(row == 2 * (col % 64) + col // 64)
    split = dot(grid, split_z).astype(BF16)
    columns = jnp.concatenate([split[k * GROUP : (k + 1) * GROUP] for k in range(8)], axis=1)
    even, odd = dot(even_up, columns), dot(odd_up, columns)
    for xp in range(2):
        for y in range(2):
            first, second = (xp * 4 + y) * 128, (xp * 4 + 2 + y) * 128
            near_part = even[:, first : first + 128] + lane_roll(odd[:, first : first + 128], 64)
            far_part = lane_roll(even[:, second : second + 128], 64) + odd[:, second : second + 128]
            start = (2 * xp + y) * COEF
            six32[start : start + COEF, :] = jnp.where(low_half, near_part, far_part)
    six = six32[...].astype(BF16)
    six_ref[...] = six
    low_msg[X_SIX:X_ROWS, :] = six
    high_msg[X_SIX:X_ROWS, :] = six
    left = iota((72, 128), 1) < 64
    first, second = six32[0:72, :], six32[72:144, :]
    up_msg[Y_SIX:Y_FIVE, :] = jnp.where(left, lane_roll(first, 64), second).astype(BF16)
    down_msg[Y_SIX:Y_FIVE, :] = jnp.where(left, first, lane_roll(second, 64)).astype(BF16)
    split_six = one_hot(row == ((col // 32) % 2) * 64 + 2 * (col % 32) + col // 64)
    split = dot(six, split_six).astype(BF16)
    five = dot(even_up, split) + lane_roll(dot(odd_up, split), 64)
    five = jnp.concatenate([five, jnp.zeros((4, 128), F32)], axis=0).astype(BF16)
    five_ref[...] = five
    for msg in (up_msg, down_msg):
        msg[Y_FIVE:Y_ROWS, :] = five


def in_hbm(value):
    return pltpu.with_memory_space_constraint(value, pltpu.MemorySpace.HBM)


def prepare(leaf, positions, masses, counts, up_operator):
    inputs = (leaf, positions, masses, counts, up_operator)
    return kernel_call(
        prep_kernel,
        (
            shape((8 * GROUP, 128), BF16),
            shape((Y_ROWS, 128), BF16),
            shape((Y_ROWS, 128), BF16),
            shape((X_ROWS, 128), BF16),
            shape((X_ROWS, 128), BF16),
            shape((GROUP, 128), BF16),
            shape((40, 128), BF16),
            shape((256, 128), F32),
            shape((768, 128), F32),
            shape((32, 128), jnp.int32),
            shape(up_operator.shape, BF16),
        ),
        [in_hbm(value) for value in inputs],
        (
            pltpu.VMEM((1152, 128), BF16),
            pltpu.VMEM((256, 128), F32),
            pltpu.VMEM((1152, 128), F32),
            pltpu.VMEM((1152, 128), F32),
            pltpu.VMEM((GROUP, 128), F32),
            pltpu.VMEM((256, 128), F32),
            pltpu.SemaphoreType.DMA((5,)),
        ),
        space=HBM,
    )


def halo_six(below, above):
    upper, lower = above[Y_SIX:Y_FIVE, :].astype(F32), below[Y_SIX:Y_FIVE, :].astype(F32)
    left = iota((72, 128), 1) < 64
    return jnp.concatenate(
        [
            jnp.where(left, upper, lane_roll(lower, 64)),
            jnp.where(left, lane_roll(upper, 64), lower),
        ],
        axis=0,
    )


def cross_kernel(place, below, above, two, own, to_low, to_high, five32):
    lane = iota((COEF, 128), 1) // 32
    five32[...] = jnp.zeros_like(five32)
    for shift, ref, first in ((0, own, 0), (3, below, Y_FIVE), (1, above, Y_FIVE), (2, two, 0)):
        at = lax.rem(place[1] + shift, 4)
        value = ref[first : first + 40, :].astype(F32)
        for y in range(2):
            moved = pltpu.roll(value, lax.rem(32 * at + 96 * y, 128), 1)[0:COEF]
            rows = slice(y * COEF, (y + 1) * COEF)
            five32[rows, :] = jnp.where(lane == at, moved, five32[rows, :])
    five = five32[...].astype(BF16)
    halo = halo_six(below, above).astype(BF16)
    for msg, x, xp in ((to_low, 0, 0), (to_high, 3, 1)):
        for side, ref in enumerate((below, above)):
            first = side * 56
            msg[first : first + 32, :] = ref[32 * x : 32 * x + 32, :]
            msg[first + 32 : first + 56, :] = ref[128 + 24 * x : 152 + 24 * x, :]
            source, first = Y_LEAF + xp * GROUP, C_LEAF + side * GROUP
            msg[first : first + GROUP, :] = ref[source : source + GROUP, :]
        msg[C_SIX:C_FIVE, :] = halo
        msg[C_FIVE:C_ROWS, :] = five


def cross(*inputs):
    return kernel_call(
        cross_kernel,
        (shape((C_ROWS, 128), BF16), shape((C_ROWS, 128), BF16)),
        inputs,
        (pltpu.VMEM((80, 128), F32),),
        scalars=1,
    )


def inverse_distance(target, source):
    squared = F32(EPS)
    for axis in range(3):
        separation = source[axis] - target[axis]
        squared = squared + separation * separation
    return lax.rsqrt(squared)


def pair_sums(shifted, sums, goals, x, step, totals):
    step_x, step_y, step_z = step
    edge = iota((8, 128), 0) == (7 if step_y > 0 else 0)
    for slot in range(8):
        source = [shifted[step_z + 1, k, slot, x] for k in range(4)]
        if step_y:
            source = [pltpu.roll(value, (-step_y) % 8, 0) for value in source]
            source[1] = source[1] + F32(step_y)
            source[3] = jnp.where(edge, F32(0.0), source[3])
        if step_x:
            source[0] = source[0] + F32(step_x)
        back = None
        for goal in range(8):
            inverse = inverse_distance(goals[goal], source)
            totals[goal] = totals[goal] + source[3] * inverse
            term = goals[goal][3] * inverse
            back = term if back is None else back + term
        if step_y:
            back = pltpu.roll(jnp.where(edge, F32(0.0), back), step_y % 8, 0)
        sums[step_z + 1, slot, x] = sums[step_z + 1, slot, x] + back


def plane_goals(shifted, x):
    return [[shifted[1, k, slot, x] for k in range(4)] for slot in range(8)]


def step_pairs(shifted, sums, x):
    for step_y in (-1, 0, 1):
        goals = plane_goals(shifted, x)
        totals = [sums[1, slot, x] for slot in range(8)]
        for step_z in (-1, 0, 1):
            pair_sums(shifted, sums, goals, x + 1, (1, step_y, step_z), totals)
        for slot in range(8):
            sums[1, slot, x] = totals[slot]


def plane_kernel(pos_ref, live_ref, far_hbm, down_hbm, sums, shifted, far_ref, down_ref, sems):
    copies = [
        pltpu.make_async_copy(source, target, sems.at[k])
        for k, (source, target) in enumerate(((far_hbm, far_ref), (down_hbm, down_ref)))
    ]
    for copy in copies:
        copy.start()
    sums[...] = jnp.zeros_like(sums)

    def plane(x, carry):
        for slot in range(8):
            values = [pos_ref[axis, slot, x] for axis in range(3)] + [live_ref[slot, x]]
            for index, step in enumerate((-1, 0, 1)):
                moved = [lane_roll(value, -step) for value in values]
                if step:
                    moved[2] = moved[2] + F32(step)
                for k in range(4):
                    shifted[index, k, slot, x] = moved[k]
        goals = plane_goals(shifted, x)
        totals = [jnp.zeros((8, 128), F32) for slot in range(8)]
        for slot in range(8):
            for goal in range(slot):
                inverse = inverse_distance(goals[goal], goals[slot])
                totals[goal] = totals[goal] + goals[slot][3] * inverse
                totals[slot] = totals[slot] + goals[goal][3] * inverse
        for step in ((0, 0, 1), (0, 1, -1), (0, 1, 0), (0, 1, 1)):
            pair_sums(shifted, sums, goals, x, step, totals)
        for slot in range(8):
            sums[1, slot, x] = sums[1, slot, x] + totals[slot]
        return carry

    lax.fori_loop(0, 4, plane, 0)

    def step(x, carry):
        step_pairs(shifted, sums, x)
        return carry

    lax.fori_loop(0, 2, step, 0)
    for copy in copies:
        copy.wait()


def plane_pairs(positions, live, far_operator, down_operator):
    return pl.pallas_call(
        plane_kernel,
        out_shape=(
            shape((3, 8, 4, 8, 128), F32),
            shape((3, 4, 8, 4, 8, 128), F32),
            shape(far_operator.shape, BF16),
            shape(down_operator.shape, BF16),
        ),
        in_specs=[VMEM, VMEM, HBM, HBM],
        out_specs=[VMEM] * 4,
        scratch_shapes=[pltpu.SemaphoreType.DMA((2,))],
        compiler_params=pltpu.CompilerParams(vmem_limit_bytes=16 * 1024 * 1024),
    )(positions, live, in_hbm(far_operator), in_hbm(down_operator))


def joined(target, msg, high, low, count):
    for cell in range(count):
        first = 32 * cell
        whole = msg[high + first : high + first + 32, :].astype(F32)
        rest = msg[low + 24 * cell : low + 24 * cell + 24, :].astype(F32)
        target[first : first + 24, :] = whole[0:24] + rest
        target[first + 24 : first + 32, :] = whole[24:32]


def add_sources(fetch, shifted, goals, totals):
    for slot in range(8):
        values = [fetch(k, slot) for k in range(4)]
        for step in (-1, 0, 1):
            moved = [lane_roll(value, -step) for value in values]
            if step:
                moved[2] = moved[2] + F32(step)
            for k in range(4):
                shifted[step + 1, k, slot] = moved[k]
    totals = list(totals)
    for step in range(3):
        for slot in range(8):
            source = [shifted[step, k, slot] for k in range(4)]
            for goal in range(8):
                totals[goal] = totals[goal] + source[3] * inverse_distance(goals[goal], source)
    return tuple(totals)


def rows_kernel(
    inner_ref, pos_ref, count_ref, below, above, low_corner, high_corner, out_ref,
    sources, shifted, added,
):
    turn = jnp.where(iota((8, 128), 0) >= 4, F32(1.0), F32(-1.0))
    for side, msg in enumerate((below, above)):
        first = side * 128
        joined(sources.at[1, pl.ds(first, 128)], msg, 0, 128, 4)
        high = side * 56
        joined(sources.at[0, pl.ds(first, 32)], low_corner, high, high + 32, 1)
        sources[0, first + 32 : first + 128, :] = sources[1, first : first + 96, :]
        sources[2, first : first + 96, :] = sources[1, first + 32 : first + 128, :]
        joined(sources.at[2, pl.ds(first + 96, 32)], high_corner, high, high + 32, 1)
    goals = []
    for slot in range(8):
        at = [(axis * 8 + slot) * 32 for axis in range(3)]
        goals.append(
            [
                jnp.concatenate(
                    [pos_ref[pl.ds(a, 4, stride=8), :], pos_ref[pl.ds(a + 7, 4, stride=8), :]], axis=0
                )
                for a in at
            ]
        )

    def body(step_x, totals):
        def fetch(k, slot):
            value = sources[step_x, pl.ds(8 * k + slot, 8, stride=32), :]
            if k == 0:
                value = value + (step_x - 1).astype(F32)
            return value + turn if k == 1 else value

        return add_sources(fetch, shifted, goals, totals)

    totals = lax.fori_loop(0, 3, body, tuple(jnp.zeros((8, 128), F32) for slot in range(8)))
    added[...] = jnp.zeros_like(added)
    for slot in range(8):
        added[pl.ds(slot * 32, 4, stride=8), :] = totals[slot][0:4]
        added[pl.ds(slot * 32 + 7, 4, stride=8), :] = totals[slot][4:8]
    count = count_ref[...]
    for slot in range(8):
        rows = slice(slot * 32, slot * 32 + 32)
        total = inner_ref[rows, :] + added[rows, :]
        out_ref[rows, :] = jnp.where(count > slot, -total / 8, F32(0.0))


def faces_kernel(sums_ref, shifted_ref, pos_ref, low, high, out_ref, sides, shifted, sums):
    sums[...] = sums_ref[...]
    step_pairs(shifted_ref, sums, 2)
    for x in range(4):
        for slot in range(8):
            out_ref[slot, x] = (
                sums[1, slot, x] + lane_roll(sums[0, slot, x], -1) + lane_roll(sums[2, slot, x], 1)
            )
    sides[...] = jnp.zeros_like(sides)
    for index, msg in enumerate((low, high)):
        joined(sides.at[index, pl.ds(32, 256)], msg, 0, 256, 8)

    def face(index, carry):
        x = 3 * index
        goals = [[pos_ref[axis, slot, x] for axis in range(3)] for slot in range(8)]

        def body(step_y, totals):
            def fetch(k, slot):
                value = sides[index, pl.ds(step_y * 32 + 8 * k + slot, 8, stride=32), :]
                if k == 0:
                    value = value + (2 * index - 1).astype(F32)
                return value + (step_y - 1).astype(F32) if k == 1 else value

            return add_sources(fetch, shifted, goals, totals)

        totals = lax.fori_loop(0, 3, body, tuple(out_ref[slot, x] for slot in range(8)))
        for slot in range(8):
            out_ref[slot, x] = totals[slot]
        return carry

    lax.fori_loop(0, 2, face, 0)


def row_pairs(*inputs):
    return kernel_call(
        rows_kernel,
        (shape((256, 128), F32),),
        inputs,
        (
            pltpu.VMEM((3, 256, 128), F32),
            pltpu.VMEM((3, 4, 8, 8, 128), F32),
            pltpu.VMEM((256, 128), F32),
        ),
    )[0]


def face_pairs(*inputs):
    return kernel_call(
        faces_kernel,
        (shape((8, 4, 8, 128), F32),),
        inputs,
        (
            pltpu.VMEM((2, 320, 128), F32),
            pltpu.VMEM((3, 4, 8, 8, 128), F32),
            pltpu.VMEM((3, 8, 4, 8, 128), F32),
        ),
    )[0]


def far_starts():
    starts, count = {}, 0
    for step_x in range(-3, 4):
        for step_y in range(-3, 4):
            starts[step_x, step_y] = count * COEF
            count += 7 if max(abs(step_x), abs(step_y)) >= 2 else 4
    return starts


def operator_kernel(far_ref, out_ref, far32, stack):
    far32[:, 0:11264] = far_ref[:, 0:11264].astype(F32)
    far32[:, 11264:11520] = jnp.zeros((COEF, 256), F32)
    far32[:, 11264:11376] = far_ref[:, 11264:11376].astype(F32)
    lane = iota((COEF, 256), 1)

    def window(start):
        base = start // 128 * 128
        value = far32[:, base : base + 384]
        shift = start - base
        return (pltpu.roll(value, 384 - shift, 1) if shift else value)[:, 0:256]

    starts = far_starts()
    for step_x in range(-3, 4):
        for step_y in range(-3, 4):
            start = starts[step_x, step_y]
            if max(abs(step_x), abs(step_y)) >= 2:
                block = jnp.where(lane < 7 * COEF, window(start), F32(0.0))
            else:
                block = jnp.where(
                    lane < 2 * COEF,
                    window(start),
                    jnp.where(
                        (lane >= 5 * COEF) & (lane < 7 * COEF), window(start - 3 * COEF), F32(0.0)
                    ),
                )
            for bit_x in range(2):
                for bit_y in range(2):
                    source_x, source_y = step_x + bit_x, step_y + bit_y
                    if -2 <= source_x <= 3 and -2 <= source_y <= 3:
                        shift_x, child_x = source_x // 2 + 1, source_x % 2
                        shift_y, child_y = source_y // 2 + 1, source_y % 2
                        first = shift_y * GROUP + (2 * child_x + child_y) * COEF
                        bits = (2 * bit_x + bit_y) * 256
                        stack[shift_x, first : first + COEF, bits : bits + 256] = block
    out_ref[...] = stack[...].astype(BF16)


def far_matrix(far_operator):
    return kernel_call(
        operator_kernel,
        (shape((3, 3 * GROUP, 1024), BF16),),
        (far_operator,),
        (pltpu.VMEM((COEF, 11520), F32), pltpu.VMEM((3, 3 * GROUP, 1024), F32)),
    )[0]


def z_sum(products, bits, lanes, first):
    odd = iota((COEF, 128), 1) % 2 != first
    total = None
    for step in range(-3, 4):
        start = bits * 256 + (step + 3) * COEF
        value = lane_roll(products[start : start + COEF, lanes], -step)
        if step == 3:
            value = jnp.where(odd, F32(0.0), value)
        if step == -3:
            value = jnp.where(odd, value, F32(0.0))
        total = value if total is None else total + value
    return total


def multiply(matrix, rows, sources):
    total = None
    for shift_x, source in enumerate(sources):
        term = dot_tn(matrix[shift_x, :, rows], source)
        total = term if total is None else total + term
    return total


def windows_x(cells, parent):
    rows = slice(parent * GROUP, (parent + 3) * GROUP)
    return [cells[rows, shift_x * 128 : shift_x * 128 + 256] for shift_x in range(3)]


def middle_kernel(matrix, grid_ref, low, high, products, cells):
    cells[:, 0:128] = low[X_LEAF:X_SIX, :]
    cells[:, 128:256] = grid_ref[0 : 4 * GROUP, :]
    cells[:, 256:384] = grid_ref[4 * GROUP : 8 * GROUP, :]
    cells[:, 384:512] = high[X_LEAF:X_SIX, :]
    for parent in range(2):
        products[parent] = multiply(matrix, slice(0, 1024), windows_x(cells, parent))


def middle_products(*inputs):
    return kernel_call(
        middle_kernel,
        (shape((2, 1024, 256), F32),),
        inputs,
        (pltpu.VMEM((4 * GROUP, 512), BF16),),
    )[0]


def levels_kernel(
    place, matrix, middle, grid_ref, six_ref, below, above, low, high, low_corner, high_corner,
    near_three, up_three, down_three, up_ref, down_ref, out_ref,
    cells, fives, fours, three32, windows, products, coarse, down32, downs, expand, lifted,
):
    gx, gy = place[0], place[1]
    row, col = iota((128, 128), 0), iota((128, 128), 1)

    for first, msg, corner in ((0, low, low_corner), (384, high, high_corner)):
        lanes = slice(first, first + 128)
        cells[0:GROUP, lanes] = corner[C_LEAF : C_LEAF + GROUP, :]
        cells[GROUP : 5 * GROUP, lanes] = msg[X_LEAF:X_SIX, :]
        cells[5 * GROUP : 6 * GROUP, lanes] = corner[C_LEAF + GROUP : C_SIX, :]
    for xp in range(2):
        lanes = slice(128 + 128 * xp, 256 + 128 * xp)
        source = Y_LEAF + xp * GROUP
        cells[0:GROUP, lanes] = below[source : source + GROUP, :]
        cells[GROUP : 5 * GROUP, lanes] = grid_ref[xp * 4 * GROUP : (xp + 1) * 4 * GROUP, :]
        cells[5 * GROUP : 6 * GROUP, lanes] = above[source : source + GROUP, :]

    todo = [(side, half) for side in range(2) for half in range(2)]

    def leaf_products(count=1):
        for side, half in todo[:count]:
            rows = slice(half * 512, half * 512 + 512)
            products[side + 1, rows, :] = multiply(matrix, rows, windows_x(cells, 3 * side))
        del todo[:count]

    size = fives.shape[0] // 72
    for shift, msg, first in (
        (-1, near_three, 0), (0, near_three, 80), (1, near_three, 160),
        (-4, up_three, 0), (-3, up_three, 80), (-2, up_three, 160),
        (2, down_three, 0), (3, down_three, 80), (4, down_three, 160),
    ):
        at = pl.multiple_of(lax.rem(gx + shift + size, size) * 72, 8)
        fives[pl.ds(at, 72), :] = msg[first : first + 72, :].astype(F32)
    even_up, odd_up = up_blocks(up_ref)
    leaf_products()

    def upward(grouped, split):
        children = dot(grouped.astype(BF16), split).astype(BF16)
        value = dot(even_up, children) + lane_roll(dot(odd_up, children), 64)
        return value.astype(BF16).astype(F32)

    lane = col % 64
    split_five = one_hot(
        (row == ((lane // 16 % 2) * 2 + lane // 32) * 32 + 2 * (lane % 16) + col // 64)
    )
    for x in range(4):
        value = upward(fives[x * GROUP : (x + 1) * GROUP, :], split_five)
        first = (x // 2) * GROUP + (x % 2) * 2 * COEF
        fours[first : first + COEF, :] = value
        fours[first + COEF : first + 2 * COEF, :] = lane_roll(value, 96)
    leaf_products()
    split_four = one_hot((row == (lane // 8) * 16 + 2 * (lane % 8) + col // 64) & (lane < 16))
    for x in range(2):
        value = upward(fours[x * GROUP : (x + 1) * GROUP, :], split_four)
        three32[x * 2 * COEF : x * 2 * COEF + COEF, :] = value
        three32[x * 2 * COEF + COEF : (x + 1) * 2 * COEF, :] = lane_roll(value, 120)
    leaf_products()
    def wrapped(first, base, size):
        cell = lax.rem(col - first - 3 + size, size)
        return one_hot((row == base + cell) & (col >= first) & (col < first + size + 6))

    three = dot(three32[...].astype(BF16), wrapped(92, 0, 8))
    six_lanes = [wrapped(0, 0, 64), wrapped(0, 64, 64)]
    for shift_x in range(3):
        if shift_x == 1:
            own, other = six_ref[...], halo_six(below, above).astype(BF16)
        else:
            own = (low if shift_x == 0 else high)[X_SIX:X_ROWS, :]
            other = (low_corner if shift_x == 0 else high_corner)[C_SIX:C_FIVE, :]
        at = pl.multiple_of(lax.rem(gx // 2 + shift_x + 3, 4) * GROUP, 8)
        five = fives[pl.ds(at, GROUP), :].astype(BF16)
        at = pl.multiple_of(lax.rem(gx // 4 + shift_x + 1, 2) * GROUP, 8)
        four = fours[pl.ds(at, GROUP), :].astype(BF16)
        for shift_y in range(3):
            left = dot(other if shift_y == 0 else own, six_lanes[0 if shift_y == 1 else 1])
            right = dot(other if shift_y == 2 else own, six_lanes[1 if shift_y == 1 else 0])
            y_five = lax.rem(gy + shift_y + 3, 4)
            y_four = lax.rem(gy // 2 + shift_y + 1, 2)
            left = left + dot(five, wrapped(70, y_five * 32, 32))
            right = right + dot(four, wrapped(70, y_four * 16, 16)) + three
            rows = slice(shift_y * GROUP, (shift_y + 1) * GROUP)
            windows[shift_x, rows, 0:128] = left.astype(BF16)
            windows[shift_x, rows, 128:256] = right.astype(BF16)
    for half in range(2):
        rows = slice(half * 512, half * 512 + 512)
        products[0, rows, :] = multiply(matrix, rows, [windows[shift_x] for shift_x in range(3)])
    leaf_products()
    coarse[...] = jnp.zeros_like(coarse)
    for bits in range(4):
        for lanes in (slice(0, 128), slice(128, 256)):
            coarse[bits * 40 : bits * 40 + COEF, lanes] = z_sum(products.at[0], bits, lanes, 1)
    eye = one_hot(iota((8 * COEF, 8 * COEF), 0) == iota((8 * COEF, 8 * COEF), 1))
    down32[...] = dot_nt(eye, down_ref[...])
    downs[...] = jnp.zeros_like(downs)
    for bits in range(4):
        for bit in range(2):
            first = (2 * bits + bit) * COEF
            downs[bit, bits * 40 : bits * 40 + COEF, :] = down32[first : first + COEF, :]
    operators = [downs[bit].astype(BF16) for bit in range(2)]

    def spread(value, mask):
        return [dot(part, one_hot(mask)).astype(BF16) for part in parts(value)]

    def lift(wide, lanes, first):
        halves = [dot(value, wide[0]) + dot(value, wide[1]) for value in operators]
        even = iota(halves[0].shape, 1) % 2 == first
        lifted[:, lanes] = jnp.where(even, halves[0], halves[1])

    def block(bits):
        return pl.ds(bits * 40 if isinstance(bits, int) else pl.multiple_of(bits * 40, 8), COEF)

    left, right, both = slice(0, 128), slice(128, 256), slice(0, 256)
    bits = 2 * lax.rem(gx // 4, 2) + lax.rem(gy // 2, 2)
    value = coarse[block(bits), right]
    wide = spread(value, (row == 95 + (col - 73) // 2) & (col >= 73) & (col < 89))
    lift(wide, left, 1)
    leaf_products()
    bits = 2 * lax.rem(gx // 2, 2) + lax.rem(gy, 2)
    value = coarse[block(bits), right] + lifted[block(bits), left]
    wide = spread(value, (row == 73 + (col - 73) // 2) & (col >= 73) & (col < 105))
    lift(wide, left, 1)
    leaf_products()
    wides = []
    for y in range(2):
        bits = 2 * lax.rem(gx, 2) + y
        value = coarse[block(bits), left] + lifted[block(bits), left]
        wides.append(spread(value, (row == 73 + (col - 3) // 2) & (col >= 3) & (col < 67)))
    lift([jnp.concatenate(pair, axis=1) for pair in zip(*wides)], both, 1)
    leaf_products()
    doubled = one_hot(row == 3 + col // 2)
    for k, part in enumerate(parts(coarse[...] + lifted[:, both])):
        for y in range(2):
            wide = dot(part[:, y * 128 : y * 128 + 128], doubled)
            for bits in range(4):
                at = ((bits // 2) * 4 + 2 * y + bits % 2) * 128
                expand[k, :, at : at + 128] = wide[bits * 40 : bits * 40 + COEF].astype(BF16)
    leaf_products(8)
    lift([expand[k] for k in range(2)], slice(0, 1024), 0)
    for parent in range(4):
        source = middle.at[parent - 1] if parent in (1, 2) else products.at[1 + parent // 3]
        for xp in range(2):
            at = (xp * 4 + parent) * 128
            for bits in range(4):
                value = z_sum(source, bits, slice(xp * 128, xp * 128 + 128), 0)
                x, y = 2 * xp + bits // 2, 2 * parent + bits % 2
                rows = pl.ds(x * 8 + y, COEF, stride=32)
                out_ref[rows, :] = value + lifted[block(bits), at : at + 128]


def all_levels(*inputs):
    return kernel_call(
        levels_kernel,
        (shape((1152, 128), F32),),
        inputs,
        (
            pltpu.VMEM((6 * GROUP, 512), BF16),
            pltpu.VMEM((576, 128), F32),
            pltpu.VMEM((2 * GROUP, 128), F32),
            pltpu.VMEM((GROUP, 128), F32),
            pltpu.VMEM((3, 3 * GROUP, 256), BF16),
            pltpu.VMEM((3, 1024, 256), F32),
            pltpu.VMEM((160, 256), F32),
            pltpu.VMEM((8 * COEF, COEF), F32),
            pltpu.VMEM((2, 160, COEF), F32),
            pltpu.VMEM((2, COEF, 1024), BF16),
            pltpu.VMEM((160, 1024), F32),
        ),
        scalars=1,
    )[0]


def moved(value, step_x, step_y):
    size_x, size_y = lax.axis_size("gx"), lax.axis_size("gy")
    table = [
        (x * size_y + y, (x + step_x) % size_x * size_y + (y + step_y) % size_y)
        for x in range(size_x)
        for y in range(size_y)
    ]
    return lax.ppermute(value, ("gx", "gy"), table)


def per_device(
    leaf_multipoles, positions, masses, counts, up_operator, far_operator, down_operator
):
    place = jnp.stack([lax.axis_index("gx"), lax.axis_index("gy")]).astype(jnp.int32)
    (
        grid, up_msg, down_msg, low_msg, high_msg, six, five, live,
        positions, counts, up_operator,
    ) = prepare(
        leaf_multipoles.reshape(1152, 128), positions.reshape(768, 128), masses.reshape(256, 128),
        counts.reshape(32, 128), up_operator.T,
    )
    positions = positions.reshape(3, 8, 4, 8, 128)
    below, above, two = moved(up_msg, 0, 1), moved(down_msg, 0, -1), moved(five, 0, 2)
    low, high = moved(high_msg, 1, 0), moved(low_msg, -1, 0)
    inner, shifted, far_operator, down_operator = plane_pairs(
        positions, live.reshape(8, 4, 8, 128), far_operator, down_operator
    )
    matrix = far_matrix(far_operator)
    below, above, two, inner, matrix = lax.optimization_barrier((below, above, two, inner, matrix))
    to_low, to_high = cross(place, below, above, two, five)
    low_corner, high_corner = moved(to_high, 1, 0), moved(to_low, -1, 0)
    inner = face_pairs(inner, shifted, positions, low, high)
    low_corner, high_corner, inner = lax.optimization_barrier((low_corner, high_corner, inner))
    three = jnp.concatenate([low_corner[C_FIVE:], to_low[C_FIVE:], high_corner[C_FIVE:]], axis=0)
    up_three, down_three = moved(three, 3, 0), moved(three, -3, 0)
    potential = row_pairs(
        inner.reshape(256, 128), positions.reshape(768, 128), counts, below, above, low_corner,
        high_corner,
    )
    middle = middle_products(lax.optimization_barrier((matrix, low_corner))[0], grid, low, high)
    up_three, down_three, potential, middle = lax.optimization_barrier(
        (up_three, down_three, potential, middle)
    )
    expansion = all_levels(
        place, matrix, middle, grid, six, below, above, low, high, low_corner, high_corner,
        three, up_three, down_three, up_operator, down_operator,
    )
    return expansion.reshape(36, 4, 8, 128), potential.reshape(8, 4, 8, 128)


def extended(cells, sides, width):
    for axis, dim in sides:
        count = lax.axis_size(axis)
        head = lax.slice_in_dim(cells, 0, width, axis=dim)
        tail = lax.slice_in_dim(cells, cells.shape[dim] - width, cells.shape[dim], axis=dim)
        cells = jnp.concatenate(
            [
                lax.ppermute(tail, axis, [(i, (i + 1) % count) for i in range(count)]),
                cells,
                lax.ppermute(head, axis, [((i + 1) % count, i) for i in range(count)]),
            ],
            axis=dim,
        )
    return cells


def shift_list():
    return [
        (step_x, step_y, step_z)
        for step_x in (-1, 0, 1)
        for step_y in (-1, 0, 1)
        for step_z in (-1, 0, 1)
    ]


def child_bits(number):
    return (number // 4, number // 2 % 2, number % 2)


def offset_table():
    vectors = [
        (step_x, step_y, step_z)
        for step_x in range(-3, 4)
        for step_y in range(-3, 4)
        for step_z in range(-3, 4)
        if max(abs(step_x), abs(step_y), abs(step_z)) >= 2
    ]
    lookup = np.full((27, 8, 8), len(vectors), dtype=np.int32)
    for shift_id, offset in enumerate(shift_list()):
        for source in range(8):
            for target in range(8):
                vector = tuple(
                    (
                        2 * offset[axis_id]
                        + child_bits(source)[axis_id]
                        - child_bits(target)[axis_id]
                        for axis_id in range(3)
                    )
                )
                if max(abs(vector[0]), abs(vector[1]), abs(vector[2])) >= 2:
                    lookup[shift_id, source, target] = vectors.index(vector)
    return lookup


def assemble(far_operator):
    coeff_count = far_operator.shape[0]
    blocks = far_operator.reshape(coeff_count, -1, coeff_count)
    blocks = jnp.concatenate(
        [blocks, jnp.zeros((coeff_count, 1, coeff_count), blocks.dtype)], axis=1
    )
    picked = jnp.take(blocks, jnp.asarray(offset_table().reshape(-1), dtype=jnp.int32), axis=1)
    picked = picked.reshape(coeff_count, 27, 8, 8, coeff_count).transpose(1, 2, 0, 3, 4)
    return picked.reshape(27, 8 * coeff_count, 8 * coeff_count)


def group_cells(volume):
    size_x, size_y, size_z, coeff_count = volume.shape
    reshaped = volume.reshape(size_x // 2, 2, size_y // 2, 2, size_z // 2, 2, coeff_count)
    return reshaped.transpose(0, 2, 4, 1, 3, 5, 6).reshape(
        size_x // 2, size_y // 2, size_z // 2, 8 * coeff_count
    )


def spread_cells(grouped):
    size_x, size_y, size_z, total_rows = grouped.shape
    coeff_count = total_rows // 8
    reshaped = grouped.reshape(size_x, size_y, size_z, 2, 2, 2, coeff_count)
    return reshaped.transpose(0, 3, 1, 4, 2, 5, 6).reshape(
        2 * size_x, 2 * size_y, 2 * size_z, coeff_count
    )


def wrap_pad(volume, axis_id):
    extent = volume.shape[axis_id]
    lower = lax.slice_in_dim(volume, extent - 1, extent, axis=axis_id)
    upper = lax.slice_in_dim(volume, 0, 1, axis=axis_id)
    return jnp.concatenate([lower, volume, upper], axis=axis_id)


def wrap_window(volume, axis_id, anchor, extent):
    return lax.dynamic_slice_in_dim(wrap_pad(volume, axis_id), anchor, extent + 2, axis_id)


def region(index_now, cells, levels_up):
    anchor = index_now * cells // 2**levels_up
    extent = max(cells // 2**levels_up, 1)
    return (anchor, extent)


def cut(children, index_x, index_y, cells_x, cells_y, levels_up):
    anchor_x, extent_x = region(index_x, cells_x, levels_up)
    parent_x = region(index_x, cells_x, levels_up + 1)[0]
    anchor_y, extent_y = region(index_y, cells_y, levels_up)
    parent_y = region(index_y, cells_y, levels_up + 1)[0]
    children = lax.dynamic_slice_in_dim(children, anchor_x - 2 * parent_x, extent_x, 0)
    return lax.dynamic_slice_in_dim(children, anchor_y - 2 * parent_y, extent_y, 1)


def coarse_window(grouped, index_x, index_y, cells_x, cells_y, levels_up):
    anchor_x, extent_x = region(index_x, cells_x, levels_up)
    anchor_y, extent_y = region(index_y, cells_y, levels_up)
    windowed = wrap_window(grouped, 0, anchor_x, extent_x)
    windowed = wrap_window(windowed, 1, anchor_y, extent_y)
    return wrap_pad(windowed, 2)


def upward(up_operator, grouped):
    parent = jnp.einsum("xyzs,sj->xyzj", grouped, up_operator, preferred_element_type=jnp.float32)
    return parent.astype(jnp.bfloat16)


def downward(down_operator, parent):
    children = jnp.einsum(
        "xyzi,it->xyzt", parent, down_operator.astype(jnp.float32), precision=lax.Precision.HIGHEST
    )
    return spread_cells(children)


def far_field(padded, kernel):
    size_x = padded.shape[0] - 2
    size_y = padded.shape[1] - 2
    size_z = padded.shape[2] - 2
    running = None
    for shift_id, offset in enumerate(shift_list()):
        window_piece = padded[
            1 + offset[0] : 1 + offset[0] + size_x, 1 + offset[1] : 1 + offset[1] + size_y
        ]
        product_term = jnp.einsum(
            "xyzs,st->xyzt", window_piece, kernel[shift_id], preferred_element_type=jnp.float32
        )
        product_term = product_term[:, :, 1 + offset[2] : 1 + offset[2] + size_z]
        running = product_term if running is None else running + product_term
    return running


def near_field(positions, masses, counts):
    slot_count = masses.shape[0]
    size_x, size_y, size_z = (masses.shape[1], masses.shape[2], masses.shape[3])
    live_slot = lax.broadcasted_iota(jnp.int32, masses.shape, 0) < counts[None]
    live_mass = jnp.where(live_slot, masses, jnp.float32(0.0))
    stacked = jnp.concatenate([positions, live_mass[None]], axis=0)
    padded = wrap_pad(extended(stacked, (("gx", 2), ("gy", 3)), 1), 4)
    block_size = min(8, slot_count)
    same_slot = lax.broadcasted_iota(
        jnp.int32, (block_size, slot_count, 1, 1, 1), 0
    ) + 0 == lax.broadcasted_iota(jnp.int32, (block_size, slot_count, 1, 1, 1), 1)
    running = jnp.zeros((block_size, size_x, size_y, size_z), jnp.float32)
    for offset in shift_list():
        source = padded[
            :,
            :,
            1 + offset[0] : 1 + offset[0] + size_x,
            1 + offset[1] : 1 + offset[1] + size_y,
            1 + offset[2] : 1 + offset[2] + size_z,
        ]
        squared = jnp.float32(SOFTENING * SOFTENING)
        for axis_id in range(3):
            separation = (
                source[axis_id][None] + jnp.float32(offset[axis_id]) - positions[axis_id][:, None]
            )
            squared = squared + separation * separation
        pair_terms = source[3][None] * lax.rsqrt(squared)
        if offset == (0, 0, 0):
            pair_terms = jnp.where(same_slot, jnp.float32(0.0), pair_terms)
        running = running + jnp.sum(pair_terms, axis=1)
    results = running
    running = results
    return jnp.where(live_slot, -running / slot_count, jnp.float32(0.0))


def general_device(
    leaf_multipoles, positions, masses, counts, up_operator, far_operator, down_operator
):
    potential = near_field(positions, masses, counts)
    kernel = assemble(far_operator)
    index_x = lax.axis_index("gx")
    index_y = lax.axis_index("gy")
    cells_x = leaf_multipoles.shape[1]
    cells_y = leaf_multipoles.shape[2]
    leaf_cells = jnp.transpose(leaf_multipoles, (1, 2, 3, 0))
    grouped_leaf = group_cells(leaf_cells)
    padded = wrap_pad(extended(grouped_leaf, (("gx", 0), ("gy", 1)), 1), 2)
    far_leaf = spread_cells(far_field(padded, kernel))
    grouped_six = group_cells(upward(up_operator, grouped_leaf))
    padded = wrap_pad(extended(grouped_six, (("gx", 0), ("gy", 1)), 1), 2)
    far_six = spread_cells(far_field(padded, kernel))
    moments_five = upward(up_operator, grouped_six)
    columns = lax.all_gather(moments_five, "gy", axis=1, tiled=True)
    whole_five = lax.all_gather(columns, "gx", axis=0, tiled=True)
    grouped_five = group_cells(whole_five)
    window_five = coarse_window(grouped_five, index_x, index_y, cells_x, cells_y, 3)
    moments_four = upward(up_operator, grouped_five)
    far_five = cut(
        spread_cells(far_field(window_five, kernel)), index_x, index_y, cells_x, cells_y, 2
    )
    grouped_four = group_cells(moments_four)
    window_four = coarse_window(grouped_four, index_x, index_y, cells_x, cells_y, 4)
    far_four = cut(
        spread_cells(far_field(window_four, kernel)), index_x, index_y, cells_x, cells_y, 3
    )
    grouped_three = group_cells(upward(up_operator, grouped_four))
    window_three = coarse_window(grouped_three, index_x, index_y, cells_x, cells_y, 5)
    far_three = cut(
        spread_cells(far_field(window_three, kernel)), index_x, index_y, cells_x, cells_y, 4
    )
    expansion = far_three
    expansion = far_four + cut(
        downward(down_operator, expansion), index_x, index_y, cells_x, cells_y, 3
    )
    expansion = far_five + cut(
        downward(down_operator, expansion), index_x, index_y, cells_x, cells_y, 2
    )
    expansion = far_six + cut(
        downward(down_operator, expansion), index_x, index_y, cells_x, cells_y, 1
    )
    expansion = far_leaf + cut(
        downward(down_operator, expansion), index_x, index_y, cells_x, cells_y, 0
    )
    return (jnp.transpose(expansion, (3, 0, 1, 2)), potential)


def solution(mesh):
    small = (mesh.shape["gx"], mesh.shape["gy"]) == (8, 4)
    return jax.shard_map(
        per_device if small else general_device,
        mesh=mesh,
        in_specs=(
            P(None, "gx", "gy", None),
            P(None, None, "gx", "gy", None),
            P(None, "gx", "gy", None),
            P("gx", "gy", None),
            P(),
            P(),
            P(),
        ),
        out_specs=(P(None, "gx", "gy", None), P(None, "gx", "gy", None)),
        check_vma=False,
    )
```

```python
import functools

import jax
import jax.numpy as jnp
import numpy as np
from jax import lax
from jax.experimental import pallas as pl
from jax.experimental.pallas import tpu as pltpu
from jax.sharding import PartitionSpec as P

SOFTENING = 0.05
EPS = SOFTENING * SOFTENING
F32 = jnp.float32
BF16 = jnp.bfloat16
COEF = 36
GROUP = 4 * COEF
Y_LEAF = 128 + 96
Y_SIX = Y_LEAF + 2 * GROUP
Y_FIVE = Y_SIX + GROUP // 2
Y_ROWS = Y_FIVE + 40
X_LEAF = 256 + 192
X_SIX = X_LEAF + 4 * GROUP
X_ROWS = X_SIX + GROUP
C_LEAF = 2 * 56
C_SIX = C_LEAF + 2 * GROUP
C_FIVE = C_SIX + GROUP
C_ROWS = C_FIVE + 80

VMEM = pl.BlockSpec(memory_space=pltpu.VMEM)
SMEM = pl.BlockSpec(memory_space=pltpu.SMEM)
HBM = pl.BlockSpec(memory_space=pltpu.MemorySpace.HBM)


def shape(dims, dtype):
    return jax.ShapeDtypeStruct(dims, dtype)


def kernel_call(body, outs, inputs, scratch=(), scalars=0, space=VMEM, target=VMEM, limit=20):
    return pl.pallas_call(
        body,
        out_shape=outs,
        in_specs=[SMEM] * scalars + [space] * (len(inputs) - scalars),
        out_specs=[target] * len(outs),
        scratch_shapes=list(scratch),
        compiler_params=pltpu.CompilerParams(vmem_limit_bytes=limit * 1024 * 1024),
    )(*inputs)


def iota(dims, axis):
    return lax.broadcasted_iota(jnp.int32, dims, axis)


def dot(lhs, rhs):
    return lax.dot_general(lhs, rhs, (((1,), (0,)), ((), ())), preferred_element_type=F32)


def dot_tn(lhs, rhs):
    return lax.dot_general(lhs, rhs, (((0,), (0,)), ((), ())), preferred_element_type=F32)


def dot_nt(lhs, rhs):
    return lax.dot_general(lhs, rhs, (((1,), (1,)), ((), ())), preferred_element_type=F32)


def one_hot(mask):
    return jnp.where(mask, F32(1.0), F32(0.0)).astype(BF16)


def pick(rows, source):
    return one_hot(iota((rows, source.shape[1]), 0) == source)


def parts(value):
    high = value.astype(BF16)
    return high, (value - high.astype(F32)).astype(BF16)


def lane_roll(value, shift):
    return pltpu.roll(value, shift % 128, 1) if shift % 128 else value


def up_blocks(up_ref):
    col = iota((1, GROUP), 1)
    block = jnp.where(col < 2 * COEF, jnp.where(col < COEF, 0, 1), jnp.where(col < 3 * COEF, 2, 3))
    return [
        dot(up_ref[...], pick(8 * COEF, col + (block + bit) * COEF)).astype(BF16) for bit in range(2)
    ]


def prep_kernel(
    leaf_hbm, pos_hbm, mass_hbm, count_hbm, up_hbm,
    grid_ref, up_msg, down_msg, low_msg, high_msg, six_ref, five_ref, live_ref,
    pos_ref, count_ref, halves_ref,
    up_ref, leaf_ref, mass_ref, m32, x32, six32, near32, sems,
):
    copies = [
        pltpu.make_async_copy(source, target, sems.at[k])
        for k, (source, target) in enumerate(
            (
                (leaf_hbm, leaf_ref), (pos_hbm, pos_ref), (mass_hbm, mass_ref),
                (count_hbm, count_ref), (up_hbm, up_ref),
            )
        )
    ]
    for copy in copies:
        copy.start()
    copies[0].wait()
    m32[0:1152, :] = leaf_ref[...].astype(F32)
    for x in range(4):
        for y in range(8):
            start = ((x // 2) * 4 + y // 2) * GROUP + (2 * (x % 2) + y % 2) * COEF
            x32[start : start + COEF, :] = m32[pl.ds(x * 8 + y, COEF, stride=32), :]
    grid = x32[0:1152, :].astype(BF16)
    grid_ref[...] = grid
    for msg, parent in ((up_msg, 3), (down_msg, 0)):
        for xp in range(2):
            msg[Y_LEAF + xp * GROUP : Y_LEAF + (xp + 1) * GROUP, :] = grid_ref[
                (xp * 4 + parent) * GROUP : (xp * 4 + parent + 1) * GROUP, :
            ]
    low_msg[X_LEAF:X_SIX, :] = grid_ref[0 : 4 * GROUP, :]
    high_msg[X_LEAF:X_SIX, :] = grid_ref[4 * GROUP : 8 * GROUP, :]
    for copy in copies[1:]:
        copy.wait()
    count = count_ref[...]
    for slot in range(8):
        live_ref[slot * 32 : slot * 32 + 32, :] = jnp.where(
            count > slot, mass_ref[slot * 32 : slot * 32 + 32, :], F32(0.0)
        )
    for msg, y in ((up_msg, 7), (down_msg, 0)):
        rows = []
        for x in range(4):
            rows.append(pos_ref[pl.ds(x * 8 + y, 24, stride=32), :])
            rows.append(live_ref[pl.ds(x * 8 + y, 8, stride=32), :])
        high, low = parts(jnp.concatenate(rows, axis=0))
        msg[0:128, :] = high
        for x in range(4):
            msg[128 + 24 * x : 152 + 24 * x, :] = low[32 * x : 32 * x + 24]
    for msg, x in ((low_msg, 0), (high_msg, 3)):
        for slot in range(8):
            for axis in range(3):
                start = (axis * 8 + slot) * 32 + x * 8
                near32[pl.ds(axis * 8 + slot, 8, stride=32), :] = pos_ref[start : start + 8, :]
            start = slot * 32 + x * 8
            near32[pl.ds(24 + slot, 8, stride=32), :] = live_ref[start : start + 8, :]
        high, low = parts(near32[...])
        msg[0:256, :] = high
        for y in range(8):
            msg[256 + 24 * y : 280 + 24 * y, :] = low[32 * y : 32 * y + 24]
    low_half = iota((COEF, 128), 1) < 64
    even_up, odd_up = up_blocks(up_ref)
    halves_ref[0], halves_ref[1] = even_up, odd_up
    col = iota((1, 128), 1)
    split_z = pick(128, 2 * (col % 64) + col // 64)
    split = dot(grid, split_z).astype(BF16)
    columns = jnp.concatenate([split[k * GROUP : (k + 1) * GROUP] for k in range(8)], axis=1)
    even, odd = dot(even_up, columns), dot(odd_up, columns)
    for xp in range(2):
        for y in range(2):
            first, second = (xp * 4 + y) * 128, (xp * 4 + 2 + y) * 128
            near_part = even[:, first : first + 128] + lane_roll(odd[:, first : first + 128], 64)
            far_part = lane_roll(even[:, second : second + 128], 64) + odd[:, second : second + 128]
            start = (2 * xp + y) * COEF
            six32[start : start + COEF, :] = jnp.where(low_half, near_part, far_part)
    six = six32[0:GROUP, :].astype(BF16)
    six_ref[...] = six
    low_msg[X_SIX:X_ROWS, :] = six
    high_msg[X_SIX:X_ROWS, :] = six
    left = iota((72, 128), 1) < 64
    first, second = six32[0:72, :], six32[72:144, :]
    up_msg[Y_SIX:Y_FIVE, :] = jnp.where(left, lane_roll(first, 64), second).astype(BF16)
    down_msg[Y_SIX:Y_FIVE, :] = jnp.where(left, first, lane_roll(second, 64)).astype(BF16)
    split_six = pick(128, ((col // 32) % 2) * 64 + 2 * (col % 32) + col // 64)
    split = dot(six, split_six).astype(BF16)
    five = dot(even_up, split) + lane_roll(dot(odd_up, split), 64)
    five = jnp.concatenate([five, jnp.zeros((4, 128), F32)], axis=0).astype(BF16)
    five_ref[...] = five
    for msg in (up_msg, down_msg):
        msg[Y_FIVE:Y_ROWS, :] = five


def in_hbm(value):
    return pltpu.with_memory_space_constraint(value, pltpu.MemorySpace.HBM)


def prepare(leaf, positions, masses, counts, up_operator):
    inputs = (leaf, positions, masses, counts, up_operator)
    return kernel_call(
        prep_kernel,
        (
            shape((8 * GROUP, 128), BF16),
            shape((Y_ROWS, 128), BF16),
            shape((Y_ROWS, 128), BF16),
            shape((X_ROWS, 128), BF16),
            shape((X_ROWS, 128), BF16),
            shape((GROUP, 128), BF16),
            shape((40, 128), BF16),
            shape((256, 128), F32),
            shape((768, 128), F32),
            shape((32, 128), jnp.int32),
            shape((2, COEF, GROUP), BF16),
        ),
        [in_hbm(value) for value in inputs],
        (
            pltpu.VMEM(up_operator.shape, BF16),
            pltpu.VMEM((1152, 128), BF16),
            pltpu.VMEM((256, 128), F32),
            pltpu.VMEM((1280, 128), F32),
            pltpu.VMEM((1160, 128), F32),
            pltpu.VMEM((GROUP + 8, 128), F32),
            pltpu.VMEM((256, 128), F32),
            pltpu.SemaphoreType.DMA((5,)),
        ),
        space=HBM,
    )


def halo_six(below, above):
    upper, lower = above[Y_SIX:Y_FIVE, :].astype(F32), below[Y_SIX:Y_FIVE, :].astype(F32)
    left = iota((72, 128), 1) < 64
    return jnp.concatenate(
        [
            jnp.where(left, upper, lane_roll(lower, 64)),
            jnp.where(left, lane_roll(upper, 64), lower),
        ],
        axis=0,
    )


def cross_kernel(place, below, above, two, own, to_low, to_high, five32):
    lane = iota((COEF, 128), 1) // 32
    five32[...] = jnp.zeros_like(five32)
    for shift, ref, first in ((0, own, 0), (3, below, Y_FIVE), (1, above, Y_FIVE), (2, two, 0)):
        at = lax.rem(place[1] + shift, 4)
        value = ref[first : first + 40, :].astype(F32)
        for y in range(2):
            moved = pltpu.roll(value, lax.rem(32 * at + 96 * y, 128), 1)[0:COEF]
            rows = slice(y * COEF, (y + 1) * COEF)
            five32[rows, :] = jnp.where(lane == at, moved, five32[rows, :])
    five = five32[...].astype(BF16)
    halo = halo_six(below, above).astype(BF16)
    for msg, x, xp in ((to_low, 0, 0), (to_high, 3, 1)):
        for side, ref in enumerate((below, above)):
            first = side * 56
            msg[first : first + 32, :] = ref[32 * x : 32 * x + 32, :]
            msg[first + 32 : first + 56, :] = ref[128 + 24 * x : 152 + 24 * x, :]
            source, first = Y_LEAF + xp * GROUP, C_LEAF + side * GROUP
            msg[first : first + GROUP, :] = ref[source : source + GROUP, :]
        msg[C_SIX:C_FIVE, :] = halo
        msg[C_FIVE:C_ROWS, :] = five


def cross(*inputs):
    return kernel_call(
        cross_kernel,
        (shape((C_ROWS, 128), BF16), shape((C_ROWS, 128), BF16)),
        inputs,
        (pltpu.VMEM((80, 128), F32),),
        scalars=1,
    )


def inverse_distance(target, source):
    squared = F32(EPS)
    for axis in range(3):
        separation = source[axis] - target[axis]
        squared = squared + separation * separation
    return lax.rsqrt(squared)


def pair_sums(shifted, sums, goals, x, step, totals):
    step_x, step_y, step_z = step
    edge = iota((8, 128), 0) == (7 if step_y > 0 else 0)
    for slot in range(8):
        source = [shifted[step_z + 1, k, slot, x] for k in range(4)]
        if step_y:
            source = [pltpu.roll(value, (-step_y) % 8, 0) for value in source]
            source[1] = source[1] + F32(step_y)
            source[3] = jnp.where(edge, F32(0.0), source[3])
        if step_x:
            source[0] = source[0] + F32(step_x)
        back = None
        for goal in range(8):
            inverse = inverse_distance(goals[goal], source)
            totals[goal] = totals[goal] + source[3] * inverse
            term = goals[goal][3] * inverse
            back = term if back is None else back + term
        if step_y:
            back = pltpu.roll(jnp.where(edge, F32(0.0), back), step_y % 8, 0)
        sums[step_z + 1, slot, x] = sums[step_z + 1, slot, x] + back


def plane_goals(shifted, x):
    return [[shifted[1, k, slot, x] for k in range(4)] for slot in range(8)]


def step_pairs(shifted, sums, x):
    for step_y in (-1, 0, 1):
        goals = plane_goals(shifted, x)
        totals = [sums[1, slot, x] for slot in range(8)]
        for step_z in (-1, 0, 1):
            pair_sums(shifted, sums, goals, x + 1, (1, step_y, step_z), totals)
        for slot in range(8):
            sums[1, slot, x] = totals[slot]


def plane_kernel(pos_ref, live_ref, far_hbm, down_hbm, sums, shifted, far_ref, down_ref, sems):
    copies = [
        pltpu.make_async_copy(source, target, sems.at[k])
        for k, (source, target) in enumerate(((far_hbm, far_ref), (down_hbm, down_ref)))
    ]
    for copy in copies:
        copy.start()
    sums[...] = jnp.zeros_like(sums)

    def plane(x, carry):
        for slot in range(8):
            values = [pos_ref[axis, slot, x] for axis in range(3)] + [live_ref[slot, x]]
            for index, step in enumerate((-1, 0, 1)):
                moved = [lane_roll(value, -step) for value in values]
                if step:
                    moved[2] = moved[2] + F32(step)
                for k in range(4):
                    shifted[index, k, slot, x] = moved[k]
        goals = plane_goals(shifted, x)
        totals = [jnp.zeros((8, 128), F32) for slot in range(8)]
        for slot in range(8):
            for goal in range(slot):
                inverse = inverse_distance(goals[goal], goals[slot])
                totals[goal] = totals[goal] + goals[slot][3] * inverse
                totals[slot] = totals[slot] + goals[goal][3] * inverse
        for step in ((0, 0, 1), (0, 1, -1), (0, 1, 0), (0, 1, 1)):
            pair_sums(shifted, sums, goals, x, step, totals)
        for slot in range(8):
            sums[1, slot, x] = sums[1, slot, x] + totals[slot]
        return carry

    lax.fori_loop(0, 4, plane, 0)

    def step(x, carry):
        step_pairs(shifted, sums, x)
        return carry

    lax.fori_loop(0, 2, step, 0)
    for copy in copies:
        copy.wait()


def plane_pairs(positions, live, far_operator, down_operator):
    return pl.pallas_call(
        plane_kernel,
        out_shape=(
            shape((3, 8, 4, 8, 128), F32),
            shape((3, 4, 8, 4, 8, 128), F32),
            shape(far_operator.shape, BF16),
            shape(down_operator.shape, BF16),
        ),
        in_specs=[VMEM, VMEM, HBM, HBM],
        out_specs=[VMEM] * 4,
        scratch_shapes=[pltpu.SemaphoreType.DMA((2,))],
        compiler_params=pltpu.CompilerParams(vmem_limit_bytes=16 * 1024 * 1024),
    )(positions, live, in_hbm(far_operator), in_hbm(down_operator))


def joined(target, msg, high, low, count):
    for cell in range(count):
        first = 32 * cell
        whole = msg[high + first : high + first + 32, :].astype(F32)
        rest = msg[low + 24 * cell : low + 24 * cell + 24, :].astype(F32)
        target[first : first + 24, :] = whole[0:24] + rest
        target[first + 24 : first + 32, :] = whole[24:32]


def add_sources(fetch, shifted, goals, totals):
    for slot in range(8):
        values = [fetch(k, slot) for k in range(4)]
        for step in (-1, 0, 1):
            moved = [lane_roll(value, -step) for value in values]
            if step:
                moved[2] = moved[2] + F32(step)
            for k in range(4):
                shifted[step + 1, k, slot] = moved[k]
    totals = list(totals)
    for step in range(3):
        for slot in range(8):
            source = [shifted[step, k, slot] for k in range(4)]
            for goal in range(8):
                totals[goal] = totals[goal] + source[3] * inverse_distance(goals[goal], source)
    return tuple(totals)


def rows_kernel(
    inner_ref, pos_ref, count_ref, below, above, low_corner, high_corner, out_ref,
    sources, shifted, added, places,
):
    turn = jnp.where(iota((8, 128), 0) >= 4, F32(1.0), F32(-1.0))
    for side, msg in enumerate((below, above)):
        first = side * 128
        joined(sources.at[1, pl.ds(first, 128)], msg, 0, 128, 4)
        high = side * 56
        joined(sources.at[0, pl.ds(first, 32)], low_corner, high, high + 32, 1)
        sources[0, first + 32 : first + 128, :] = sources[1, first : first + 96, :]
        sources[2, first : first + 96, :] = sources[1, first + 32 : first + 128, :]
        joined(sources.at[2, pl.ds(first + 96, 32)], high_corner, high, high + 32, 1)
    places[0:768, :] = pos_ref[...]
    goals = []
    for slot in range(8):
        at = [(axis * 8 + slot) * 32 for axis in range(3)]
        goals.append(
            [
                jnp.concatenate(
                    [places[pl.ds(a, 4, stride=8), :], places[pl.ds(a + 7, 4, stride=8), :]], axis=0
                )
                for a in at
            ]
        )

    def body(step_x, totals):
        def fetch(k, slot):
            value = sources[step_x, pl.ds(8 * k + slot, 8, stride=32), :]
            if k == 0:
                value = value + (step_x - 1).astype(F32)
            return value + turn if k == 1 else value

        return add_sources(fetch, shifted, goals, totals)

    totals = lax.fori_loop(0, 3, body, tuple(jnp.zeros((8, 128), F32) for slot in range(8)))
    added[...] = jnp.zeros_like(added)
    for slot in range(8):
        added[pl.ds(slot * 32, 4, stride=8), :] = totals[slot][0:4]
        added[pl.ds(slot * 32 + 7, 4, stride=8), :] = totals[slot][4:8]
    count = count_ref[...]
    for slot in range(8):
        rows = slice(slot * 32, slot * 32 + 32)
        total = inner_ref[rows, :] + added[rows, :]
        out_ref[rows, :] = jnp.where(count > slot, -total / 8, F32(0.0))


def faces_kernel(sums_ref, shifted_ref, pos_ref, low, high, out_ref, sides, shifted, sums):
    sums[...] = sums_ref[...]
    step_pairs(shifted_ref, sums, 2)
    for x in range(4):
        for slot in range(8):
            out_ref[slot, x] = (
                sums[1, slot, x] + lane_roll(sums[0, slot, x], -1) + lane_roll(sums[2, slot, x], 1)
            )
    sides[...] = jnp.zeros_like(sides)
    for index, msg in enumerate((low, high)):
        joined(sides.at[index, pl.ds(32, 256)], msg, 0, 256, 8)

    def face(index, carry):
        x = 3 * index
        goals = [[pos_ref[axis, slot, x] for axis in range(3)] for slot in range(8)]

        def body(step_y, totals):
            def fetch(k, slot):
                value = sides[index, pl.ds(step_y * 32 + 8 * k + slot, 8, stride=32), :]
                if k == 0:
                    value = value + (2 * index - 1).astype(F32)
                return value + (step_y - 1).astype(F32) if k == 1 else value

            return add_sources(fetch, shifted, goals, totals)

        totals = lax.fori_loop(0, 3, body, tuple(out_ref[slot, x] for slot in range(8)))
        for slot in range(8):
            out_ref[slot, x] = totals[slot]
        return carry

    lax.fori_loop(0, 2, face, 0)


def row_pairs(*inputs):
    return kernel_call(
        rows_kernel,
        (shape((256, 128), F32),),
        inputs,
        (
            pltpu.VMEM((3, 256, 128), F32),
            pltpu.VMEM((3, 4, 8, 8, 128), F32),
            pltpu.VMEM((320, 128), F32),
            pltpu.VMEM((832, 128), F32),
        ),
    )[0]


def face_pairs(*inputs):
    return kernel_call(
        faces_kernel,
        (shape((8, 4, 8, 128), F32),),
        inputs,
        (
            pltpu.VMEM((2, 320, 128), F32),
            pltpu.VMEM((3, 4, 8, 8, 128), F32),
            pltpu.VMEM((3, 8, 4, 8, 128), F32),
        ),
    )[0]


def far_starts():
    starts, count = {}, 0
    for step_x in range(-3, 4):
        for step_y in range(-3, 4):
            starts[step_x, step_y] = count * COEF
            count += 7 if max(abs(step_x), abs(step_y)) >= 2 else 4
    return starts


def operator_kernel(far_ref, out_ref, far32, stack):
    far32[0:COEF, 0:11264] = far_ref[:, 0:11264].astype(F32)
    far32[:, 11264:11520] = jnp.zeros((40, 256), F32)
    far32[0:COEF, 11264:11376] = far_ref[:, 11264:11376].astype(F32)
    lane = iota((COEF, 256), 1)

    def window(start):
        base = start // 128 * 128
        value = far32[0:COEF, base : base + 384]
        shift = start - base
        return (pltpu.roll(value, 384 - shift, 1) if shift else value)[:, 0:256]

    starts = far_starts()
    for step_x in range(-3, 4):
        for step_y in range(-3, 4):
            start = starts[step_x, step_y]
            if max(abs(step_x), abs(step_y)) >= 2:
                block = jnp.where(lane < 7 * COEF, window(start), F32(0.0))
            else:
                block = jnp.where(
                    lane < 2 * COEF,
                    window(start),
                    jnp.where(
                        (lane >= 5 * COEF) & (lane < 7 * COEF), window(start - 3 * COEF), F32(0.0)
                    ),
                )
            for bit_x in range(2):
                for bit_y in range(2):
                    source_x, source_y = step_x + bit_x, step_y + bit_y
                    if -2 <= source_x <= 3 and -2 <= source_y <= 3:
                        shift_x, child_x = source_x // 2 + 1, source_x % 2
                        shift_y, child_y = source_y // 2 + 1, source_y % 2
                        first = shift_y * GROUP + (2 * child_x + child_y) * COEF
                        bits = (2 * bit_x + bit_y) * 256
                        stack[shift_x, first : first + COEF, bits : bits + 256] = block
    out_ref[...] = stack[:, 0 : 3 * GROUP, :].astype(BF16)


def far_matrix(far_operator):
    return kernel_call(
        operator_kernel,
        (shape((3, 3 * GROUP, 1024), BF16),),
        (far_operator,),
        (pltpu.VMEM((40, 11520), F32), pltpu.VMEM((3, 3 * GROUP + 8, 1024), F32)),
    )[0]


def z_sum(products, bits, lanes, first):
    odd = iota((COEF, 128), 1) % 2 != first
    total = None
    for step in range(-3, 4):
        start = bits * 256 + (step + 3) * COEF
        value = lane_roll(products[start : start + COEF, lanes], -step)
        if step == 3:
            value = jnp.where(odd, F32(0.0), value)
        if step == -3:
            value = jnp.where(odd, value, F32(0.0))
        total = value if total is None else total + value
    return total


def multiply(matrix, rows, sources):
    total = None
    for shift_x, source in enumerate(sources):
        term = dot_tn(matrix[shift_x, :, rows], source)
        total = term if total is None else total + term
    return total


def windows_x(cells, parent):
    rows = slice(parent * GROUP, (parent + 3) * GROUP)
    return [cells[rows, shift_x * 128 : shift_x * 128 + 256] for shift_x in range(3)]


def middle_kernel(matrix, grid_ref, low, high, products, cells):
    cells[:, 0:128] = low[X_LEAF:X_SIX, :]
    cells[:, 128:256] = grid_ref[0 : 4 * GROUP, :]
    cells[:, 256:384] = grid_ref[4 * GROUP : 8 * GROUP, :]
    cells[:, 384:512] = high[X_LEAF:X_SIX, :]
    for parent in range(2):
        products[parent] = multiply(matrix, slice(0, 1024), windows_x(cells, parent))


def middle_products(*inputs):
    return kernel_call(
        middle_kernel,
        (shape((2, 1024, 256), F32),),
        inputs,
        (pltpu.VMEM((4 * GROUP, 512), BF16),),
    )[0]


def levels_kernel(
    place, matrix, middle, grid_ref, six_ref, below, above, low, high, low_corner, high_corner,
    near_three, up_three, down_three, halves_ref, down_ref, out_ref,
    cells, fives, fours, three32, windows, products, coarse, down32, downs, expand, lifted,
    leaving, sems,
):
    gx, gy = place[0], place[1]
    col = iota((1, 128), 1)

    for first, msg, corner in ((0, low, low_corner), (384, high, high_corner)):
        lanes = slice(first, first + 128)
        cells[0:GROUP, lanes] = corner[C_LEAF : C_LEAF + GROUP, :]
        cells[GROUP : 5 * GROUP, lanes] = msg[X_LEAF:X_SIX, :]
        cells[5 * GROUP : 6 * GROUP, lanes] = corner[C_LEAF + GROUP : C_SIX, :]
    for xp in range(2):
        lanes = slice(128 + 128 * xp, 256 + 128 * xp)
        source = Y_LEAF + xp * GROUP
        cells[0:GROUP, lanes] = below[source : source + GROUP, :]
        cells[GROUP : 5 * GROUP, lanes] = grid_ref[xp * 4 * GROUP : (xp + 1) * 4 * GROUP, :]
        cells[5 * GROUP : 6 * GROUP, lanes] = above[source : source + GROUP, :]

    todo = [(side, half) for side in range(2) for half in range(2)]

    def leaf_products(count=1):
        for side, half in todo[:count]:
            rows = slice(half * 512, half * 512 + 512)
            products[side + 1, rows, :] = multiply(matrix, rows, windows_x(cells, 3 * side))
        del todo[:count]

    size = fives.shape[0] // 72
    for shift, msg, first in (
        (-1, near_three, 0), (0, near_three, 80), (1, near_three, 160),
        (-4, up_three, 0), (-3, up_three, 80), (-2, up_three, 160),
        (2, down_three, 0), (3, down_three, 80), (4, down_three, 160),
    ):
        at = pl.multiple_of(lax.rem(gx + shift + size, size) * 72, 8)
        fives[pl.ds(at, 72), :] = msg[first : first + 72, :].astype(F32)
    even_up, odd_up = halves_ref[0], halves_ref[1]
    leaf_products()

    def upward(grouped, split):
        children = dot(grouped.astype(BF16), split).astype(BF16)
        value = dot(even_up, children) + lane_roll(dot(odd_up, children), 64)
        return value.astype(BF16).astype(F32)

    lane = col % 64
    split_five = pick(
        128, ((lane // 16 % 2) * 2 + lane // 32) * 32 + 2 * (lane % 16) + col // 64
    )
    for x in range(4):
        value = upward(fives[x * GROUP : (x + 1) * GROUP, :], split_five)
        first = (x // 2) * GROUP + (x % 2) * 2 * COEF
        fours[first : first + COEF, :] = value
        fours[first + COEF : first + 2 * COEF, :] = lane_roll(value, 96)
    leaf_products()
    split_four = pick(
        128, jnp.where(lane < 16, (lane // 8) * 16 + 2 * (lane % 8) + col // 64, -1)
    )
    for x in range(2):
        value = upward(fours[x * GROUP : (x + 1) * GROUP, :], split_four)
        three32[x * 2 * COEF : x * 2 * COEF + COEF, :] = value
        three32[x * 2 * COEF + COEF : (x + 1) * 2 * COEF, :] = lane_roll(value, 120)
    leaf_products()
    def wrapped(first, base, size):
        cell = (col - first - 3 + size) & (size - 1)
        return pick(128, jnp.where((col >= first) & (col < first + size + 6), base + cell, -1))

    three = dot(three32[0:GROUP, :].astype(BF16), wrapped(92, 0, 8))
    six_lanes = [wrapped(0, 0, 64), wrapped(0, 64, 64)]
    five_lanes = [wrapped(70, lax.rem(gy + step + 3, 4) * 32, 32) for step in range(3)]
    four_lanes = [wrapped(70, lax.rem(gy // 2 + step + 1, 2) * 16, 16) for step in range(3)]
    for shift_x in range(3):
        if shift_x == 1:
            own, other = six_ref[...], halo_six(below, above).astype(BF16)
        else:
            own = (low if shift_x == 0 else high)[X_SIX:X_ROWS, :]
            other = (low_corner if shift_x == 0 else high_corner)[C_SIX:C_FIVE, :]
        at = pl.multiple_of(lax.rem(gx // 2 + shift_x + 3, 4) * GROUP, 8)
        five = fives[pl.ds(at, GROUP), :].astype(BF16)
        at = pl.multiple_of(lax.rem(gx // 4 + shift_x + 1, 2) * GROUP, 8)
        four = fours[pl.ds(at, GROUP), :].astype(BF16)
        for shift_y in range(3):
            left = dot(other if shift_y == 0 else own, six_lanes[0 if shift_y == 1 else 1])
            right = dot(other if shift_y == 2 else own, six_lanes[1 if shift_y == 1 else 0])
            left = left + dot(five, five_lanes[shift_y])
            right = right + dot(four, four_lanes[shift_y]) + three
            rows = slice(shift_y * GROUP, (shift_y + 1) * GROUP)
            windows[shift_x, rows, 0:128] = left.astype(BF16)
            windows[shift_x, rows, 128:256] = right.astype(BF16)
    for half in range(2):
        rows = slice(half * 512, half * 512 + 512)
        products[0, rows, :] = multiply(matrix, rows, [windows[shift_x] for shift_x in range(3)])
    leaf_products()
    coarse[...] = jnp.zeros_like(coarse)
    for bits in range(4):
        for lanes in (slice(0, 128), slice(128, 256)):
            coarse[bits * 40 : bits * 40 + COEF, lanes] = z_sum(products.at[0], bits, lanes, 1)
    eye = pick(8 * COEF, iota((1, 8 * COEF), 1))
    down32[0 : 8 * COEF, :] = dot_nt(eye, down_ref[...])
    downs[...] = jnp.zeros_like(downs)
    for bits in range(4):
        for bit in range(2):
            first = (2 * bits + bit) * COEF
            downs[bit, bits * 40 : bits * 40 + COEF, :] = down32[first : first + COEF, :]
    operators = [downs[bit].astype(BF16) for bit in range(2)]

    def spread(value, first, start, count):
        inside = (col >= start) & (col < start + count)
        taken = pick(128, jnp.where(inside, first + (col - start) // 2, -1))
        return [dot(part, taken).astype(BF16) for part in parts(value)]

    def lift(wide, lanes, first):
        halves = [dot(value, wide[0]) + dot(value, wide[1]) for value in operators]
        even = iota(halves[0].shape, 1) % 2 == first
        lifted[:, lanes] = jnp.where(even, halves[0], halves[1])

    def block(bits):
        return pl.ds(bits * 40 if isinstance(bits, int) else pl.multiple_of(bits * 40, 8), COEF)

    left, right, both = slice(0, 128), slice(128, 256), slice(0, 256)
    bits = 2 * lax.rem(gx // 4, 2) + lax.rem(gy // 2, 2)
    value = coarse[block(bits), right]
    wide = spread(value, 95, 73, 16)
    lift(wide, left, 1)
    leaf_products()
    bits = 2 * lax.rem(gx // 2, 2) + lax.rem(gy, 2)
    value = coarse[block(bits), right] + lifted[block(bits), left]
    wide = spread(value, 73, 73, 32)
    lift(wide, left, 1)
    leaf_products()
    wides = []
    for y in range(2):
        bits = 2 * lax.rem(gx, 2) + y
        value = coarse[block(bits), left] + lifted[block(bits), left]
        wides.append(spread(value, 73, 3, 64))
    lift([jnp.concatenate(pair, axis=1) for pair in zip(*wides)], both, 1)
    leaf_products()
    doubled = pick(128, 3 + col // 2)
    for k, part in enumerate(parts(coarse[...] + lifted[:, both])):
        for y in range(2):
            wide = dot(part[:, y * 128 : y * 128 + 128], doubled)
            for bits in range(4):
                at = ((bits // 2) * 4 + 2 * y + bits % 2) * 128
                expand[k, 0:COEF, at : at + 128] = wide[bits * 40 : bits * 40 + COEF].astype(BF16)
    leaf_products(8)
    lift([expand[k, 0:COEF, :] for k in range(2)], slice(0, 1024), 0)
    copies = []
    for x in range(4):
        xp = x // 2
        for y in range(8):
            parent, bits = y // 2, 2 * (x % 2) + y % 2
            source = middle.at[parent - 1] if parent in (1, 2) else products.at[1 + parent // 3]
            value = z_sum(source, bits, slice(xp * 128, xp * 128 + 128), 0)
            at = (xp * 4 + parent) * 128
            leaving[x, pl.ds(y, COEF, stride=8), :] = value + lifted[block(bits), at : at + 128]
        copies.append(
            pltpu.make_async_copy(
                leaving.at[x, pl.ds(0, 8 * COEF)].reshape(COEF, 8, 128), out_ref.at[:, x], sems.at[x]
            )
        )
        copies[-1].start()
    for copy in copies:
        copy.wait()


def all_levels(*inputs):
    return kernel_call(
        levels_kernel,
        (shape((COEF, 4, 8, 128), F32),),
        inputs,
        (
            pltpu.VMEM((6 * GROUP, 512), BF16),
            pltpu.VMEM((576, 128), F32),
            pltpu.VMEM((2 * GROUP + 8, 128), F32),
            pltpu.VMEM((GROUP + 8, 128), F32),
            pltpu.VMEM((3, 3 * GROUP, 256), BF16),
            pltpu.VMEM((3, 1024, 256), F32),
            pltpu.VMEM((160, 256), F32),
            pltpu.VMEM((8 * COEF + 8, COEF), F32),
            pltpu.VMEM((2, 160, COEF), F32),
            pltpu.VMEM((2, 40, 1024), BF16),
            pltpu.VMEM((160, 1024), F32),
            pltpu.VMEM((4, 8 * COEF + 32, 128), F32),
            pltpu.SemaphoreType.DMA((4,)),
        ),
        scalars=1,
        target=HBM,
    )[0]


def moved(value, step_x, step_y):
    size_x, size_y = lax.axis_size("gx"), lax.axis_size("gy")
    table = [
        (x * size_y + y, (x + step_x) % size_x * size_y + (y + step_y) % size_y)
        for x in range(size_x)
        for y in range(size_y)
    ]
    return lax.ppermute(value, ("gx", "gy"), table)


def per_device(
    leaf_multipoles, positions, masses, counts, up_operator, far_operator, down_operator
):
    place = jnp.stack([lax.axis_index("gx"), lax.axis_index("gy")]).astype(jnp.int32)
    (
        grid, up_msg, down_msg, low_msg, high_msg, six, five, live,
        positions, counts, up_halves,
    ) = prepare(
        leaf_multipoles.reshape(1152, 128), positions.reshape(768, 128), masses.reshape(256, 128),
        counts.reshape(32, 128), up_operator.T,
    )
    positions = positions.reshape(3, 8, 4, 8, 128)
    below, above, two = moved(up_msg, 0, 1), moved(down_msg, 0, -1), moved(five, 0, 2)
    low, high = moved(high_msg, 1, 0), moved(low_msg, -1, 0)
    inner, shifted, far_operator, down_operator = plane_pairs(
        positions, live.reshape(8, 4, 8, 128), far_operator, down_operator
    )
    matrix = far_matrix(far_operator)
    below, above, two, inner, matrix = lax.optimization_barrier((below, above, two, inner, matrix))
    to_low, to_high = cross(place, below, above, two, five)
    low_corner, high_corner = moved(to_high, 1, 0), moved(to_low, -1, 0)
    inner = face_pairs(inner, shifted, positions, low, high)
    low_corner, high_corner, inner = lax.optimization_barrier((low_corner, high_corner, inner))
    three = jnp.concatenate([low_corner[C_FIVE:], to_low[C_FIVE:], high_corner[C_FIVE:]], axis=0)
    up_three, down_three = moved(three, 3, 0), moved(three, -3, 0)
    potential = row_pairs(
        inner.reshape(256, 128), positions.reshape(768, 128), counts, below, above, low_corner,
        high_corner,
    )
    middle = middle_products(lax.optimization_barrier((matrix, low_corner))[0], grid, low, high)
    up_three, down_three, potential, middle = lax.optimization_barrier(
        (up_three, down_three, potential, middle)
    )
    expansion = all_levels(
        place, matrix, middle, grid, six, below, above, low, high, low_corner, high_corner,
        three, up_three, down_three, up_halves, down_operator,
    )
    return expansion, potential.reshape(8, 4, 8, 128)


def extended(cells, sides, width):
    for axis, dim in sides:
        count = lax.axis_size(axis)
        head = lax.slice_in_dim(cells, 0, width, axis=dim)
        tail = lax.slice_in_dim(cells, cells.shape[dim] - width, cells.shape[dim], axis=dim)
        cells = jnp.concatenate(
            [
                lax.ppermute(tail, axis, [(i, (i + 1) % count) for i in range(count)]),
                cells,
                lax.ppermute(head, axis, [((i + 1) % count, i) for i in range(count)]),
            ],
            axis=dim,
        )
    return cells


def shift_list():
    return [
        (step_x, step_y, step_z)
        for step_x in (-1, 0, 1)
        for step_y in (-1, 0, 1)
        for step_z in (-1, 0, 1)
    ]


def child_bits(number):
    return (number // 4, number // 2 % 2, number % 2)


def offset_table():
    vectors = [
        (step_x, step_y, step_z)
        for step_x in range(-3, 4)
        for step_y in range(-3, 4)
        for step_z in range(-3, 4)
        if max(abs(step_x), abs(step_y), abs(step_z)) >= 2
    ]
    lookup = np.full((27, 8, 8), len(vectors), dtype=np.int32)
    for shift_id, offset in enumerate(shift_list()):
        for source in range(8):
            for target in range(8):
                vector = tuple(
                    (
                        2 * offset[axis_id]
                        + child_bits(source)[axis_id]
                        - child_bits(target)[axis_id]
                        for axis_id in range(3)
                    )
                )
                if max(abs(vector[0]), abs(vector[1]), abs(vector[2])) >= 2:
                    lookup[shift_id, source, target] = vectors.index(vector)
    return lookup


def assemble(far_operator):
    coeff_count = far_operator.shape[0]
    blocks = far_operator.reshape(coeff_count, -1, coeff_count)
    blocks = jnp.concatenate(
        [blocks, jnp.zeros((coeff_count, 1, coeff_count), blocks.dtype)], axis=1
    )
    picked = jnp.take(blocks, jnp.asarray(offset_table().reshape(-1), dtype=jnp.int32), axis=1)
    picked = picked.reshape(coeff_count, 27, 8, 8, coeff_count).transpose(1, 2, 0, 3, 4)
    return picked.reshape(27, 8 * coeff_count, 8 * coeff_count)


def group_cells(volume):
    size_x, size_y, size_z, coeff_count = volume.shape
    reshaped = volume.reshape(size_x // 2, 2, size_y // 2, 2, size_z // 2, 2, coeff_count)
    return reshaped.transpose(0, 2, 4, 1, 3, 5, 6).reshape(
        size_x // 2, size_y // 2, size_z // 2, 8 * coeff_count
    )


def spread_cells(grouped):
    size_x, size_y, size_z, total_rows = grouped.shape
    coeff_count = total_rows // 8
    reshaped = grouped.reshape(size_x, size_y, size_z, 2, 2, 2, coeff_count)
    return reshaped.transpose(0, 3, 1, 4, 2, 5, 6).reshape(
        2 * size_x, 2 * size_y, 2 * size_z, coeff_count
    )


def wrap_pad(volume, axis_id):
    extent = volume.shape[axis_id]
    lower = lax.slice_in_dim(volume, extent - 1, extent, axis=axis_id)
    upper = lax.slice_in_dim(volume, 0, 1, axis=axis_id)
    return jnp.concatenate([lower, volume, upper], axis=axis_id)


def wrap_window(volume, axis_id, anchor, extent):
    return lax.dynamic_slice_in_dim(wrap_pad(volume, axis_id), anchor, extent + 2, axis_id)


def region(index_now, cells, levels_up):
    anchor = index_now * cells // 2**levels_up
    extent = max(cells // 2**levels_up, 1)
    return (anchor, extent)


def cut(children, index_x, index_y, cells_x, cells_y, levels_up):
    anchor_x, extent_x = region(index_x, cells_x, levels_up)
    parent_x = region(index_x, cells_x, levels_up + 1)[0]
    anchor_y, extent_y = region(index_y, cells_y, levels_up)
    parent_y = region(index_y, cells_y, levels_up + 1)[0]
    children = lax.dynamic_slice_in_dim(children, anchor_x - 2 * parent_x, extent_x, 0)
    return lax.dynamic_slice_in_dim(children, anchor_y - 2 * parent_y, extent_y, 1)


def coarse_window(grouped, index_x, index_y, cells_x, cells_y, levels_up):
    anchor_x, extent_x = region(index_x, cells_x, levels_up)
    anchor_y, extent_y = region(index_y, cells_y, levels_up)
    windowed = wrap_window(grouped, 0, anchor_x, extent_x)
    windowed = wrap_window(windowed, 1, anchor_y, extent_y)
    return wrap_pad(windowed, 2)


def upward(up_operator, grouped):
    parent = jnp.einsum("xyzs,sj->xyzj", grouped, up_operator, preferred_element_type=jnp.float32)
    return parent.astype(jnp.bfloat16)


def downward(down_operator, parent):
    children = jnp.einsum(
        "xyzi,it->xyzt", parent, down_operator.astype(jnp.float32), precision=lax.Precision.HIGHEST
    )
    return spread_cells(children)


def far_field(padded, kernel):
    size_x = padded.shape[0] - 2
    size_y = padded.shape[1] - 2
    size_z = padded.shape[2] - 2
    running = None
    for shift_id, offset in enumerate(shift_list()):
        window_piece = padded[
            1 + offset[0] : 1 + offset[0] + size_x, 1 + offset[1] : 1 + offset[1] + size_y
        ]
        product_term = jnp.einsum(
            "xyzs,st->xyzt", window_piece, kernel[shift_id], preferred_element_type=jnp.float32
        )
        product_term = product_term[:, :, 1 + offset[2] : 1 + offset[2] + size_z]
        running = product_term if running is None else running + product_term
    return running


def near_field(positions, masses, counts):
    slot_count = masses.shape[0]
    size_x, size_y, size_z = (masses.shape[1], masses.shape[2], masses.shape[3])
    live_slot = lax.broadcasted_iota(jnp.int32, masses.shape, 0) < counts[None]
    live_mass = jnp.where(live_slot, masses, jnp.float32(0.0))
    stacked = jnp.concatenate([positions, live_mass[None]], axis=0)
    padded = wrap_pad(extended(stacked, (("gx", 2), ("gy", 3)), 1), 4)
    block_size = min(8, slot_count)
    same_slot = lax.broadcasted_iota(
        jnp.int32, (block_size, slot_count, 1, 1, 1), 0
    ) + 0 == lax.broadcasted_iota(jnp.int32, (block_size, slot_count, 1, 1, 1), 1)
    running = jnp.zeros((block_size, size_x, size_y, size_z), jnp.float32)
    for offset in shift_list():
        source = padded[
            :,
            :,
            1 + offset[0] : 1 + offset[0] + size_x,
            1 + offset[1] : 1 + offset[1] + size_y,
            1 + offset[2] : 1 + offset[2] + size_z,
        ]
        squared = jnp.float32(SOFTENING * SOFTENING)
        for axis_id in range(3):
            separation = (
                source[axis_id][None] + jnp.float32(offset[axis_id]) - positions[axis_id][:, None]
            )
            squared = squared + separation * separation
        pair_terms = source[3][None] * lax.rsqrt(squared)
        if offset == (0, 0, 0):
            pair_terms = jnp.where(same_slot, jnp.float32(0.0), pair_terms)
        running = running + jnp.sum(pair_terms, axis=1)
    results = running
    running = results
    return jnp.where(live_slot, -running / slot_count, jnp.float32(0.0))


def general_device(
    leaf_multipoles, positions, masses, counts, up_operator, far_operator, down_operator
):
    potential = near_field(positions, masses, counts)
    kernel = assemble(far_operator)
    index_x = lax.axis_index("gx")
    index_y = lax.axis_index("gy")
    cells_x = leaf_multipoles.shape[1]
    cells_y = leaf_multipoles.shape[2]
    leaf_cells = jnp.transpose(leaf_multipoles, (1, 2, 3, 0))
    grouped_leaf = group_cells(leaf_cells)
    padded = wrap_pad(extended(grouped_leaf, (("gx", 0), ("gy", 1)), 1), 2)
    far_leaf = spread_cells(far_field(padded, kernel))
    grouped_six = group_cells(upward(up_operator, grouped_leaf))
    padded = wrap_pad(extended(grouped_six, (("gx", 0), ("gy", 1)), 1), 2)
    far_six = spread_cells(far_field(padded, kernel))
    moments_five = upward(up_operator, grouped_six)
    columns = lax.all_gather(moments_five, "gy", axis=1, tiled=True)
    whole_five = lax.all_gather(columns, "gx", axis=0, tiled=True)
    grouped_five = group_cells(whole_five)
    window_five = coarse_window(grouped_five, index_x, index_y, cells_x, cells_y, 3)
    moments_four = upward(up_operator, grouped_five)
    far_five = cut(
        spread_cells(far_field(window_five, kernel)), index_x, index_y, cells_x, cells_y, 2
    )
    grouped_four = group_cells(moments_four)
    window_four = coarse_window(grouped_four, index_x, index_y, cells_x, cells_y, 4)
    far_four = cut(
        spread_cells(far_field(window_four, kernel)), index_x, index_y, cells_x, cells_y, 3
    )
    grouped_three = group_cells(upward(up_operator, grouped_four))
    window_three = coarse_window(grouped_three, index_x, index_y, cells_x, cells_y, 5)
    far_three = cut(
        spread_cells(far_field(window_three, kernel)), index_x, index_y, cells_x, cells_y, 4
    )
    expansion = far_three
    expansion = far_four + cut(
        downward(down_operator, expansion), index_x, index_y, cells_x, cells_y, 3
    )
    expansion = far_five + cut(
        downward(down_operator, expansion), index_x, index_y, cells_x, cells_y, 2
    )
    expansion = far_six + cut(
        downward(down_operator, expansion), index_x, index_y, cells_x, cells_y, 1
    )
    expansion = far_leaf + cut(
        downward(down_operator, expansion), index_x, index_y, cells_x, cells_y, 0
    )
    return (jnp.transpose(expansion, (3, 0, 1, 2)), potential)


def solution(mesh):
    small = (mesh.shape["gx"], mesh.shape["gy"]) == (8, 4)
    return jax.shard_map(
        per_device if small else general_device,
        mesh=mesh,
        in_specs=(
            P(None, "gx", "gy", None),
            P(None, None, "gx", "gy", None),
            P(None, "gx", "gy", None),
            P("gx", "gy", None),
            P(),
            P(),
            P(),
        ),
        out_specs=(P(None, "gx", "gy", None), P(None, "gx", "gy", None)),
        check_vma=False,
    )
```

```python
import functools

import jax
import jax.numpy as jnp
import numpy as np
from jax import lax
from jax.experimental import pallas as pl
from jax.experimental.pallas import tpu as pltpu
from jax.sharding import PartitionSpec as P

SOFTENING = 0.05
EPS = SOFTENING * SOFTENING
F32 = jnp.float32
BF16 = jnp.bfloat16
COEF = 36
GROUP = 4 * COEF
Y_LEAF = 128 + 96
Y_SIX = Y_LEAF + 2 * GROUP
Y_FIVE = Y_SIX + GROUP // 2
Y_ROWS = Y_FIVE + 40
X_LEAF = 256 + 192
X_SIX = X_LEAF + 4 * GROUP
X_ROWS = X_SIX + GROUP
C_LEAF = 2 * 56
C_SIX = C_LEAF + 2 * GROUP
C_FIVE = C_SIX + GROUP
C_ROWS = C_FIVE + 80

VMEM = pl.BlockSpec(memory_space=pltpu.VMEM)
SMEM = pl.BlockSpec(memory_space=pltpu.SMEM)
HBM = pl.BlockSpec(memory_space=pltpu.MemorySpace.HBM)


def shape(dims, dtype):
    return jax.ShapeDtypeStruct(dims, dtype)


def kernel_call(body, outs, inputs, scratch=(), scalars=0, space=VMEM, target=VMEM, limit=20):
    return pl.pallas_call(
        body,
        out_shape=outs,
        in_specs=[SMEM] * scalars + [space] * (len(inputs) - scalars),
        out_specs=[target] * len(outs),
        scratch_shapes=list(scratch),
        compiler_params=pltpu.CompilerParams(vmem_limit_bytes=limit * 1024 * 1024),
    )(*inputs)


def iota(dims, axis):
    return lax.broadcasted_iota(jnp.int32, dims, axis)


def dot(lhs, rhs):
    return lax.dot_general(lhs, rhs, (((1,), (0,)), ((), ())), preferred_element_type=F32)


def dot_tn(lhs, rhs):
    return lax.dot_general(lhs, rhs, (((0,), (0,)), ((), ())), preferred_element_type=F32)


def dot_nt(lhs, rhs):
    return lax.dot_general(lhs, rhs, (((1,), (1,)), ((), ())), preferred_element_type=F32)


def one_hot(mask):
    return jnp.where(mask, F32(1.0), F32(0.0)).astype(BF16)


def pick(rows, source):
    return one_hot(iota((rows, source.shape[1]), 0) == source)


def parts(value):
    high = value.astype(BF16)
    return high, (value - high.astype(F32)).astype(BF16)


def lane_roll(value, shift):
    return pltpu.roll(value, shift % 128, 1) if shift % 128 else value


def up_blocks(up_ref):
    col = iota((1, GROUP), 1)
    block = jnp.where(col < 2 * COEF, jnp.where(col < COEF, 0, 1), jnp.where(col < 3 * COEF, 2, 3))
    return [
        dot(up_ref[...], pick(8 * COEF, col + (block + bit) * COEF)).astype(BF16) for bit in range(2)
    ]


def prep_kernel(
    leaf_hbm, pos_hbm, mass_hbm, count_hbm, up_hbm,
    grid_ref, up_msg, down_msg, low_msg, high_msg, six_ref, five_ref, live_ref,
    pos_ref, count_ref, halves_ref,
    up_ref, leaf_ref, mass_ref, m32, x32, six32, near32, sems,
):
    copies = [
        pltpu.make_async_copy(source, target, sems.at[k])
        for k, (source, target) in enumerate(
            (
                (leaf_hbm, leaf_ref), (pos_hbm, pos_ref), (mass_hbm, mass_ref),
                (count_hbm, count_ref), (up_hbm, up_ref),
            )
        )
    ]
    for copy in copies:
        copy.start()
    copies[0].wait()
    m32[0:1152, :] = leaf_ref[...].astype(F32)
    for x in range(4):
        for y in range(8):
            start = ((x // 2) * 4 + y // 2) * GROUP + (2 * (x % 2) + y % 2) * COEF
            x32[start : start + COEF, :] = m32[pl.ds(x * 8 + y, COEF, stride=32), :]
    grid = x32[0:1152, :].astype(BF16)
    grid_ref[...] = grid
    for msg, parent in ((up_msg, 3), (down_msg, 0)):
        for xp in range(2):
            msg[Y_LEAF + xp * GROUP : Y_LEAF + (xp + 1) * GROUP, :] = grid_ref[
                (xp * 4 + parent) * GROUP : (xp * 4 + parent + 1) * GROUP, :
            ]
    low_msg[X_LEAF:X_SIX, :] = grid_ref[0 : 4 * GROUP, :]
    high_msg[X_LEAF:X_SIX, :] = grid_ref[4 * GROUP : 8 * GROUP, :]
    copies[4].wait()
    low_half = iota((COEF, 128), 1) < 64
    even_up, odd_up = up_blocks(up_ref)
    halves_ref[0], halves_ref[1] = even_up, odd_up
    col = iota((1, 128), 1)
    split_z = pick(128, 2 * (col % 64) + col // 64)
    split = dot(grid, split_z).astype(BF16)
    columns = jnp.concatenate([split[k * GROUP : (k + 1) * GROUP] for k in range(8)], axis=1)
    even, odd = dot(even_up, columns), dot(odd_up, columns)
    for xp in range(2):
        for y in range(2):
            first, second = (xp * 4 + y) * 128, (xp * 4 + 2 + y) * 128
            near_part = even[:, first : first + 128] + lane_roll(odd[:, first : first + 128], 64)
            far_part = lane_roll(even[:, second : second + 128], 64) + odd[:, second : second + 128]
            start = (2 * xp + y) * COEF
            six32[start : start + COEF, :] = jnp.where(low_half, near_part, far_part)
    six = six32[0:GROUP, :].astype(BF16)
    six_ref[...] = six
    low_msg[X_SIX:X_ROWS, :] = six
    high_msg[X_SIX:X_ROWS, :] = six
    left = iota((72, 128), 1) < 64
    first, second = six32[0:72, :], six32[72:144, :]
    up_msg[Y_SIX:Y_FIVE, :] = jnp.where(left, lane_roll(first, 64), second).astype(BF16)
    down_msg[Y_SIX:Y_FIVE, :] = jnp.where(left, first, lane_roll(second, 64)).astype(BF16)
    split_six = pick(128, ((col // 32) % 2) * 64 + 2 * (col % 32) + col // 64)
    split = dot(six, split_six).astype(BF16)
    five = dot(even_up, split) + lane_roll(dot(odd_up, split), 64)
    five = jnp.concatenate([five, jnp.zeros((4, 128), F32)], axis=0).astype(BF16)
    five_ref[...] = five
    for msg in (up_msg, down_msg):
        msg[Y_FIVE:Y_ROWS, :] = five
    for copy in copies[1:4]:
        copy.wait()
    count = count_ref[...]
    for slot in range(8):
        live_ref[slot * 32 : slot * 32 + 32, :] = jnp.where(
            count > slot, mass_ref[slot * 32 : slot * 32 + 32, :], F32(0.0)
        )
    for msg, y in ((up_msg, 7), (down_msg, 0)):
        rows = []
        for x in range(4):
            rows.append(pos_ref[pl.ds(x * 8 + y, 24, stride=32), :])
            rows.append(live_ref[pl.ds(x * 8 + y, 8, stride=32), :])
        high, low = parts(jnp.concatenate(rows, axis=0))
        msg[0:128, :] = high
        for x in range(4):
            msg[128 + 24 * x : 152 + 24 * x, :] = low[32 * x : 32 * x + 24]
    for msg, x in ((low_msg, 0), (high_msg, 3)):
        for slot in range(8):
            for axis in range(3):
                start = (axis * 8 + slot) * 32 + x * 8
                near32[pl.ds(axis * 8 + slot, 8, stride=32), :] = pos_ref[start : start + 8, :]
            start = slot * 32 + x * 8
            near32[pl.ds(24 + slot, 8, stride=32), :] = live_ref[start : start + 8, :]
        high, low = parts(near32[...])
        msg[0:256, :] = high
        for y in range(8):
            msg[256 + 24 * y : 280 + 24 * y, :] = low[32 * y : 32 * y + 24]


def in_hbm(value):
    return pltpu.with_memory_space_constraint(value, pltpu.MemorySpace.HBM)


def prepare(leaf, positions, masses, counts, up_operator):
    inputs = (leaf, positions, masses, counts, up_operator)
    return kernel_call(
        prep_kernel,
        (
            shape((8 * GROUP, 128), BF16),
            shape((Y_ROWS, 128), BF16),
            shape((Y_ROWS, 128), BF16),
            shape((X_ROWS, 128), BF16),
            shape((X_ROWS, 128), BF16),
            shape((GROUP, 128), BF16),
            shape((40, 128), BF16),
            shape((256, 128), F32),
            shape((768, 128), F32),
            shape((32, 128), jnp.int32),
            shape((2, COEF, GROUP), BF16),
        ),
        [in_hbm(value) for value in inputs],
        (
            pltpu.VMEM(up_operator.shape, BF16),
            pltpu.VMEM((1152, 128), BF16),
            pltpu.VMEM((256, 128), F32),
            pltpu.VMEM((1280, 128), F32),
            pltpu.VMEM((1160, 128), F32),
            pltpu.VMEM((GROUP + 8, 128), F32),
            pltpu.VMEM((256, 128), F32),
            pltpu.SemaphoreType.DMA((5,)),
        ),
        space=HBM,
    )


def halo_six(below, above):
    upper, lower = above[Y_SIX:Y_FIVE, :].astype(F32), below[Y_SIX:Y_FIVE, :].astype(F32)
    left = iota((72, 128), 1) < 64
    return jnp.concatenate(
        [
            jnp.where(left, upper, lane_roll(lower, 64)),
            jnp.where(left, lane_roll(upper, 64), lower),
        ],
        axis=0,
    )


def cross_kernel(place, below, above, two, own, to_low, to_high, five32):
    lane = iota((COEF, 128), 1) // 32
    five32[...] = jnp.zeros_like(five32)
    for shift, ref, first in ((0, own, 0), (3, below, Y_FIVE), (1, above, Y_FIVE), (2, two, 0)):
        at = lax.rem(place[1] + shift, 4)
        value = ref[first : first + 40, :].astype(F32)
        for y in range(2):
            moved = pltpu.roll(value, lax.rem(32 * at + 96 * y, 128), 1)[0:COEF]
            rows = slice(y * COEF, (y + 1) * COEF)
            five32[rows, :] = jnp.where(lane == at, moved, five32[rows, :])
    five = five32[...].astype(BF16)
    halo = halo_six(below, above).astype(BF16)
    for msg, x, xp in ((to_low, 0, 0), (to_high, 3, 1)):
        for side, ref in enumerate((below, above)):
            first = side * 56
            msg[first : first + 32, :] = ref[32 * x : 32 * x + 32, :]
            msg[first + 32 : first + 56, :] = ref[128 + 24 * x : 152 + 24 * x, :]
            source, first = Y_LEAF + xp * GROUP, C_LEAF + side * GROUP
            msg[first : first + GROUP, :] = ref[source : source + GROUP, :]
        msg[C_SIX:C_FIVE, :] = halo
        msg[C_FIVE:C_ROWS, :] = five


def cross(*inputs):
    return kernel_call(
        cross_kernel,
        (shape((C_ROWS, 128), BF16), shape((C_ROWS, 128), BF16)),
        inputs,
        (pltpu.VMEM((80, 128), F32),),
        scalars=1,
    )


def inverse_distance(target, source):
    squared = F32(EPS)
    for axis in range(3):
        separation = source[axis] - target[axis]
        squared = squared + separation * separation
    return lax.rsqrt(squared)


def pair_sums(shifted, sums, goals, x, step, totals):
    step_x, step_y, step_z = step
    edge = iota((8, 128), 0) == (7 if step_y > 0 else 0)
    for slot in range(8):
        source = [shifted[step_z + 1, k, slot, x] for k in range(4)]
        if step_y:
            source = [pltpu.roll(value, (-step_y) % 8, 0) for value in source]
            source[1] = source[1] + F32(step_y)
            source[3] = jnp.where(edge, F32(0.0), source[3])
        if step_x:
            source[0] = source[0] + F32(step_x)
        back = None
        for goal in range(8):
            inverse = inverse_distance(goals[goal], source)
            totals[goal] = totals[goal] + source[3] * inverse
            term = goals[goal][3] * inverse
            back = term if back is None else back + term
        if step_y:
            back = pltpu.roll(jnp.where(edge, F32(0.0), back), step_y % 8, 0)
        sums[step_z + 1, slot, x] = sums[step_z + 1, slot, x] + back


def plane_goals(shifted, x):
    return [[shifted[1, k, slot, x] for k in range(4)] for slot in range(8)]


def step_pairs(shifted, sums, x):
    for step_y in (-1, 0, 1):
        goals = plane_goals(shifted, x)
        totals = [sums[1, slot, x] for slot in range(8)]
        for step_z in (-1, 0, 1):
            pair_sums(shifted, sums, goals, x + 1, (1, step_y, step_z), totals)
        for slot in range(8):
            sums[1, slot, x] = totals[slot]


def plane_kernel(pos_ref, live_ref, far_hbm, down_hbm, sums, shifted, far_ref, down_ref, sems):
    copies = [
        pltpu.make_async_copy(source, target, sems.at[k])
        for k, (source, target) in enumerate(((far_hbm, far_ref), (down_hbm, down_ref)))
    ]
    for copy in copies:
        copy.start()
    sums[...] = jnp.zeros_like(sums)

    def plane(x, carry):
        for slot in range(8):
            values = [pos_ref[axis, slot, x] for axis in range(3)] + [live_ref[slot, x]]
            for index, step in enumerate((-1, 0, 1)):
                moved = [lane_roll(value, -step) for value in values]
                if step:
                    moved[2] = moved[2] + F32(step)
                for k in range(4):
                    shifted[index, k, slot, x] = moved[k]
        goals = plane_goals(shifted, x)
        totals = [jnp.zeros((8, 128), F32) for slot in range(8)]
        for slot in range(8):
            for goal in range(slot):
                inverse = inverse_distance(goals[goal], goals[slot])
                totals[goal] = totals[goal] + goals[slot][3] * inverse
                totals[slot] = totals[slot] + goals[goal][3] * inverse
        for step in ((0, 0, 1), (0, 1, -1), (0, 1, 0), (0, 1, 1)):
            pair_sums(shifted, sums, goals, x, step, totals)
        for slot in range(8):
            sums[1, slot, x] = sums[1, slot, x] + totals[slot]
        return carry

    lax.fori_loop(0, 4, plane, 0)

    def step(x, carry):
        step_pairs(shifted, sums, x)
        return carry

    lax.fori_loop(0, 2, step, 0)
    for copy in copies:
        copy.wait()


def plane_pairs(positions, live, far_operator, down_operator):
    return pl.pallas_call(
        plane_kernel,
        out_shape=(
            shape((3, 8, 4, 8, 128), F32),
            shape((3, 4, 8, 4, 8, 128), F32),
            shape(far_operator.shape, BF16),
            shape(down_operator.shape, BF16),
        ),
        in_specs=[VMEM, VMEM, HBM, HBM],
        out_specs=[VMEM] * 4,
        scratch_shapes=[pltpu.SemaphoreType.DMA((2,))],
        compiler_params=pltpu.CompilerParams(vmem_limit_bytes=16 * 1024 * 1024),
    )(positions, live, in_hbm(far_operator), in_hbm(down_operator))


def joined(target, msg, high, low, count):
    for cell in range(count):
        first = 32 * cell
        whole = msg[high + first : high + first + 32, :].astype(F32)
        rest = msg[low + 24 * cell : low + 24 * cell + 24, :].astype(F32)
        target[first : first + 24, :] = whole[0:24] + rest
        target[first + 24 : first + 32, :] = whole[24:32]


def add_sources(fetch, shifted, goals, totals):
    for slot in range(8):
        values = [fetch(k, slot) for k in range(4)]
        for step in (-1, 0, 1):
            moved = [lane_roll(value, -step) for value in values]
            if step:
                moved[2] = moved[2] + F32(step)
            for k in range(4):
                shifted[step + 1, k, slot] = moved[k]
    totals = list(totals)
    for step in range(3):
        for slot in range(8):
            source = [shifted[step, k, slot] for k in range(4)]
            for goal in range(8):
                totals[goal] = totals[goal] + source[3] * inverse_distance(goals[goal], source)
    return tuple(totals)


def rows_kernel(
    inner_ref, pos_ref, count_ref, below, above, low_corner, high_corner, out_ref,
    sources, shifted, added, places,
):
    turn = jnp.where(iota((8, 128), 0) >= 4, F32(1.0), F32(-1.0))
    for side, msg in enumerate((below, above)):
        first = side * 128
        joined(sources.at[1, pl.ds(first, 128)], msg, 0, 128, 4)
        high = side * 56
        joined(sources.at[0, pl.ds(first, 32)], low_corner, high, high + 32, 1)
        sources[0, first + 32 : first + 128, :] = sources[1, first : first + 96, :]
        sources[2, first : first + 96, :] = sources[1, first + 32 : first + 128, :]
        joined(sources.at[2, pl.ds(first + 96, 32)], high_corner, high, high + 32, 1)
    places[0:768, :] = pos_ref[...]
    goals = []
    for slot in range(8):
        at = [(axis * 8 + slot) * 32 for axis in range(3)]
        goals.append(
            [
                jnp.concatenate(
                    [places[pl.ds(a, 4, stride=8), :], places[pl.ds(a + 7, 4, stride=8), :]], axis=0
                )
                for a in at
            ]
        )

    def body(step_x, totals):
        def fetch(k, slot):
            value = sources[step_x, pl.ds(8 * k + slot, 8, stride=32), :]
            if k == 0:
                value = value + (step_x - 1).astype(F32)
            return value + turn if k == 1 else value

        return add_sources(fetch, shifted, goals, totals)

    totals = lax.fori_loop(0, 3, body, tuple(jnp.zeros((8, 128), F32) for slot in range(8)))
    added[...] = jnp.zeros_like(added)
    for slot in range(8):
        added[pl.ds(slot * 32, 4, stride=8), :] = totals[slot][0:4]
        added[pl.ds(slot * 32 + 7, 4, stride=8), :] = totals[slot][4:8]
    count = count_ref[...]
    for slot in range(8):
        rows = slice(slot * 32, slot * 32 + 32)
        total = inner_ref[rows, :] + added[rows, :]
        out_ref[rows, :] = jnp.where(count > slot, -total / 8, F32(0.0))


def faces_kernel(sums_ref, shifted_ref, pos_ref, low, high, out_ref, sides, shifted, sums):
    sums[...] = sums_ref[...]
    step_pairs(shifted_ref, sums, 2)
    for x in range(4):
        for slot in range(8):
            out_ref[slot, x] = (
                sums[1, slot, x] + lane_roll(sums[0, slot, x], -1) + lane_roll(sums[2, slot, x], 1)
            )
    sides[...] = jnp.zeros_like(sides)
    for index, msg in enumerate((low, high)):
        joined(sides.at[index, pl.ds(32, 256)], msg, 0, 256, 8)

    def face(index, carry):
        x = 3 * index
        goals = [[pos_ref[axis, slot, x] for axis in range(3)] for slot in range(8)]

        def body(step_y, totals):
            def fetch(k, slot):
                value = sides[index, pl.ds(step_y * 32 + 8 * k + slot, 8, stride=32), :]
                if k == 0:
                    value = value + (2 * index - 1).astype(F32)
                return value + (step_y - 1).astype(F32) if k == 1 else value

            return add_sources(fetch, shifted, goals, totals)

        totals = lax.fori_loop(0, 3, body, tuple(out_ref[slot, x] for slot in range(8)))
        for slot in range(8):
            out_ref[slot, x] = totals[slot]
        return carry

    lax.fori_loop(0, 2, face, 0)


def row_pairs(*inputs):
    return kernel_call(
        rows_kernel,
        (shape((256, 128), F32),),
        inputs,
        (
            pltpu.VMEM((3, 256, 128), F32),
            pltpu.VMEM((3, 4, 8, 8, 128), F32),
            pltpu.VMEM((320, 128), F32),
            pltpu.VMEM((832, 128), F32),
        ),
    )[0]


def face_pairs(*inputs):
    return kernel_call(
        faces_kernel,
        (shape((8, 4, 8, 128), F32),),
        inputs,
        (
            pltpu.VMEM((2, 320, 128), F32),
            pltpu.VMEM((3, 4, 8, 8, 128), F32),
            pltpu.VMEM((3, 8, 4, 8, 128), F32),
        ),
    )[0]


def far_starts():
    starts, count = {}, 0
    for step_x in range(-3, 4):
        for step_y in range(-3, 4):
            starts[step_x, step_y] = count * COEF
            count += 7 if max(abs(step_x), abs(step_y)) >= 2 else 4
    return starts


def operator_kernel(far_ref, out_ref, far32, stack):
    far32[0:COEF, 0:11264] = far_ref[:, 0:11264].astype(F32)
    far32[:, 11264:11520] = jnp.zeros((40, 256), F32)
    far32[0:COEF, 11264:11376] = far_ref[:, 11264:11376].astype(F32)
    lane = iota((COEF, 256), 1)

    def window(start):
        base = start // 128 * 128
        value = far32[0:COEF, base : base + 384]
        shift = start - base
        return (pltpu.roll(value, 384 - shift, 1) if shift else value)[:, 0:256]

    starts = far_starts()
    for step_x in range(-3, 4):
        for step_y in range(-3, 4):
            start = starts[step_x, step_y]
            if max(abs(step_x), abs(step_y)) >= 2:
                block = jnp.where(lane < 7 * COEF, window(start), F32(0.0))
            else:
                block = jnp.where(
                    lane < 2 * COEF,
                    window(start),
                    jnp.where(
                        (lane >= 5 * COEF) & (lane < 7 * COEF), window(start - 3 * COEF), F32(0.0)
                    ),
                )
            for bit_x in range(2):
                for bit_y in range(2):
                    source_x, source_y = step_x + bit_x, step_y + bit_y
                    if -2 <= source_x <= 3 and -2 <= source_y <= 3:
                        shift_x, child_x = source_x // 2 + 1, source_x % 2
                        shift_y, child_y = source_y // 2 + 1, source_y % 2
                        first = shift_y * GROUP + (2 * child_x + child_y) * COEF
                        bits = (2 * bit_x + bit_y) * 256
                        stack[shift_x, first : first + COEF, bits : bits + 256] = block
    out_ref[...] = stack[:, 0 : 3 * GROUP, :].astype(BF16)


def far_matrix(far_operator):
    return kernel_call(
        operator_kernel,
        (shape((3, 3 * GROUP, 1024), BF16),),
        (far_operator,),
        (pltpu.VMEM((40, 11520), F32), pltpu.VMEM((3, 3 * GROUP + 8, 1024), F32)),
    )[0]


def z_sum(products, bits, lanes, first):
    odd = iota((COEF, 128), 1) % 2 != first
    total = None
    for step in range(-3, 4):
        start = bits * 256 + (step + 3) * COEF
        value = lane_roll(products[start : start + COEF, lanes], -step)
        if step == 3:
            value = jnp.where(odd, F32(0.0), value)
        if step == -3:
            value = jnp.where(odd, value, F32(0.0))
        total = value if total is None else total + value
    return total


def multiply(matrix, rows, sources):
    total = None
    for shift_x, source in enumerate(sources):
        term = dot_tn(matrix[shift_x, :, rows], source)
        total = term if total is None else total + term
    return total


def windows_x(cells, parent):
    rows = slice(parent * GROUP, (parent + 3) * GROUP)
    return [cells[rows, shift_x * 128 : shift_x * 128 + 256] for shift_x in range(3)]


def middle_kernel(matrix, grid_ref, low, high, potential, products, out_ref, cells, sem):
    leaving = pltpu.make_async_copy(potential, out_ref, sem)
    leaving.start()
    cells[:, 0:128] = low[X_LEAF:X_SIX, :]
    cells[:, 128:256] = grid_ref[0 : 4 * GROUP, :]
    cells[:, 256:384] = grid_ref[4 * GROUP : 8 * GROUP, :]
    cells[:, 384:512] = high[X_LEAF:X_SIX, :]
    for parent in range(2):
        products[parent] = multiply(matrix, slice(0, 1024), windows_x(cells, parent))
    leaving.wait()


def middle_products(*inputs):
    return pl.pallas_call(
        middle_kernel,
        out_shape=(shape((2, 1024, 256), F32), shape((256, 128), F32)),
        in_specs=[VMEM] * 5,
        out_specs=[VMEM, HBM],
        scratch_shapes=[pltpu.VMEM((4 * GROUP, 512), BF16), pltpu.SemaphoreType.DMA],
        compiler_params=pltpu.CompilerParams(vmem_limit_bytes=20 * 1024 * 1024),
    )(*inputs)


def levels_kernel(
    place, matrix, middle, grid_ref, six_ref, below, above, low, high, low_corner, high_corner,
    near_three, up_three, down_three, halves_ref, down_ref, out_ref,
    cells, fives, fours, three32, windows, products, coarse, down32, downs, expand, lifted,
    leaving, sems,
):
    gx, gy = place[0], place[1]
    col = iota((1, 128), 1)

    for first, msg, corner in ((0, low, low_corner), (384, high, high_corner)):
        lanes = slice(first, first + 128)
        cells[0:GROUP, lanes] = corner[C_LEAF : C_LEAF + GROUP, :]
        cells[GROUP : 5 * GROUP, lanes] = msg[X_LEAF:X_SIX, :]
        cells[5 * GROUP : 6 * GROUP, lanes] = corner[C_LEAF + GROUP : C_SIX, :]
    for xp in range(2):
        lanes = slice(128 + 128 * xp, 256 + 128 * xp)
        source = Y_LEAF + xp * GROUP
        cells[0:GROUP, lanes] = below[source : source + GROUP, :]
        cells[GROUP : 5 * GROUP, lanes] = grid_ref[xp * 4 * GROUP : (xp + 1) * 4 * GROUP, :]
        cells[5 * GROUP : 6 * GROUP, lanes] = above[source : source + GROUP, :]

    todo = [(side, half) for side in range(2) for half in range(2)]

    def leaf_products(count=1):
        for side, half in todo[:count]:
            rows = slice(half * 512, half * 512 + 512)
            products[side + 1, rows, :] = multiply(matrix, rows, windows_x(cells, 3 * side))
        del todo[:count]

    size = fives.shape[0] // 72
    for shift, msg, first in (
        (-1, near_three, 0), (0, near_three, 80), (1, near_three, 160),
        (-4, up_three, 0), (-3, up_three, 80), (-2, up_three, 160),
        (2, down_three, 0), (3, down_three, 80), (4, down_three, 160),
    ):
        at = pl.multiple_of(lax.rem(gx + shift + size, size) * 72, 8)
        fives[pl.ds(at, 72), :] = msg[first : first + 72, :].astype(F32)
    even_up, odd_up = halves_ref[0], halves_ref[1]
    leaf_products()

    def upward(grouped, split):
        children = dot(grouped.astype(BF16), split).astype(BF16)
        value = dot(even_up, children) + lane_roll(dot(odd_up, children), 64)
        return value.astype(BF16).astype(F32)

    lane = col % 64
    split_five = pick(
        128, ((lane // 16 % 2) * 2 + lane // 32) * 32 + 2 * (lane % 16) + col // 64
    )
    for x in range(4):
        value = upward(fives[x * GROUP : (x + 1) * GROUP, :], split_five)
        first = (x // 2) * GROUP + (x % 2) * 2 * COEF
        fours[first : first + COEF, :] = value
        fours[first + COEF : first + 2 * COEF, :] = lane_roll(value, 96)
    leaf_products()
    split_four = pick(
        128, jnp.where(lane < 16, (lane // 8) * 16 + 2 * (lane % 8) + col // 64, -1)
    )
    for x in range(2):
        value = upward(fours[x * GROUP : (x + 1) * GROUP, :], split_four)
        three32[x * 2 * COEF : x * 2 * COEF + COEF, :] = value
        three32[x * 2 * COEF + COEF : (x + 1) * 2 * COEF, :] = lane_roll(value, 120)
    leaf_products()
    def wrapped(first, base, size):
        cell = (col - first - 3 + size) & (size - 1)
        return pick(128, jnp.where((col >= first) & (col < first + size + 6), base + cell, -1))

    three = dot(three32[0:GROUP, :].astype(BF16), wrapped(92, 0, 8))
    six_lanes = [wrapped(0, 0, 64), wrapped(0, 64, 64)]
    five_lanes = [wrapped(70, lax.rem(gy + step + 3, 4) * 32, 32) for step in range(3)]
    four_lanes = [wrapped(70, lax.rem(gy // 2 + step + 1, 2) * 16, 16) for step in range(3)]
    for shift_x in range(3):
        if shift_x == 1:
            own, other = six_ref[...], halo_six(below, above).astype(BF16)
        else:
            own = (low if shift_x == 0 else high)[X_SIX:X_ROWS, :]
            other = (low_corner if shift_x == 0 else high_corner)[C_SIX:C_FIVE, :]
        at = pl.multiple_of(lax.rem(gx // 2 + shift_x + 3, 4) * GROUP, 8)
        five = fives[pl.ds(at, GROUP), :].astype(BF16)
        at = pl.multiple_of(lax.rem(gx // 4 + shift_x + 1, 2) * GROUP, 8)
        four = fours[pl.ds(at, GROUP), :].astype(BF16)
        for shift_y in range(3):
            left = dot(other if shift_y == 0 else own, six_lanes[0 if shift_y == 1 else 1])
            right = dot(other if shift_y == 2 else own, six_lanes[1 if shift_y == 1 else 0])
            left = left + dot(five, five_lanes[shift_y])
            right = right + dot(four, four_lanes[shift_y]) + three
            rows = slice(shift_y * GROUP, (shift_y + 1) * GROUP)
            windows[shift_x, rows, 0:128] = left.astype(BF16)
            windows[shift_x, rows, 128:256] = right.astype(BF16)
    for half in range(2):
        rows = slice(half * 512, half * 512 + 512)
        products[0, rows, :] = multiply(matrix, rows, [windows[shift_x] for shift_x in range(3)])
    leaf_products()
    coarse[...] = jnp.zeros_like(coarse)
    for bits in range(4):
        for lanes in (slice(0, 128), slice(128, 256)):
            coarse[bits * 40 : bits * 40 + COEF, lanes] = z_sum(products.at[0], bits, lanes, 1)
    eye = pick(8 * COEF, iota((1, 8 * COEF), 1))
    down32[0 : 8 * COEF, :] = dot_nt(eye, down_ref[...])
    downs[...] = jnp.zeros_like(downs)
    for bits in range(4):
        for bit in range(2):
            first = (2 * bits + bit) * COEF
            downs[bit, bits * 40 : bits * 40 + COEF, :] = down32[first : first + COEF, :]
    operators = [downs[bit].astype(BF16) for bit in range(2)]

    def spread(value, first, start, count):
        inside = (col >= start) & (col < start + count)
        taken = pick(128, jnp.where(inside, first + (col - start) // 2, -1))
        return [dot(part, taken).astype(BF16) for part in parts(value)]

    def lift(wide, lanes, first):
        halves = [dot(value, wide[0]) + dot(value, wide[1]) for value in operators]
        even = iota(halves[0].shape, 1) % 2 == first
        lifted[:, lanes] = jnp.where(even, halves[0], halves[1])

    def block(bits):
        return pl.ds(bits * 40 if isinstance(bits, int) else pl.multiple_of(bits * 40, 8), COEF)

    left, right, both = slice(0, 128), slice(128, 256), slice(0, 256)
    bits = 2 * lax.rem(gx // 4, 2) + lax.rem(gy // 2, 2)
    value = coarse[block(bits), right]
    wide = spread(value, 95, 73, 16)
    lift(wide, left, 1)
    leaf_products()
    bits = 2 * lax.rem(gx // 2, 2) + lax.rem(gy, 2)
    value = coarse[block(bits), right] + lifted[block(bits), left]
    wide = spread(value, 73, 73, 32)
    lift(wide, left, 1)
    leaf_products()
    wides = []
    for y in range(2):
        bits = 2 * lax.rem(gx, 2) + y
        value = coarse[block(bits), left] + lifted[block(bits), left]
        wides.append(spread(value, 73, 3, 64))
    lift([jnp.concatenate(pair, axis=1) for pair in zip(*wides)], both, 1)
    leaf_products()
    doubled = pick(128, 3 + col // 2)
    for k, part in enumerate(parts(coarse[...] + lifted[:, both])):
        for y in range(2):
            wide = dot(part[:, y * 128 : y * 128 + 128], doubled)
            for bits in range(4):
                at = ((bits // 2) * 4 + 2 * y + bits % 2) * 128
                expand[k, 0:COEF, at : at + 128] = wide[bits * 40 : bits * 40 + COEF].astype(BF16)
    leaf_products(8)
    lift([expand[k, 0:COEF, :] for k in range(2)], slice(0, 1024), 0)
    copies = []
    for x in range(4):
        xp = x // 2
        for y in range(8):
            parent, bits = y // 2, 2 * (x % 2) + y % 2
            source = middle.at[parent - 1] if parent in (1, 2) else products.at[1 + parent // 3]
            value = z_sum(source, bits, slice(xp * 128, xp * 128 + 128), 0)
            at = (xp * 4 + parent) * 128
            leaving[x, pl.ds(y, COEF, stride=8), :] = value + lifted[block(bits), at : at + 128]
        copies.append(
            pltpu.make_async_copy(
                leaving.at[x, pl.ds(0, 8 * COEF)].reshape(COEF, 8, 128), out_ref.at[:, x], sems.at[x]
            )
        )
        copies[-1].start()
    for copy in copies:
        copy.wait()


def all_levels(*inputs):
    return kernel_call(
        levels_kernel,
        (shape((COEF, 4, 8, 128), F32),),
        inputs,
        (
            pltpu.VMEM((6 * GROUP, 512), BF16),
            pltpu.VMEM((576, 128), F32),
            pltpu.VMEM((2 * GROUP + 8, 128), F32),
            pltpu.VMEM((GROUP + 8, 128), F32),
            pltpu.VMEM((3, 3 * GROUP, 256), BF16),
            pltpu.VMEM((3, 1024, 256), F32),
            pltpu.VMEM((160, 256), F32),
            pltpu.VMEM((8 * COEF + 8, COEF), F32),
            pltpu.VMEM((2, 160, COEF), F32),
            pltpu.VMEM((2, 40, 1024), BF16),
            pltpu.VMEM((160, 1024), F32),
            pltpu.VMEM((4, 8 * COEF + 32, 128), F32),
            pltpu.SemaphoreType.DMA((4,)),
        ),
        scalars=1,
        target=HBM,
    )[0]


def moved(value, step_x, step_y):
    size_x, size_y = lax.axis_size("gx"), lax.axis_size("gy")
    table = [
        (x * size_y + y, (x + step_x) % size_x * size_y + (y + step_y) % size_y)
        for x in range(size_x)
        for y in range(size_y)
    ]
    return lax.ppermute(value, ("gx", "gy"), table)


def per_device(
    leaf_multipoles, positions, masses, counts, up_operator, far_operator, down_operator
):
    place = jnp.stack([lax.axis_index("gx"), lax.axis_index("gy")]).astype(jnp.int32)
    (
        grid, up_msg, down_msg, low_msg, high_msg, six, five, live,
        positions, counts, up_halves,
    ) = prepare(
        leaf_multipoles.reshape(1152, 128), positions.reshape(768, 128), masses.reshape(256, 128),
        counts.reshape(32, 128), up_operator.T,
    )
    positions = positions.reshape(3, 8, 4, 8, 128)
    below, above, two = moved(up_msg, 0, 1), moved(down_msg, 0, -1), moved(five, 0, 2)
    low, high = moved(high_msg, 1, 0), moved(low_msg, -1, 0)
    inner, shifted, far_operator, down_operator = plane_pairs(
        positions, live.reshape(8, 4, 8, 128), far_operator, down_operator
    )
    matrix = far_matrix(far_operator)
    below, above, two, inner, matrix = lax.optimization_barrier((below, above, two, inner, matrix))
    to_low, to_high = cross(place, below, above, two, five)
    low_corner, high_corner = moved(to_high, 1, 0), moved(to_low, -1, 0)
    inner = face_pairs(inner, shifted, positions, low, high)
    low_corner, high_corner, inner = lax.optimization_barrier((low_corner, high_corner, inner))
    three = jnp.concatenate([low_corner[C_FIVE:], to_low[C_FIVE:], high_corner[C_FIVE:]], axis=0)
    up_three, down_three = moved(three, 3, 0), moved(three, -3, 0)
    potential = row_pairs(
        inner.reshape(256, 128), positions.reshape(768, 128), counts, below, above, low_corner,
        high_corner,
    )
    middle, potential = middle_products(matrix, grid, low, high, potential)
    up_three, down_three, potential, middle = lax.optimization_barrier(
        (up_three, down_three, potential, middle)
    )
    expansion = all_levels(
        place, matrix, middle, grid, six, below, above, low, high, low_corner, high_corner,
        three, up_three, down_three, up_halves, down_operator,
    )
    return expansion, potential.reshape(8, 4, 8, 128)


def extended(cells, sides, width):
    for axis, dim in sides:
        count = lax.axis_size(axis)
        head = lax.slice_in_dim(cells, 0, width, axis=dim)
        tail = lax.slice_in_dim(cells, cells.shape[dim] - width, cells.shape[dim], axis=dim)
        cells = jnp.concatenate(
            [
                lax.ppermute(tail, axis, [(i, (i + 1) % count) for i in range(count)]),
                cells,
                lax.ppermute(head, axis, [((i + 1) % count, i) for i in range(count)]),
            ],
            axis=dim,
        )
    return cells


def shift_list():
    return [
        (step_x, step_y, step_z)
        for step_x in (-1, 0, 1)
        for step_y in (-1, 0, 1)
        for step_z in (-1, 0, 1)
    ]


def child_bits(number):
    return (number // 4, number // 2 % 2, number % 2)


def offset_table():
    vectors = [
        (step_x, step_y, step_z)
        for step_x in range(-3, 4)
        for step_y in range(-3, 4)
        for step_z in range(-3, 4)
        if max(abs(step_x), abs(step_y), abs(step_z)) >= 2
    ]
    lookup = np.full((27, 8, 8), len(vectors), dtype=np.int32)
    for shift_id, offset in enumerate(shift_list()):
        for source in range(8):
            for target in range(8):
                vector = tuple(
                    (
                        2 * offset[axis_id]
                        + child_bits(source)[axis_id]
                        - child_bits(target)[axis_id]
                        for axis_id in range(3)
                    )
                )
                if max(abs(vector[0]), abs(vector[1]), abs(vector[2])) >= 2:
                    lookup[shift_id, source, target] = vectors.index(vector)
    return lookup


def assemble(far_operator):
    coeff_count = far_operator.shape[0]
    blocks = far_operator.reshape(coeff_count, -1, coeff_count)
    blocks = jnp.concatenate(
        [blocks, jnp.zeros((coeff_count, 1, coeff_count), blocks.dtype)], axis=1
    )
    picked = jnp.take(blocks, jnp.asarray(offset_table().reshape(-1), dtype=jnp.int32), axis=1)
    picked = picked.reshape(coeff_count, 27, 8, 8, coeff_count).transpose(1, 2, 0, 3, 4)
    return picked.reshape(27, 8 * coeff_count, 8 * coeff_count)


def group_cells(volume):
    size_x, size_y, size_z, coeff_count = volume.shape
    reshaped = volume.reshape(size_x // 2, 2, size_y // 2, 2, size_z // 2, 2, coeff_count)
    return reshaped.transpose(0, 2, 4, 1, 3, 5, 6).reshape(
        size_x // 2, size_y // 2, size_z // 2, 8 * coeff_count
    )


def spread_cells(grouped):
    size_x, size_y, size_z, total_rows = grouped.shape
    coeff_count = total_rows // 8
    reshaped = grouped.reshape(size_x, size_y, size_z, 2, 2, 2, coeff_count)
    return reshaped.transpose(0, 3, 1, 4, 2, 5, 6).reshape(
        2 * size_x, 2 * size_y, 2 * size_z, coeff_count
    )


def wrap_pad(volume, axis_id):
    extent = volume.shape[axis_id]
    lower = lax.slice_in_dim(volume, extent - 1, extent, axis=axis_id)
    upper = lax.slice_in_dim(volume, 0, 1, axis=axis_id)
    return jnp.concatenate([lower, volume, upper], axis=axis_id)


def wrap_window(volume, axis_id, anchor, extent):
    return lax.dynamic_slice_in_dim(wrap_pad(volume, axis_id), anchor, extent + 2, axis_id)


def region(index_now, cells, levels_up):
    anchor = index_now * cells // 2**levels_up
    extent = max(cells // 2**levels_up, 1)
    return (anchor, extent)


def cut(children, index_x, index_y, cells_x, cells_y, levels_up):
    anchor_x, extent_x = region(index_x, cells_x, levels_up)
    parent_x = region(index_x, cells_x, levels_up + 1)[0]
    anchor_y, extent_y = region(index_y, cells_y, levels_up)
    parent_y = region(index_y, cells_y, levels_up + 1)[0]
    children = lax.dynamic_slice_in_dim(children, anchor_x - 2 * parent_x, extent_x, 0)
    return lax.dynamic_slice_in_dim(children, anchor_y - 2 * parent_y, extent_y, 1)


def coarse_window(grouped, index_x, index_y, cells_x, cells_y, levels_up):
    anchor_x, extent_x = region(index_x, cells_x, levels_up)
    anchor_y, extent_y = region(index_y, cells_y, levels_up)
    windowed = wrap_window(grouped, 0, anchor_x, extent_x)
    windowed = wrap_window(windowed, 1, anchor_y, extent_y)
    return wrap_pad(windowed, 2)


def upward(up_operator, grouped):
    parent = jnp.einsum("xyzs,sj->xyzj", grouped, up_operator, preferred_element_type=jnp.float32)
    return parent.astype(jnp.bfloat16)


def downward(down_operator, parent):
    children = jnp.einsum(
        "xyzi,it->xyzt", parent, down_operator.astype(jnp.float32), precision=lax.Precision.HIGHEST
    )
    return spread_cells(children)


def far_field(padded, kernel):
    size_x = padded.shape[0] - 2
    size_y = padded.shape[1] - 2
    size_z = padded.shape[2] - 2
    running = None
    for shift_id, offset in enumerate(shift_list()):
        window_piece = padded[
            1 + offset[0] : 1 + offset[0] + size_x, 1 + offset[1] : 1 + offset[1] + size_y
        ]
        product_term = jnp.einsum(
            "xyzs,st->xyzt", window_piece, kernel[shift_id], preferred_element_type=jnp.float32
        )
        product_term = product_term[:, :, 1 + offset[2] : 1 + offset[2] + size_z]
        running = product_term if running is None else running + product_term
    return running


def near_field(positions, masses, counts):
    slot_count = masses.shape[0]
    size_x, size_y, size_z = (masses.shape[1], masses.shape[2], masses.shape[3])
    live_slot = lax.broadcasted_iota(jnp.int32, masses.shape, 0) < counts[None]
    live_mass = jnp.where(live_slot, masses, jnp.float32(0.0))
    stacked = jnp.concatenate([positions, live_mass[None]], axis=0)
    padded = wrap_pad(extended(stacked, (("gx", 2), ("gy", 3)), 1), 4)
    block_size = min(8, slot_count)
    same_slot = lax.broadcasted_iota(
        jnp.int32, (block_size, slot_count, 1, 1, 1), 0
    ) + 0 == lax.broadcasted_iota(jnp.int32, (block_size, slot_count, 1, 1, 1), 1)
    running = jnp.zeros((block_size, size_x, size_y, size_z), jnp.float32)
    for offset in shift_list():
        source = padded[
            :,
            :,
            1 + offset[0] : 1 + offset[0] + size_x,
            1 + offset[1] : 1 + offset[1] + size_y,
            1 + offset[2] : 1 + offset[2] + size_z,
        ]
        squared = jnp.float32(SOFTENING * SOFTENING)
        for axis_id in range(3):
            separation = (
                source[axis_id][None] + jnp.float32(offset[axis_id]) - positions[axis_id][:, None]
            )
            squared = squared + separation * separation
        pair_terms = source[3][None] * lax.rsqrt(squared)
        if offset == (0, 0, 0):
            pair_terms = jnp.where(same_slot, jnp.float32(0.0), pair_terms)
        running = running + jnp.sum(pair_terms, axis=1)
    results = running
    running = results
    return jnp.where(live_slot, -running / slot_count, jnp.float32(0.0))


def general_device(
    leaf_multipoles, positions, masses, counts, up_operator, far_operator, down_operator
):
    potential = near_field(positions, masses, counts)
    kernel = assemble(far_operator)
    index_x = lax.axis_index("gx")
    index_y = lax.axis_index("gy")
    cells_x = leaf_multipoles.shape[1]
    cells_y = leaf_multipoles.shape[2]
    leaf_cells = jnp.transpose(leaf_multipoles, (1, 2, 3, 0))
    grouped_leaf = group_cells(leaf_cells)
    padded = wrap_pad(extended(grouped_leaf, (("gx", 0), ("gy", 1)), 1), 2)
    far_leaf = spread_cells(far_field(padded, kernel))
    grouped_six = group_cells(upward(up_operator, grouped_leaf))
    padded = wrap_pad(extended(grouped_six, (("gx", 0), ("gy", 1)), 1), 2)
    far_six = spread_cells(far_field(padded, kernel))
    moments_five = upward(up_operator, grouped_six)
    columns = lax.all_gather(moments_five, "gy", axis=1, tiled=True)
    whole_five = lax.all_gather(columns, "gx", axis=0, tiled=True)
    grouped_five = group_cells(whole_five)
    window_five = coarse_window(grouped_five, index_x, index_y, cells_x, cells_y, 3)
    moments_four = upward(up_operator, grouped_five)
    far_five = cut(
        spread_cells(far_field(window_five, kernel)), index_x, index_y, cells_x, cells_y, 2
    )
    grouped_four = group_cells(moments_four)
    window_four = coarse_window(grouped_four, index_x, index_y, cells_x, cells_y, 4)
    far_four = cut(
        spread_cells(far_field(window_four, kernel)), index_x, index_y, cells_x, cells_y, 3
    )
    grouped_three = group_cells(upward(up_operator, grouped_four))
    window_three = coarse_window(grouped_three, index_x, index_y, cells_x, cells_y, 5)
    far_three = cut(
        spread_cells(far_field(window_three, kernel)), index_x, index_y, cells_x, cells_y, 4
    )
    expansion = far_three
    expansion = far_four + cut(
        downward(down_operator, expansion), index_x, index_y, cells_x, cells_y, 3
    )
    expansion = far_five + cut(
        downward(down_operator, expansion), index_x, index_y, cells_x, cells_y, 2
    )
    expansion = far_six + cut(
        downward(down_operator, expansion), index_x, index_y, cells_x, cells_y, 1
    )
    expansion = far_leaf + cut(
        downward(down_operator, expansion), index_x, index_y, cells_x, cells_y, 0
    )
    return (jnp.transpose(expansion, (3, 0, 1, 2)), potential)


def solution(mesh):
    small = (mesh.shape["gx"], mesh.shape["gy"]) == (8, 4)
    return jax.shard_map(
        per_device if small else general_device,
        mesh=mesh,
        in_specs=(
            P(None, "gx", "gy", None),
            P(None, None, "gx", "gy", None),
            P(None, "gx", "gy", None),
            P("gx", "gy", None),
            P(),
            P(),
            P(),
        ),
        out_specs=(P(None, "gx", "gy", None), P(None, "gx", "gy", None)),
        check_vma=False,
    )
```
